128 devices in a mesh: dx: 8 (over x, core), dy: 16 (over y, z).
Axes of the slice: x: 4, y: 4, z: 4, core: 2. Of those that a mesh axis runs over, the one named last changes fastest.
Arguments:
- positions: float32 [3, 262144], P(None, ('dx', 'dy')), may hold values from -6 to 6
- masses: float32 [262144], P(('dx', 'dy')), may hold values from 0.003 to 0.03
- centers: float32 [3, 131072], P(None, ('dx', 'dy')), may hold values from -3 to 3
- radii: float32 [131072], P(('dx', 'dy')), may hold values from 0.6 to 1.8
- pair_block: int32 [262144], P(('dx', 'dy')), may hold values from 0 to 15
- pair_halo: int32 [262144], P(('dx', 'dy')), may hold values from -1 to 1023, as said below
Outputs:
- centers_out: float32 [3, 131072], P(None, ('dx', 'dy'))
- radii_out: float32 [131072], P(('dx', 'dy'))
- profile: float32 [16, 131072], P(None, ('dx', 'dy'))
The draws below stay inside these ranges and needn't reach their ends.
Inputs may be any that keep to these rules, and one draw needn't show every extreme that they name: `pair_halo`: for each domain and each owner, the 16 slots hold the live halo indices first and then -1; in every draw some owner receives 16 live slots from every domain.
All inputs are finite; a program needn't handle non-finite values.
Results may differ from the reference program's by a relative error of at most 0.0003.
Values sent between devices are 32-bit elements; how exact they have to be, the bound alone decides.
No kernel may reach another device: no remote copies, remote signals or barrier semaphores. Data moves between devices by JAX's collectives and lax.ppermute only.
A program may use at most 64 MiB of HBM per device.

```python
import math
import jax
import jax.numpy as jnp
from jax import lax

SHELLS = 16
BLOCK = 128
ITERS = 2
BLOCKS_DEV = 16
CAP = 16
HALO_DEV = 1024
HALOS = 131072
PARTICLES = 262144
PAIRS = 262144
DEVICES = 128


def draw_pair_halo(key, part):
    key_heavy = jax.random.fold_in(key, 11)
    key_light = jax.random.fold_in(key, 12)
    key_column = jax.random.fold_in(key, 13)
    key_index = jax.random.fold_in(key, 14)
    heavy = jax.random.randint(key_heavy, (DEVICES, 1), 0, 4) == 0
    light = jax.random.randint(key_light, (DEVICES, DEVICES), 0, CAP // 2 + 1)
    column = jax.random.randint(key_column, (), 0, DEVICES)
    full = heavy | (jnp.arange(DEVICES)[None, :] == column)
    live = jnp.where(full, CAP, light)
    halos = jax.random.randint(key_index, (DEVICES, DEVICES, CAP), 0, HALO_DEV)
    slot = jnp.arange(CAP)[None, None, :]
    return jnp.where(slot < live[:, :, None], halos, -1).reshape(-1).astype(jnp.int32)


def set_ends(array, key, smallest, top_value):
    longest = array.shape.index(max(array.shape))
    spots = []
    for shift in (0, 1):
        where = [jax.random.randint(jax.random.fold_in(key, axis), (), 0, length) for axis, length in enumerate(array.shape)]
        where[longest] = (where[longest] + shift) % array.shape[longest]
        spots.append(tuple(where))
    return array.at[spots[0]].set(smallest).at[spots[1]].set(top_value)


def levels(rng, shape, pieces, least, high):
    def one(dim, parts):
        steps = jax.random.uniform(jax.random.fold_in(jax.random.fold_in(rng, 6), dim), (parts,), jnp.float32, least / len(pieces), high / len(pieces))
        return jnp.repeat(jnp.exp(steps), shape[dim] // parts).reshape((-1,) + (1,) * (len(shape) - dim - 1))

    level = one(*pieces[0])
    for cut in pieces[1:]:
        level = level * one(*cut)
    return level


def scatter_about(rng, dims, deviation, limit, pieces=(), kind=jnp.bfloat16):
    factor_of = levels(rng, dims, pieces, -0.22, 0.18) if pieces else 1.0
    drawn = jax.random.normal(rng, dims, jnp.float32) * deviation * factor_of
    return jnp.minimum(jnp.maximum(drawn, -limit), limit).astype(kind)


def setup_inputs(seed: int = 0) -> dict:
    streams_of = jax.random.split(jax.random.key(seed), 7)
    positions = scatter_about(streams_of[0], (3, PARTICLES), 1.0, 6.0, ((1, 128),), jnp.float32)
    masses = jnp.clip(jnp.exp(math.log(0.03) - 2.3025851 * jax.random.uniform(streams_of[1], (PARTICLES,), jnp.float32) ** levels(streams_of[1], (PARTICLES,), ((0, 128),), -0.2, 0.2)), 0.003, 0.03)
    centers = scatter_about(streams_of[2], (3, HALOS), 0.3, 3.0, ((1, 128),), jnp.float32)
    radii = jnp.clip(jnp.exp(math.log(1.8) - 1.0986122 * jax.random.uniform(streams_of[3], (HALOS,), jnp.float32) ** levels(streams_of[3], (HALOS,), ((0, 128),), -0.2, 0.2)), 0.6, 1.8)
    pair_block = set_ends(jax.random.randint(streams_of[4], (PAIRS,), 0, BLOCKS_DEV), jax.random.fold_in(streams_of[4], 1), 0, BLOCKS_DEV - 1).astype(jnp.int32)
    pair_halo = draw_pair_halo(jax.random.fold_in(streams_of[6], 71), 0)
    return {"positions": positions, "masses": masses, "centers": centers, "radii": radii, "pair_block": pair_block, "pair_halo": pair_halo}


def slot_terms(points, weights, center, radius, live):
    offset = points - center[:, :, None]
    dist = jnp.sqrt(lax.optimization_barrier(jnp.sum(offset * offset, axis=0)))
    scaled = dist * (SHELLS / 2.0 / radius)[:, None]
    middles = jnp.arange(SHELLS, dtype=jnp.float32) + 0.5
    tent = jnp.maximum(0.0, 1.0 - jnp.abs(scaled[None] - middles[:, None, None]))
    massed = weights * live[:, None]
    shells = lax.optimization_barrier(jnp.sum(tent * massed[None], axis=2))
    inner = jnp.clip(SHELLS / 2.0 - scaled, 0.0, 1.0) * massed
    total = lax.optimization_barrier(jnp.sum(inner, axis=1))
    moment = lax.optimization_barrier(jnp.sum(offset * inner[None], axis=2))
    return jnp.concatenate([shells, total[None], moment], axis=0)

def advance(centers, radii, sums):
    profile = jnp.cumsum(sums[:SHELLS], axis=0)
    enclosed = profile[SHELLS // 2 - 1]
    ratio = (1.0 + enclosed) / (1.0 + radii * radii * radii)
    new_radii = radii * ratio ** (1.0 / 3.0)
    new_centers = centers + sums[SHELLS + 1:] / jnp.maximum(sums[SHELLS], 1.0)
    return (new_centers, new_radii, profile)

def reference(positions, masses, centers, radii, pair_block, pair_halo):
    points = positions.reshape(3, DEVICES, BLOCKS_DEV, BLOCK)
    weights = masses.reshape(DEVICES, BLOCKS_DEV, BLOCK)
    blocks = pair_block.reshape(DEVICES, DEVICES * CAP)
    halos = pair_halo.reshape(DEVICES, DEVICES, CAP)
    owners = jnp.arange(DEVICES, dtype=jnp.int32)[None, :, None] * HALO_DEV
    target = jnp.where(halos >= 0, halos + owners, HALOS).reshape(DEVICES, DEVICES * CAP).astype(jnp.int32)
    profile = None
    for step in range(ITERS):

        def source(total, index):
            mine = lax.dynamic_index_in_dim(blocks, index, 0, keepdims=False)
            pts = jnp.take(lax.dynamic_index_in_dim(points, index, 1, keepdims=False), mine, axis=1)
            wts = jnp.take(lax.dynamic_index_in_dim(weights, index, 0, keepdims=False), mine, axis=0)
            dest = lax.dynamic_index_in_dim(target, index, 0, keepdims=False)
            safe = jnp.minimum(dest, HALOS - 1)
            live = (dest < HALOS).astype(jnp.float32)
            terms = slot_terms(pts, wts, jnp.take(centers, safe, axis=1), jnp.take(radii, safe), live)
            return (total + jax.ops.segment_sum(terms.T, dest, num_segments=HALOS + 1), None)
        start = jnp.zeros((HALOS + 1, SHELLS + 4), jnp.float32)
        sums, _ = lax.scan(source, start, jnp.arange(DEVICES, dtype=jnp.int32))
        centers, radii, profile = advance(centers, radii, sums[:HALOS].T)
    return (centers, radii, profile)
```

```python
import jax
import jax.numpy as jnp
from jax import lax
from jax.experimental import pallas as pl
from jax.experimental.pallas import tpu as pltpu
from jax.sharding import PartitionSpec as P

SHELLS = 16
BLOCK = 128
ITERS = 2
LANES = 128
ROWS = 24
AXES = ("dx", "dy")


def split(value, terms):
    parts = []
    for _ in range(terms):
        part = value.astype(jnp.bfloat16)
        parts.append(part)
        value = value - part.astype(jnp.float32)
    return parts


def kernel(particles, asked, centers, radii, centers_out, radii_out, profile_out, wide, one_hot, points, slot_state, partial):
    domains, _, blocks, _ = particles.shape
    halos = radii.shape[1]
    slots = asked.shape[2]
    tiles = slot_state.shape[0]
    group = LANES // slots

    lane = lax.broadcasted_iota(jnp.int32, (group, LANES), 1)
    own = lane // slots == lax.broadcasted_iota(jnp.int32, (group, LANES), 0)
    rows = []
    for which in range(2):
        wide[...] = jnp.zeros_like(wide)
        wide[:, :slots] = asked[which].astype(jnp.float32)
        row = wide[...]
        shift = slots
        while shift < LANES:
            row = row + pltpu.roll(row, shift, 1)
            shift *= 2
        rows.append([jnp.sum(jnp.where(own, row[t * group : (t + 1) * group], 0.0), axis=0, keepdims=True) for t in range(tiles)])
    halo_rows, block_rows = rows

    halo_index = lax.broadcasted_iota(jnp.int32, (halos, LANES), 0).astype(jnp.float32)
    for t in range(tiles):
        hit = halo_index == halo_rows[t]
        one_hot[:, t * LANES : (t + 1) * LANES] = jnp.where(hit, 1.0, 0.0).astype(jnp.bfloat16)

    count = group * blocks
    block_index = lax.broadcasted_iota(jnp.int32, (count, LANES), 0).astype(jnp.float32)
    first = (lax.broadcasted_iota(jnp.int32, (1, LANES), 1) // slots * blocks).astype(jnp.float32)
    for t in range(tiles):
        hit = block_index == block_rows[t] + first
        pick = jnp.where(hit, 1.0, 0.0).astype(jnp.bfloat16)
        for c in range(4):
            chosen = particles[t * group : (t + 1) * group, c].reshape(count, BLOCK).T
            high, low = split(chosen, 2)
            points[t, c] = jnp.dot(high, pick, preferred_element_type=jnp.float32) + jnp.dot(
                low, pick, preferred_element_type=jnp.float32
            )

    center = centers[...]
    radius = radii[...]
    partial[...] = jnp.zeros_like(partial)
    for step in range(ITERS):
        state = jnp.concatenate([center, radius], axis=0)
        stacked = jnp.concatenate([s.astype(jnp.float32) for s in split(state, 3)] + [jnp.zeros_like(state)], axis=0)
        got = jnp.dot(stacked.astype(jnp.bfloat16), one_hot[...], preferred_element_type=jnp.float32)
        got = got[0:4] + got[4:8] + got[8:12]
        for t in range(tiles):
            slot_state[t, 0:4] = got[:, t * LANES : (t + 1) * LANES]

        def one_tile(t, carry):
            mine = slot_state[t]
            cx, cy, cz, rad = mine[0:1], mine[1:2], mine[2:3], mine[3:4]
            scale = (SHELLS / 2.0) / jnp.where(rad > 0.0, rad, 1.0)
            ramps = [None] * (SHELLS + 1)
            inner = [None] * 4

            def add(sums, k, value):
                sums[k] = value if sums[k] is None else sums[k] + value

            for p in range(0, BLOCK, 8):
                x = points[t, 0, p : p + 8] - cx
                y = points[t, 1, p : p + 8] - cy
                z = points[t, 2, p : p + 8] - cz
                mass = points[t, 3, p : p + 8]
                scaled = jnp.sqrt(x * x + y * y + z * z) * scale
                half = mass * 0.5
                reach = half - mass * scaled
                for k in range(SHELLS + 1):
                    add(ramps, k, jnp.maximum(reach, 0.0))
                    if k == SHELLS // 2 - 1:
                        weight = jnp.maximum(jnp.minimum(reach + half, mass), 0.0)
                    reach = reach + mass
                add(inner, 0, weight)
                add(inner, 1, weight * x)
                add(inner, 2, weight * y)
                add(inner, 3, weight * z)
            for k in range(SHELLS):
                cumulative = ramps[k + 1] - ramps[k] - ramps[0]
                partial[t, k : k + 1] = jnp.sum(cumulative, axis=0, keepdims=True)
            for k in range(4):
                partial[t, SHELLS + k : SHELLS + k + 1] = jnp.sum(inner[k], axis=0, keepdims=True)
            return carry

        lax.fori_loop(0, tiles, one_tile, 0)
        terms = jnp.concatenate([partial[t] for t in range(tiles)], axis=1)
        high, low = split(terms, 2)
        across = (((1,), (1,)), ((), ()))
        sums = lax.dot_general(high, one_hot[...], across, preferred_element_type=jnp.float32) + lax.dot_general(
            low, one_hot[...], across, preferred_element_type=jnp.float32
        )
        profile = sums[:SHELLS]
        enclosed = profile[SHELLS // 2 - 1 : SHELLS // 2]
        ratio = (1.0 + enclosed) / (1.0 + radius * radius * radius)
        radius = radius * jnp.exp(jnp.log(ratio) * (1.0 / 3.0))
        center = center + sums[SHELLS + 1 : SHELLS + 4] / jnp.maximum(sums[SHELLS : SHELLS + 1], 1.0)
    centers_out[...] = center
    radii_out[...] = radius
    profile_out[...] = profile


def body(positions, masses, centers, radii, pair_block, pair_halo):
    devices = lax.axis_size(AXES)
    halos = radii.shape[0]
    blocks = masses.shape[0] // BLOCK
    slots = pair_halo.shape[0] // devices
    tiles = devices * slots // LANES
    mine = jnp.concatenate([positions, masses[None]], axis=0).reshape(4 * blocks, BLOCK)
    for axis in reversed(AXES):
        mine = lax.all_gather(mine, axis, axis=0, tiled=True)
    particles = mine.reshape(devices, 4, blocks, BLOCK)
    pairs = jnp.stack([pair_halo.reshape(devices, slots), pair_block.reshape(devices, slots)])
    asked = lax.all_to_all(pairs, AXES, split_axis=1, concat_axis=1, tiled=True)
    centers, radii, profile = pl.pallas_call(
        kernel,
        out_shape=(
            jax.ShapeDtypeStruct((3, halos), jnp.float32),
            jax.ShapeDtypeStruct((1, halos), jnp.float32),
            jax.ShapeDtypeStruct((SHELLS, halos), jnp.float32),
        ),
        scratch_shapes=[
            pltpu.VMEM((devices, LANES), jnp.float32),
            pltpu.VMEM((halos, devices * slots), jnp.bfloat16),
            pltpu.VMEM((tiles, 4, BLOCK, LANES), jnp.float32),
            pltpu.VMEM((tiles, 8, LANES), jnp.float32),
            pltpu.VMEM((tiles, ROWS, LANES), jnp.float32),
        ],
        compiler_params=pltpu.CompilerParams(vmem_limit_bytes=48 * 2**20),
    )(particles, asked, centers, radii[None])
    return (centers, radii[0], profile)


def solution(mesh):
    in_specs = (
        P(None, AXES),
        P(AXES),
        P(None, AXES),
        P(AXES),
        P(AXES),
        P(AXES),
    )
    out_specs = (P(None, AXES), P(AXES), P(None, AXES))
    return jax.shard_map(body, mesh=mesh, in_specs=in_specs, out_specs=out_specs, check_vma=False)
```

```python
import jax
import jax.numpy as jnp
from jax import lax
from jax.experimental import pallas as pl
from jax.experimental.pallas import tpu as pltpu
from jax.sharding import Mesh, PartitionSpec as P

SHELLS = 16
BLOCK = 128
ITERS = 2
LANES = 128
ROWS = 24
AXES = ("x", "core", "y", "z")


def split(value, terms):
    parts = []
    for _ in range(terms):
        part = value.astype(jnp.bfloat16)
        parts.append(part)
        value = value - part.astype(jnp.float32)
    return parts


def kernel(order, asked, centers, radii, *refs):
    particles, (centers_out, radii_out, profile_out, wide, one_hot, points, slot_state, partial) = refs[:-8], refs[-8:]
    chunk, _, blocks, _ = particles[0].shape
    halos = radii.shape[1]
    slots = asked.shape[1] // 2
    tiles = slot_state.shape[0]
    group = LANES // slots
    chunk_tiles = chunk // group

    lane = lax.broadcasted_iota(jnp.int32, (group, LANES), 1)
    own = lane // slots == lax.broadcasted_iota(jnp.int32, (group, LANES), 0)
    rows = []
    wide[...] = jnp.zeros_like(wide)
    for d in range(wide.shape[0]):
        wide[d : d + 1, : 2 * slots] = asked[pl.ds(order[d], 1)].astype(jnp.float32)
    lanes = lax.broadcasted_iota(jnp.int32, wide.shape, 1)
    for which in range(2):
        row = jnp.where(lanes // slots == which, wide[...], 0.0)
        shift = slots
        while shift < LANES:
            row = row + pltpu.roll(row, shift, 1)
            shift *= 2
        rows.append([jnp.sum(jnp.where(own, row[t * group : (t + 1) * group], 0.0), axis=0, keepdims=True) for t in range(tiles)])
    halo_rows, block_rows = rows

    halo_index = lax.broadcasted_iota(jnp.int32, (halos, LANES), 0).astype(jnp.float32)
    for t in range(tiles):
        hit = halo_index == halo_rows[t]
        one_hot[:, t * LANES : (t + 1) * LANES] = jnp.where(hit, 1.0, 0.0).astype(jnp.bfloat16)

    count = group * blocks
    block_index = lax.broadcasted_iota(jnp.int32, (count, LANES), 0).astype(jnp.float32)
    first = (lax.broadcasted_iota(jnp.int32, (1, LANES), 1) // slots * blocks).astype(jnp.float32)
    for t in range(tiles):
        hit = block_index == block_rows[t] + first
        pick = jnp.where(hit, 1.0, 0.0).astype(jnp.bfloat16)
        for c in range(4):
            chosen = particles[t // chunk_tiles][t % chunk_tiles * group : (t % chunk_tiles + 1) * group, c].reshape(count, BLOCK).T
            high, low = split(chosen, 2)
            points[t, c] = jnp.dot(high, pick, preferred_element_type=jnp.float32) + jnp.dot(
                low, pick, preferred_element_type=jnp.float32
            )

    center = centers[...]
    radius = radii[...]
    partial[...] = jnp.zeros_like(partial)
    for step in range(ITERS):
        state = jnp.concatenate([center, radius], axis=0)
        stacked = jnp.concatenate([s.astype(jnp.float32) for s in split(state, 3)] + [jnp.zeros_like(state)], axis=0)
        got = jnp.dot(stacked.astype(jnp.bfloat16), one_hot[...], preferred_element_type=jnp.float32)
        got = got[0:4] + got[4:8] + got[8:12]
        for t in range(tiles):
            slot_state[t, 0:4] = got[:, t * LANES : (t + 1) * LANES]

        def one_tile(t, carry):
            mine = slot_state[t]
            cx, cy, cz, rad = mine[0:1], mine[1:2], mine[2:3], mine[3:4]
            scale = (SHELLS / 2.0) / jnp.where(rad > 0.0, rad, 1.0)
            ramps = [None] * (SHELLS + 1)
            inner = [None] * 4

            def add(sums, k, value):
                sums[k] = value if sums[k] is None else sums[k] + value

            for p in range(0, BLOCK, 8):
                x = points[t, 0, p : p + 8] - cx
                y = points[t, 1, p : p + 8] - cy
                z = points[t, 2, p : p + 8] - cz
                mass = points[t, 3, p : p + 8]
                scaled = jnp.sqrt(x * x + y * y + z * z) * scale
                half = mass * 0.5
                reach = half - mass * scaled
                for k in range(SHELLS + 1):
                    add(ramps, k, jnp.maximum(reach, 0.0))
                    if k == SHELLS // 2 - 1:
                        weight = jnp.maximum(jnp.minimum(reach + half, mass), 0.0)
                    reach = reach + mass
                add(inner, 0, weight)
                add(inner, 1, weight * x)
                add(inner, 2, weight * y)
                add(inner, 3, weight * z)
            for k in range(SHELLS):
                cumulative = ramps[k + 1] - ramps[k] - ramps[0]
                partial[t, k : k + 1] = jnp.sum(cumulative, axis=0, keepdims=True)
            for k in range(4):
                partial[t, SHELLS + k : SHELLS + k + 1] = jnp.sum(inner[k], axis=0, keepdims=True)
            return carry

        lax.fori_loop(0, tiles, one_tile, 0)
        terms = jnp.concatenate([partial[t] for t in range(tiles)], axis=1)
        high, low = split(terms, 2)
        across = (((1,), (1,)), ((), ()))
        sums = lax.dot_general(high, one_hot[...], across, preferred_element_type=jnp.float32) + lax.dot_general(
            low, one_hot[...], across, preferred_element_type=jnp.float32
        )
        profile = sums[:SHELLS]
        enclosed = profile[SHELLS // 2 - 1 : SHELLS // 2]
        ratio = (1.0 + enclosed) / (1.0 + radius * radius * radius)
        radius = radius * jnp.exp(jnp.log(ratio) * (1.0 / 3.0))
        center = center + sums[SHELLS + 1 : SHELLS + 4] / jnp.maximum(sums[SHELLS : SHELLS + 1], 1.0)
    centers_out[...] = center
    radii_out[...] = radius
    profile_out[...] = profile


def shifted(value, axis):
    size = lax.axis_size(axis)
    return [value] + [lax.ppermute(value, axis, [(i, (i + k) % size) for i in range(size)]) for k in range(1, size)]


def sources():
    index = jnp.zeros((1,), jnp.int32)
    for axis, stride in (("x", 32), ("core", 16), ("y", 4), ("z", 1)):
        size = lax.axis_size(axis)
        here = (lax.axis_index(axis) - jnp.arange(size, dtype=jnp.int32)) % size * stride
        index = (index[:, None] + here[None, :]).reshape(-1)
    return index


def body(positions, masses, centers, radii, pair_block, pair_halo):
    devices = lax.axis_size(AXES)
    halos = radii.shape[0]
    blocks = masses.shape[0] // BLOCK
    slots = pair_halo.shape[0] // devices
    tiles = devices * slots // LANES
    pairs = jnp.concatenate([pair_halo.reshape(devices, slots), pair_block.reshape(devices, slots)], axis=1)
    plane = jnp.concatenate([positions, masses[None]], axis=0).reshape(1, 4, blocks, BLOCK)
    for axis in ("z", "y"):
        plane = jnp.concatenate(shifted(plane, axis), axis=0)
    plane, pairs = lax.optimization_barrier((plane, pairs))
    chunks = [part for slab in shifted(plane, "x") for part in shifted(slab, "core")]
    asked = lax.all_to_all(pairs, AXES, split_axis=0, concat_axis=0, tiled=True)
    vmem = pl.BlockSpec(memory_space=pltpu.VMEM)
    centers, radii, profile = pl.pallas_call(
        kernel,
        in_specs=[pl.BlockSpec(memory_space=pltpu.SMEM)] + [vmem] * (3 + len(chunks)),
        out_shape=(
            jax.ShapeDtypeStruct((3, halos), jnp.float32),
            jax.ShapeDtypeStruct((1, halos), jnp.float32),
            jax.ShapeDtypeStruct((SHELLS, halos), jnp.float32),
        ),
        scratch_shapes=[
            pltpu.VMEM((devices, LANES), jnp.float32),
            pltpu.VMEM((halos, devices * slots), jnp.bfloat16),
            pltpu.VMEM((tiles, 4, BLOCK, LANES), jnp.float32),
            pltpu.VMEM((tiles, 8, LANES), jnp.float32),
            pltpu.VMEM((tiles, ROWS, LANES), jnp.float32),
        ],
        compiler_params=pltpu.CompilerParams(vmem_limit_bytes=48 * 2**20),
    )(sources(), asked, centers, radii[None], *chunks)
    return (centers, radii[0], profile)


def solution(mesh):
    chips = Mesh(mesh.devices.reshape(4, 2, 4, 4), AXES)
    in_specs = (
        P(None, AXES),
        P(AXES),
        P(None, AXES),
        P(AXES),
        P(AXES),
        P(AXES),
    )
    out_specs = (P(None, AXES), P(AXES), P(None, AXES))
    return jax.shard_map(body, mesh=chips, in_specs=in_specs, out_specs=out_specs, check_vma=False)
```

```python
import functools

import jax
import jax.numpy as jnp
from jax import lax
from jax.experimental import pallas as pl
from jax.experimental.pallas import tpu as pltpu
from jax.sharding import Mesh, PartitionSpec as P

SHELLS = 16
BLOCK = 128
LANES = 128
ROWS = 24
AXES = ("x", "core", "y", "z")
VMEM = pl.BlockSpec(memory_space=pltpu.VMEM)
PARAMS = pltpu.CompilerParams(vmem_limit_bytes=16 * 2**20)


def f32(*shape):
    return jax.ShapeDtypeStruct(shape, jnp.float32)


def split(value, terms):
    parts = []
    for _ in range(terms):
        part = value.astype(jnp.bfloat16)
        parts.append(part)
        value = value - part.astype(jnp.float32)
    return parts


def gather_state(center, radius, one_hot):
    state = jnp.concatenate([center, radius], axis=0)
    stacked = jnp.concatenate([s.astype(jnp.float32) for s in split(state, 3)] + [jnp.zeros_like(state)], axis=0)
    got = jnp.dot(stacked.astype(jnp.bfloat16), one_hot, preferred_element_type=jnp.float32)
    return got[0:4] + got[4:8] + got[8:12]


def prepare(blocks, order, asked, centers, radii, one_hot, slot_state, wide):
    halos = radii.shape[1]
    slots = asked.shape[1] // 2
    tiles = slot_state.shape[0]
    group = LANES // slots
    wide[...] = jnp.zeros_like(wide)
    for d in range(wide.shape[0]):
        wide[d : d + 1, : 2 * slots] = asked[pl.ds(order[d], 1)].astype(jnp.float32)
    lane = lax.broadcasted_iota(jnp.int32, (group, LANES), 1)
    own = lane // slots == lax.broadcasted_iota(jnp.int32, (group, LANES), 0)
    lanes = lax.broadcasted_iota(jnp.int32, wide.shape, 1)
    rows = []
    for which in range(2):
        row = jnp.where(lanes // slots == which, wide[...], 0.0)
        shift = slots
        while shift < LANES:
            row = row + pltpu.roll(row, shift, 1)
            shift *= 2
        rows.append([jnp.sum(jnp.where(own, row[t * group : (t + 1) * group], 0.0), axis=0, keepdims=True) for t in range(tiles)])
    halo_rows, block_rows = rows
    halo_index = lax.broadcasted_iota(jnp.int32, (halos, LANES), 0).astype(jnp.float32)
    first = (lax.broadcasted_iota(jnp.int32, (1, LANES), 1) // slots * blocks).astype(jnp.float32)
    for t in range(tiles):
        hit = halo_index == halo_rows[t]
        one_hot[:, t * LANES : (t + 1) * LANES] = jnp.where(hit, 1.0, 0.0).astype(jnp.bfloat16)
    got = gather_state(centers[...], radii[...], one_hot[...])
    for t in range(tiles):
        slot_state[t] = jnp.concatenate(
            [got[:, t * LANES : (t + 1) * LANES], block_rows[t] + first, jnp.zeros((3, LANES), jnp.float32)], axis=0
        )


def tile_sums(mine, points, t, out, o):
    cx, cy, cz, rad = mine[0:1], mine[1:2], mine[2:3], mine[3:4]
    scale = (SHELLS / 2.0) / jnp.where(rad > 0.0, rad, 1.0)
    ramps = [None] * (SHELLS + 1)
    inner = [None] * 4

    def add(sums, k, value):
        sums[k] = value if sums[k] is None else sums[k] + value

    for p in range(0, BLOCK, 8):
        x = points[t, 0, p : p + 8] - cx
        y = points[t, 1, p : p + 8] - cy
        z = points[t, 2, p : p + 8] - cz
        mass = points[t, 3, p : p + 8]
        scaled = jnp.sqrt(x * x + y * y + z * z) * scale
        half = mass * 0.5
        reach = half - mass * scaled
        for k in range(SHELLS + 1):
            add(ramps, k, jnp.maximum(reach, 0.0))
            if k == SHELLS // 2 - 1:
                weight = jnp.maximum(jnp.minimum(reach + half, mass), 0.0)
            reach = reach + mass
        add(inner, 0, weight)
        add(inner, 1, weight * x)
        add(inner, 2, weight * y)
        add(inner, 3, weight * z)
    for k in range(SHELLS):
        cumulative = ramps[k + 1] - ramps[k] - ramps[0]
        out[o, k : k + 1] = jnp.sum(cumulative, axis=0, keepdims=True)
    for k in range(4):
        out[o, SHELLS + k : SHELLS + k + 1] = jnp.sum(inner[k], axis=0, keepdims=True)


def first_pass(offset, group, slot_state, *refs):
    chunks, (points, partial) = refs[:-2], refs[-2:]
    chunk, _, blocks, _ = chunks[0].shape
    count = group * blocks
    tiles = chunk // group
    block_index = lax.broadcasted_iota(jnp.int32, (count, LANES), 0).astype(jnp.float32)
    partial[...] = jnp.zeros_like(partial)
    for t in range(tiles * len(chunks)):
        hit = block_index == slot_state[offset + t, 4:5]
        pick = jnp.where(hit, 1.0, 0.0).astype(jnp.bfloat16)
        at = t % tiles * group
        for c in range(4):
            chosen = chunks[t // tiles][at : at + group, c].reshape(count, BLOCK).T
            high, low = split(chosen, 2)
            points[t, c] = jnp.dot(high, pick, preferred_element_type=jnp.float32) + jnp.dot(
                low, pick, preferred_element_type=jnp.float32
            )

    def one_tile(t, carry):
        tile_sums(slot_state[offset + t], points, t, partial, t)
        return carry

    lax.fori_loop(0, tiles * len(chunks), one_tile, 0)


def finish(slabs, one_hot, centers, radii, *refs):
    points, partials = refs[:slabs], refs[slabs : 2 * slabs]
    centers_out, radii_out, profile_out, slot_state, partial = refs[2 * slabs :]
    tiles = slot_state.shape[0]
    each = tiles // slabs

    def advance(center, radius, terms):
        high, low = split(terms, 2)
        across = (((1,), (1,)), ((), ()))
        sums = lax.dot_general(high, one_hot[...], across, preferred_element_type=jnp.float32) + lax.dot_general(
            low, one_hot[...], across, preferred_element_type=jnp.float32
        )
        profile = sums[:SHELLS]
        enclosed = profile[SHELLS // 2 - 1 : SHELLS // 2]
        ratio = (1.0 + enclosed) / (1.0 + radius * radius * radius)
        radius = radius * jnp.exp(jnp.log(ratio) * (1.0 / 3.0))
        center = center + sums[SHELLS + 1 : SHELLS + 4] / jnp.maximum(sums[SHELLS : SHELLS + 1], 1.0)
        return center, radius, profile

    terms = jnp.concatenate([partials[t // each][t % each] for t in range(tiles)], axis=1)
    center, radius, _ = advance(centers[...], radii[...], terms)
    got = gather_state(center, radius, one_hot[...])
    for t in range(tiles):
        slot_state[t, 0:4] = got[:, t * LANES : (t + 1) * LANES]
    partial[...] = jnp.zeros_like(partial)
    for slab in range(slabs):

        def one_tile(t, carry):
            tile_sums(slot_state[slab * each + t], points[slab], t, partial, slab * each + t)
            return carry

        lax.fori_loop(0, each, one_tile, 0)
    terms = jnp.concatenate([partial[t] for t in range(tiles)], axis=1)
    center, radius, profile = advance(center, radius, terms)
    centers_out[...] = center
    radii_out[...] = radius
    profile_out[...] = profile


def shifted(value, axis):
    size = lax.axis_size(axis)
    return [value] + [lax.ppermute(value, axis, [(i, (i + k) % size) for i in range(size)]) for k in range(1, size)]


def sources():
    index = jnp.zeros((1,), jnp.int32)
    for axis, stride in (("x", 32), ("core", 16), ("y", 4), ("z", 1)):
        size = lax.axis_size(axis)
        here = (lax.axis_index(axis) - jnp.arange(size, dtype=jnp.int32)) % size * stride
        index = (index[:, None] + here[None, :]).reshape(-1)
    return index


def body(positions, masses, centers, radii, pair_block, pair_halo):
    devices = lax.axis_size(AXES)
    halos = radii.shape[0]
    blocks = masses.shape[0] // BLOCK
    slots = pair_halo.shape[0] // devices
    tiles = devices * slots // LANES
    pairs = jnp.concatenate([pair_halo.reshape(devices, slots), pair_block.reshape(devices, slots)], axis=1)
    plane = jnp.concatenate([positions, masses[None]], axis=0).reshape(1, 4, blocks, BLOCK)
    order = sources()
    for axis in ("z", "y"):
        plane = jnp.concatenate(shifted(plane, axis), axis=0)
    plane, pairs, order = lax.optimization_barrier((plane, pairs, order))
    slabs = shifted(plane, "x")
    asked = lax.all_to_all(pairs, AXES, split_axis=0, concat_axis=0, tiled=True)
    radii = radii[None]
    one_hot, slot_state = pl.pallas_call(
        functools.partial(prepare, blocks),
        in_specs=[pl.BlockSpec(memory_space=pltpu.SMEM), VMEM, VMEM, VMEM],
        out_specs=[VMEM] * 2,
        out_shape=(jax.ShapeDtypeStruct((halos, devices * slots), jnp.bfloat16), f32(tiles, 8, LANES)),
        scratch_shapes=[pltpu.VMEM((devices, LANES), jnp.float32)],
        compiler_params=PARAMS,
    )(order, asked, centers, radii)
    each = tiles // len(slabs)
    points, partials = [], []
    for i, slab in enumerate(slabs):
        if i:
            slab, _ = lax.optimization_barrier((slab, partials[0]))
        got = pl.pallas_call(
            functools.partial(first_pass, i * each, LANES // slots),
            in_specs=[VMEM] * 3,
            out_specs=[VMEM] * 2,
            out_shape=(f32(each, 4, BLOCK, LANES), f32(each, ROWS, LANES)),
            compiler_params=PARAMS,
        )(slot_state, *shifted(slab, "core"))
        points.append(got[0])
        partials.append(got[1])
    centers, radii, profile = pl.pallas_call(
        functools.partial(finish, len(slabs)),
        in_specs=[VMEM] * (3 + 2 * len(slabs)),
        out_specs=[VMEM] * 3,
        out_shape=(f32(3, halos), f32(1, halos), f32(SHELLS, halos)),
        scratch_shapes=[pltpu.VMEM((tiles, 8, LANES), jnp.float32), pltpu.VMEM((tiles, ROWS, LANES), jnp.float32)],
        compiler_params=PARAMS,
    )(one_hot, centers, radii, *points, *partials)
    return (centers, radii[0], profile)


def solution(mesh):
    chips = Mesh(mesh.devices.reshape(4, 2, 4, 4), AXES)
    in_specs = (
        P(None, AXES),
        P(AXES),
        P(None, AXES),
        P(AXES),
        P(AXES),
        P(AXES),
    )
    out_specs = (P(None, AXES), P(AXES), P(None, AXES))
    return jax.shard_map(body, mesh=chips, in_specs=in_specs, out_specs=out_specs, check_vma=False)
```

```python
import functools

import jax
import jax.numpy as jnp
from jax import lax
from jax.experimental import pallas as pl
from jax.experimental.pallas import tpu as pltpu
from jax.sharding import Mesh, PartitionSpec as P

SHELLS = 16
BLOCK = 128
LANES = 128
ROWS = 24
AXES = ("x", "core", "y", "z")
VMEM = pl.BlockSpec(memory_space=pltpu.VMEM)
PARAMS = pltpu.CompilerParams(vmem_limit_bytes=16 * 2**20)


def f32(*shape):
    return jax.ShapeDtypeStruct(shape, jnp.float32)


def split(value, terms):
    parts = []
    for _ in range(terms):
        part = value.astype(jnp.bfloat16)
        parts.append(part)
        value = value - part.astype(jnp.float32)
    return parts


def gather_state(center, radius, one_hot):
    state = jnp.concatenate([center, radius], axis=0)
    stacked = jnp.concatenate([s.astype(jnp.float32) for s in split(state, 3)] + [jnp.zeros_like(state)], axis=0)
    got = jnp.dot(stacked.astype(jnp.bfloat16), one_hot, preferred_element_type=jnp.float32)
    return got[0:4] + got[4:8] + got[8:12]


def prepare(blocks, slots, order, asked, centers, radii, one_hot, halo_hot, slot_state, wide):
    halos = radii.shape[1]
    domains = wide.shape[0]
    tiles = slot_state.shape[0]
    group = LANES // slots
    for d in range(domains):
        wide[d : d + 1] = asked[pl.ds(order[d], 1)].astype(jnp.float32)
    lane = lax.broadcasted_iota(jnp.int32, (group, LANES), 1)
    own = lane // slots == lax.broadcasted_iota(jnp.int32, (group, LANES), 0)
    here = lax.broadcasted_iota(jnp.int32, (domains, LANES), 1) // slots == order[domains]
    rows = []
    for which in range(2):
        row = jnp.where(here, wide[:, which * LANES : (which + 1) * LANES], 0.0)
        shift = slots
        while shift < LANES:
            row = row + pltpu.roll(row, shift, 1)
            shift *= 2
        rows.append([jnp.sum(jnp.where(own, row[t * group : (t + 1) * group], 0.0), axis=0, keepdims=True) for t in range(tiles)])
    halo_rows, block_rows = rows
    halo_index = lax.broadcasted_iota(jnp.int32, (halos, LANES), 0).astype(jnp.float32)
    first = (lax.broadcasted_iota(jnp.int32, (1, LANES), 1) // slots * blocks).astype(jnp.float32)
    for t in range(tiles):
        hit = halo_index == halo_rows[t]
        one_hot[:, t * LANES : (t + 1) * LANES] = jnp.where(hit, 1.0, 0.0).astype(jnp.bfloat16)
    across = lax.broadcasted_iota(jnp.int32, (LANES, halos), 1).astype(jnp.float32)
    for t in range(tiles):
        column = jnp.broadcast_to(halo_rows[t], (LANES, LANES)).T
        for h in range(0, halos, LANES):
            hit = across[:, h : h + LANES] == column
            halo_hot[t * LANES : (t + 1) * LANES, h : h + LANES] = jnp.where(hit, 1.0, 0.0).astype(jnp.bfloat16)
    got = gather_state(centers[...], radii[...], one_hot[...])
    for t in range(tiles):
        slot_state[t] = jnp.concatenate(
            [got[:, t * LANES : (t + 1) * LANES], block_rows[t] + first, jnp.zeros((3, LANES), jnp.float32)], axis=0
        )


def tile_sums(mine, points, t, out, o):
    cx, cy, cz, rad = mine[0:1], mine[1:2], mine[2:3], mine[3:4]
    scale = (SHELLS / 2.0) / jnp.where(rad > 0.0, rad, 1.0)
    ramps = [None] * (SHELLS + 1)
    inner = [None] * 4

    def add(sums, k, value):
        sums[k] = value if sums[k] is None else sums[k] + value

    for p in range(0, BLOCK, 8):
        x = points[t, 0, p : p + 8] - cx
        y = points[t, 1, p : p + 8] - cy
        z = points[t, 2, p : p + 8] - cz
        mass = points[t, 3, p : p + 8]
        scaled = jnp.sqrt(x * x + y * y + z * z) * scale
        half = mass * 0.5
        reach = half - mass * scaled
        for k in range(SHELLS + 1):
            add(ramps, k, jnp.maximum(reach, 0.0))
            if k == SHELLS // 2 - 1:
                weight = jnp.maximum(jnp.minimum(reach + half, mass), 0.0)
            reach = reach + mass
        add(inner, 0, weight)
        add(inner, 1, weight * x)
        add(inner, 2, weight * y)
        add(inner, 3, weight * z)
    for k in range(SHELLS):
        cumulative = ramps[k + 1] - ramps[k] - ramps[0]
        out[o, k : k + 1] = jnp.sum(cumulative, axis=0, keepdims=True)
    for k in range(4):
        out[o, SHELLS + k : SHELLS + k + 1] = jnp.sum(inner[k], axis=0, keepdims=True)


def first_pass(offset, group, slot_state, *refs):
    chunks, (points, partial) = refs[:-2], refs[-2:]
    chunk, _, blocks, _ = chunks[0].shape
    count = group * blocks
    tiles = chunk // group
    block_index = lax.broadcasted_iota(jnp.int32, (count, LANES), 0).astype(jnp.float32)
    partial[...] = jnp.zeros_like(partial)
    for t in range(tiles * len(chunks)):
        hit = block_index == slot_state[offset + t, 4:5]
        pick = jnp.where(hit, 1.0, 0.0).astype(jnp.bfloat16)
        at = t % tiles * group
        for c in range(4):
            chosen = chunks[t // tiles][at : at + group, c].reshape(count, BLOCK).T
            high, low = split(chosen, 2)
            points[t, c] = jnp.dot(high, pick, preferred_element_type=jnp.float32) + jnp.dot(
                low, pick, preferred_element_type=jnp.float32
            )

    def one_tile(t, carry):
        tile_sums(slot_state[offset + t], points, t, partial, t)
        return carry

    lax.fori_loop(0, tiles * len(chunks), one_tile, 0)


def finish(slabs, one_hot, halo_hot, centers, radii, *refs):
    points, partials = refs[:slabs], refs[slabs : 2 * slabs]
    centers_out, radii_out, profile_out, slot_state, partial = refs[2 * slabs :]
    tiles = slot_state.shape[0]
    each = tiles // slabs

    def advance(center, radius, terms):
        high, low = [part.astype(jnp.float32) for part in split(terms, 2)]
        both = jnp.concatenate([high, low], axis=0).astype(jnp.bfloat16)
        sums = jnp.dot(both, halo_hot[...], preferred_element_type=jnp.float32)
        sums = sums[:ROWS] + sums[ROWS:]
        profile = sums[:SHELLS]
        enclosed = profile[SHELLS // 2 - 1 : SHELLS // 2]
        ratio = (1.0 + enclosed) / (1.0 + radius * radius * radius)
        radius = radius * jnp.exp(jnp.log(ratio) * (1.0 / 3.0))
        center = center + sums[SHELLS + 1 : SHELLS + 4] / jnp.maximum(sums[SHELLS : SHELLS + 1], 1.0)
        return center, radius, profile

    terms = jnp.concatenate([partials[t // each][t % each] for t in range(tiles)], axis=1)
    center, radius, _ = advance(centers[...], radii[...], terms)
    got = gather_state(center, radius, one_hot[...])
    for t in range(tiles):
        slot_state[t, 0:4] = got[:, t * LANES : (t + 1) * LANES]
    partial[...] = jnp.zeros_like(partial)
    for slab in range(slabs):

        def one_tile(t, carry):
            tile_sums(slot_state[slab * each + t], points[slab], t, partial, slab * each + t)
            return carry

        lax.fori_loop(0, each, one_tile, 0)
    terms = jnp.concatenate([partial[t] for t in range(tiles)], axis=1)
    center, radius, profile = advance(center, radius, terms)
    centers_out[...] = center
    radii_out[...] = radius
    profile_out[...] = profile


def shifted(value, axis):
    size = lax.axis_size(axis)
    return [value] + [lax.ppermute(value, axis, [(i, (i + k) % size) for i in range(size)]) for k in range(1, size)]


def sources():
    index = jnp.zeros((1,), jnp.int32)
    for axis, stride in (("x", 32), ("core", 16), ("y", 4), ("z", 1)):
        size = lax.axis_size(axis)
        here = (lax.axis_index(axis) - jnp.arange(size, dtype=jnp.int32)) % size * stride
        index = (index[:, None] + here[None, :]).reshape(-1)
    return index


def body(positions, masses, centers, radii, pair_block, pair_halo):
    devices = lax.axis_size(AXES)
    halos = radii.shape[0]
    blocks = masses.shape[0] // BLOCK
    slots = pair_halo.shape[0] // devices
    tiles = devices * slots // LANES
    group = LANES // slots
    pairs = jnp.concatenate([pair_halo.reshape(tiles, LANES), pair_block.reshape(tiles, LANES)], axis=1)
    pairs = jnp.broadcast_to(pairs[:, None], (tiles, group, 2 * LANES)).reshape(devices, 2 * LANES)
    asked = lax.all_to_all(pairs, AXES, split_axis=0, concat_axis=0, tiled=True)
    plane = jnp.concatenate([positions, masses[None]], axis=0).reshape(1, 4, blocks, BLOCK)
    order = jnp.concatenate([sources(), lax.axis_index(AXES)[None] % group])
    for axis in ("z", "y"):
        plane = jnp.concatenate(shifted(plane, axis), axis=0)
    plane, asked, order = lax.optimization_barrier((plane, asked, order))
    slabs = shifted(plane, "x")
    radii = radii[None]
    one_hot, halo_hot, slot_state = pl.pallas_call(
        functools.partial(prepare, blocks, slots),
        in_specs=[pl.BlockSpec(memory_space=pltpu.SMEM), VMEM, VMEM, VMEM],
        out_specs=[VMEM] * 3,
        out_shape=(
            jax.ShapeDtypeStruct((halos, devices * slots), jnp.bfloat16),
            jax.ShapeDtypeStruct((devices * slots, halos), jnp.bfloat16),
            f32(tiles, 8, LANES),
        ),
        scratch_shapes=[pltpu.VMEM((devices, 2 * LANES), jnp.float32)],
        compiler_params=PARAMS,
    )(order, asked, centers, radii)
    each = tiles // len(slabs)
    points, partials = [], []
    for i, slab in enumerate(slabs):
        if i:
            slab, _ = lax.optimization_barrier((slab, partials[0]))
        got = pl.pallas_call(
            functools.partial(first_pass, i * each, group),
            in_specs=[VMEM] * 3,
            out_specs=[VMEM] * 2,
            out_shape=(f32(each, 4, BLOCK, LANES), f32(each, ROWS, LANES)),
            compiler_params=PARAMS,
        )(slot_state, *shifted(slab, "core"))
        points.append(got[0])
        partials.append(got[1])
    centers, radii, profile = pl.pallas_call(
        functools.partial(finish, len(slabs)),
        in_specs=[VMEM] * (4 + 2 * len(slabs)),
        out_specs=[VMEM] * 3,
        out_shape=(f32(3, halos), f32(1, halos), f32(SHELLS, halos)),
        scratch_shapes=[pltpu.VMEM((tiles, 8, LANES), jnp.float32), pltpu.VMEM((tiles, ROWS, LANES), jnp.float32)],
        compiler_params=PARAMS,
    )(one_hot, halo_hot, centers, radii, *points, *partials)
    return (centers, radii[0], profile)


def solution(mesh):
    chips = Mesh(mesh.devices.reshape(4, 2, 4, 4), AXES)
    in_specs = (
        P(None, AXES),
        P(AXES),
        P(None, AXES),
        P(AXES),
        P(AXES),
        P(AXES),
    )
    out_specs = (P(None, AXES), P(AXES), P(None, AXES))
    return jax.shard_map(body, mesh=chips, in_specs=in_specs, out_specs=out_specs, check_vma=False)
```

```python
import functools

import jax
import jax.numpy as jnp
from jax import lax
from jax.experimental import pallas as pl
from jax.experimental.pallas import tpu as pltpu
from jax.sharding import Mesh, PartitionSpec as P

SHELLS = 16
BLOCK = 128
LANES = 128
ROWS = 24
AXES = ("x", "core", "y", "z")
VMEM = pl.BlockSpec(memory_space=pltpu.VMEM)
PARAMS = pltpu.CompilerParams(vmem_limit_bytes=16 * 2**20)


def f32(*shape):
    return jax.ShapeDtypeStruct(shape, jnp.float32)


def split(value, terms):
    parts = []
    for _ in range(terms):
        part = value.astype(jnp.bfloat16)
        parts.append(part)
        value = value - part.astype(jnp.float32)
    return parts


def gather_state(center, radius, one_hot):
    state = jnp.concatenate([center, radius], axis=0)
    stacked = jnp.concatenate([s.astype(jnp.float32) for s in split(state, 3)] + [jnp.zeros_like(state)], axis=0)
    got = jnp.dot(stacked.astype(jnp.bfloat16), one_hot, preferred_element_type=jnp.float32)
    return got[0:4] + got[4:8] + got[8:12]


def spread(rows, keep, own, slots):
    rows = jnp.where(keep, rows, 0.0)
    shift = slots
    while shift < LANES:
        rows = rows + pltpu.roll(rows, shift, 1)
        shift *= 2
    return jnp.sum(jnp.where(own, rows, 0.0), axis=0, keepdims=True)


def pack(positions, masses, halo, block, out):
    blocks = masses.shape[0]
    for c in range(3):
        for b in range(blocks):
            out[c * blocks + b : c * blocks + b + 1] = positions[c : c + 1, b * BLOCK : (b + 1) * BLOCK]
    at = 3 * blocks
    for part in (masses, halo, block):
        out[at : at + part.shape[0]] = part[...].astype(jnp.float32)
        at += part.shape[0]


def merge_z(slots, width, place, *refs):
    size = len(refs) // 2
    parts, outs = refs[:size], refs[size:]
    index_rows = (parts[0].shape[0] - width) // 2
    row = lax.broadcasted_iota(jnp.int32, (index_rows, LANES), 0)
    group = lax.broadcasted_iota(jnp.int32, (index_rows, LANES), 1) // slots
    for k in range(size):
        for i in range(size):
            outs[k][i * width : (i + 1) * width] = parts[i][:width]
        y = (place[2] + k) % size
        keep = (group == y % 2 * size + place[3]) & (row % 2 == y // 2)
        for which in range(2):
            for i in range(size):
                at = width + which * index_rows
                to = size * width + which * size + i
                outs[k][to : to + 1] = spread(parts[i][at : at + index_rows], keep, group == row // 2, slots)


def merge_y(*refs):
    size = len(refs) - 3
    parts, (low, high, index) = refs[:size], refs[size:]
    rows = parts[0].shape[0] - 2 * size
    for i in range(size):
        half = (low, high)[i // 2]
        half[i % 2 * rows : (i % 2 + 1) * rows] = parts[i][:rows]
        for which in range(2):
            to = which * size * size + i * size
            at = rows + which * size
            index[to : to + size] = parts[i][at : at + size]


def prepare(slots, blocks, place, mine, other, centers, radii, one_hot, halo_hot, slot_state):
    halos = radii.shape[1]
    tiles = slot_state.shape[0]
    each = tiles // 4
    lane_group = lax.broadcasted_iota(jnp.int32, (8, LANES), 1) // slots
    own = lane_group == lax.broadcasted_iota(jnp.int32, (8, LANES), 0)
    keep = lane_group == place[0] * 2 + place[1]

    def slot_rows(which):
        rows = []
        for t in range(tiles):
            at = t // each * 32 + which * 16 + t % 2 * 8
            rows.append(spread((mine, other)[t % each // 2][at : at + 8], keep, own, slots))
        return rows

    halo_rows, block_rows = slot_rows(0), slot_rows(1)
    halo_index = lax.broadcasted_iota(jnp.int32, (halos, LANES), 0).astype(jnp.float32)
    first = (lax.broadcasted_iota(jnp.int32, (1, LANES), 1) // slots * blocks).astype(jnp.float32)
    for t in range(tiles):
        hit = halo_index == halo_rows[t]
        one_hot[:, t * LANES : (t + 1) * LANES] = jnp.where(hit, 1.0, 0.0).astype(jnp.bfloat16)
    across = lax.broadcasted_iota(jnp.int32, (LANES, halos), 1).astype(jnp.float32)
    for t in range(tiles):
        column = jnp.broadcast_to(halo_rows[t], (LANES, LANES)).T
        for h in range(0, halos, LANES):
            hit = across[:, h : h + LANES] == column
            halo_hot[t * LANES : (t + 1) * LANES, h : h + LANES] = jnp.where(hit, 1.0, 0.0).astype(jnp.bfloat16)
    got = gather_state(centers[...], radii[...], one_hot[...])
    for t in range(tiles):
        slot_state[t] = jnp.concatenate(
            [got[:, t * LANES : (t + 1) * LANES], block_rows[t] + first, jnp.zeros((3, LANES), jnp.float32)], axis=0
        )


def tile_sums(mine, points, t, out, o):
    cx, cy, cz, rad = mine[0:1], mine[1:2], mine[2:3], mine[3:4]
    scale = (SHELLS / 2.0) / jnp.where(rad > 0.0, rad, 1.0)
    ramps = [None] * (SHELLS + 1)
    inner = [None] * 4

    def add(sums, k, value):
        sums[k] = value if sums[k] is None else sums[k] + value

    for p in range(0, BLOCK, 8):
        x = points[t, 0, p : p + 8] - cx
        y = points[t, 1, p : p + 8] - cy
        z = points[t, 2, p : p + 8] - cz
        mass = points[t, 3, p : p + 8]
        scaled = jnp.sqrt(x * x + y * y + z * z) * scale
        half = mass * 0.5
        reach = half - mass * scaled
        for k in range(SHELLS + 1):
            add(ramps, k, jnp.maximum(reach, 0.0))
            if k == SHELLS // 2 - 1:
                weight = jnp.maximum(jnp.minimum(reach + half, mass), 0.0)
            reach = reach + mass
        add(inner, 0, weight)
        add(inner, 1, weight * x)
        add(inner, 2, weight * y)
        add(inner, 3, weight * z)
    for k in range(SHELLS):
        cumulative = ramps[k + 1] - ramps[k] - ramps[0]
        out[o, k : k + 1] = jnp.sum(cumulative, axis=0, keepdims=True)
    for k in range(4):
        out[o, SHELLS + k : SHELLS + k + 1] = jnp.sum(inner[k], axis=0, keepdims=True)


def first_pass(offset, blocks, slot_state, *refs):
    chunks, (points, partial) = refs[:-2], refs[-2:]
    tiles = len(chunks)
    domain = 4 * blocks
    count = chunks[0].shape[0] // 4
    block_index = lax.broadcasted_iota(jnp.int32, (count, LANES), 0).astype(jnp.float32)
    partial[...] = jnp.zeros_like(partial)
    for t in range(tiles):
        hit = block_index == slot_state[offset + t, 4:5]
        pick = jnp.where(hit, 1.0, 0.0).astype(jnp.bfloat16)
        for c in range(4):
            rows = [chunks[t][a + c * blocks : a + (c + 1) * blocks] for a in range(0, chunks[t].shape[0], domain)]
            chosen = jnp.concatenate(rows, axis=0).T
            high, low = split(chosen, 2)
            points[t, c] = jnp.dot(high, pick, preferred_element_type=jnp.float32) + jnp.dot(
                low, pick, preferred_element_type=jnp.float32
            )

    def one_tile(t, carry):
        tile_sums(slot_state[offset + t], points, t, partial, t)
        return carry

    lax.fori_loop(0, tiles, one_tile, 0)


def finish(slabs, one_hot, halo_hot, centers, radii, *refs):
    points, partials = refs[:slabs], refs[slabs : 2 * slabs]
    centers_out, radii_out, profile_out, slot_state, partial = refs[2 * slabs :]
    tiles = slot_state.shape[0]
    each = tiles // slabs

    def advance(center, radius, terms):
        high, low = [part.astype(jnp.float32) for part in split(terms, 2)]
        both = jnp.concatenate([high, low], axis=0).astype(jnp.bfloat16)
        sums = jnp.dot(both, halo_hot[...], preferred_element_type=jnp.float32)
        sums = sums[:ROWS] + sums[ROWS:]
        profile = sums[:SHELLS]
        enclosed = profile[SHELLS // 2 - 1 : SHELLS // 2]
        ratio = (1.0 + enclosed) / (1.0 + radius * radius * radius)
        radius = radius * jnp.exp(jnp.log(ratio) * (1.0 / 3.0))
        center = center + sums[SHELLS + 1 : SHELLS + 4] / jnp.maximum(sums[SHELLS : SHELLS + 1], 1.0)
        return center, radius, profile

    terms = jnp.concatenate([partials[t // each][t % each] for t in range(tiles)], axis=1)
    center, radius, _ = advance(centers[...], radii[...], terms)
    got = gather_state(center, radius, one_hot[...])
    for t in range(tiles):
        slot_state[t, 0:4] = got[:, t * LANES : (t + 1) * LANES]
    partial[...] = jnp.zeros_like(partial)
    for slab in range(slabs):

        def one_tile(t, carry):
            tile_sums(slot_state[slab * each + t], points[slab], t, partial, slab * each + t)
            return carry

        lax.fori_loop(0, each, one_tile, 0)
    terms = jnp.concatenate([partial[t] for t in range(tiles)], axis=1)
    center, radius, profile = advance(center, radius, terms)
    centers_out[...] = center
    radii_out[...] = radius
    profile_out[...] = profile


def step(value, axis, by):
    size = lax.axis_size(axis)
    return lax.ppermute(value, axis, [(i, (i + by) % size) for i in range(size)])


def call(fn, outs, *args):
    specs = [pl.BlockSpec(memory_space=pltpu.SMEM) if a.ndim == 1 else VMEM for a in args]
    out_specs = [VMEM] * len(outs)
    return pl.pallas_call(fn, in_specs=specs, out_specs=out_specs, out_shape=outs, compiler_params=PARAMS)(*args)


def body(positions, masses, centers, radii, pair_block, pair_halo):
    devices = lax.axis_size(AXES)
    halos = radii.shape[0]
    blocks = masses.shape[0] // BLOCK
    slots = pair_halo.shape[0] // devices
    tiles = devices * slots // LANES
    domain = 4 * blocks
    radii = radii[None]
    place = jnp.stack([lax.axis_index(axis) for axis in AXES]).astype(jnp.int32)
    row = lambda a: a.reshape(-1, LANES)
    (payload,) = call(pack, [f32(domain + 2 * tiles, LANES)], positions, row(masses), row(pair_halo), row(pair_block))
    along_z = [payload] + [step(payload, "z", k) for k in range(1, 4)]
    to_y = call(functools.partial(merge_z, slots, domain), [f32(4 * domain + 8, LANES)] * 4, place, *along_z)
    along_y = [step(to_y[k], "y", k) if k else to_y[k] for k in range(4)]
    low, high, index = call(merge_y, [f32(8 * domain, LANES)] * 2 + [f32(32, LANES)], *along_y)
    indices = jnp.concatenate([index, step(index, "x", 1), step(index, "x", 2), step(index, "x", 3)], axis=0)
    below_low, above_high = step(low, "x", 1), step(high, "x", -1)
    below_high, above_low = step(high, "x", 1), step(low, "x", -1)
    far_low, far_high = step(below_low, "x", 1), step(above_high, "x", -1)
    slabs = [(low, high), (below_low, below_high), (far_low, far_high), (above_low, above_high)]
    one_hot, halo_hot, slot_state = call(
        functools.partial(prepare, slots, blocks),
        [
            jax.ShapeDtypeStruct((halos, devices * slots), jnp.bfloat16),
            jax.ShapeDtypeStruct((devices * slots, halos), jnp.bfloat16),
            f32(tiles, 8, LANES),
        ],
        place,
        indices,
        step(indices, "core", 1),
        centers,
        radii,
    )
    each = tiles // len(slabs)
    got = {}
    for i in (0, 1, 3, 2):
        slab = slabs[i]
        if i:
            slab, _ = lax.optimization_barrier((slab, got[0][1]))
        got[i] = call(
            functools.partial(first_pass, i * each, blocks),
            [f32(each, 4, BLOCK, LANES), f32(each, ROWS, LANES)],
            slot_state,
            *slab,
            *[step(half, "core", 1) for half in slab],
        )
    points, partials = zip(*[got[i] for i in range(len(slabs))])
    centers, radii, profile = pl.pallas_call(
        functools.partial(finish, len(slabs)),
        in_specs=[VMEM] * (4 + 2 * len(slabs)),
        out_specs=[VMEM] * 3,
        out_shape=(f32(3, halos), f32(1, halos), f32(SHELLS, halos)),
        scratch_shapes=[pltpu.VMEM((tiles, 8, LANES), jnp.float32), pltpu.VMEM((tiles, ROWS, LANES), jnp.float32)],
        compiler_params=PARAMS,
    )(one_hot, halo_hot, centers, radii, *points, *partials)
    return (centers, radii[0], profile)


def solution(mesh):
    chips = Mesh(mesh.devices.reshape(4, 2, 4, 4), AXES)
    in_specs = (
        P(None, AXES),
        P(AXES),
        P(None, AXES),
        P(AXES),
        P(AXES),
        P(AXES),
    )
    out_specs = (P(None, AXES), P(AXES), P(None, AXES))
    return jax.shard_map(body, mesh=chips, in_specs=in_specs, out_specs=out_specs, check_vma=False)
```

```python
import functools

import jax
import jax.numpy as jnp
from jax import lax
from jax.experimental import pallas as pl
from jax.experimental.pallas import tpu as pltpu
from jax.sharding import Mesh, PartitionSpec as P

SHELLS = 16
BLOCK = 128
LANES = 128
ROWS = 24
AXES = ("x", "core", "y", "z")
VMEM = pl.BlockSpec(memory_space=pltpu.VMEM)
PARAMS = pltpu.CompilerParams(vmem_limit_bytes=16 * 2**20)


def f32(*shape):
    return jax.ShapeDtypeStruct(shape, jnp.float32)


def split(value, terms):
    parts = []
    for _ in range(terms):
        part = value.astype(jnp.bfloat16)
        parts.append(part)
        value = value - part.astype(jnp.float32)
    return parts


def gather_state(state, one_hot):
    stacked = jnp.concatenate([s.astype(jnp.float32) for s in split(state, 3)] + [jnp.zeros_like(state)], axis=0)
    got = jnp.dot(stacked.astype(jnp.bfloat16), one_hot, preferred_element_type=jnp.float32)
    return got[0:4] + got[4:8] + got[8:12]


def spread(rows, keep, own, slots):
    rows = jnp.where(keep, rows, 0.0)
    shift = slots
    while shift < LANES:
        rows = rows + pltpu.roll(rows, shift, 1)
        shift *= 2
    return jnp.sum(jnp.where(own, rows, 0.0), axis=0, keepdims=True)


def pack(positions, masses, halo, block, centers, radii, out, state, *scratch):
    arrays = (positions, masses, halo, block, centers, radii)
    held, sems = scratch[:-1], scratch[-1]
    copies = [pltpu.make_async_copy(a, v, sems.at[n]) for n, (a, v) in enumerate(zip(arrays, held))]
    for copy in copies:
        copy.start()
    for copy in copies:
        copy.wait()
    blocks = masses.shape[0]
    for c in range(3):
        for b in range(blocks):
            out[c * blocks + b : c * blocks + b + 1] = held[0][c : c + 1, b * BLOCK : (b + 1) * BLOCK]
    at = 3 * blocks
    for part in held[1:4]:
        out[at : at + part.shape[0]] = part[...].astype(jnp.float32)
        at += part.shape[0]
    state[0:3] = held[4][...]
    state[3:4] = held[5][...]


def merge_z(slots, width, place, *refs):
    size = len(refs) // 2
    parts, outs = refs[:size], refs[size:]
    index_rows = (parts[0].shape[0] - width) // 2
    row = lax.broadcasted_iota(jnp.int32, (index_rows, LANES), 0)
    group = lax.broadcasted_iota(jnp.int32, (index_rows, LANES), 1) // slots
    for k in range(size):
        for i in range(size):
            outs[k][i * width : (i + 1) * width] = parts[i][:width]
        y = (place[2] + k) % size
        keep = (group == y % 2 * size + place[3]) & (row % 2 == y // 2)
        for which in range(2):
            for i in range(size):
                at = width + which * index_rows
                to = size * width + which * size + i
                outs[k][to : to + 1] = spread(parts[i][at : at + index_rows], keep, group == row // 2, slots)


def merge_y(*refs):
    size = len(refs) - 3
    parts, halves, both = refs[:size], refs[size : size + 2], refs[-1]
    rows = parts[0].shape[0] - 2 * size
    for i in range(size):
        at = i % 2
        for half, start in ((halves[i // 2], 0), (both, i // 2 * halves[0].shape[0])):
            half[start + at * rows : start + (at + 1) * rows] = parts[i][:rows]
            for which in range(2):
                to = start + 2 * rows + which * 2 * size + at * size
                half[to : to + size] = parts[i][rows + which * size : rows + (which + 1) * size]


def tile_sums(mine, points, t, out, o):
    cx, cy, cz, rad = mine[0:1], mine[1:2], mine[2:3], mine[3:4]
    scale = (SHELLS / 2.0) / jnp.where(rad > 0.0, rad, 1.0)
    ramps = [None] * (SHELLS + 1)
    inner = [None] * 4

    def add(sums, k, value):
        sums[k] = value if sums[k] is None else sums[k] + value

    for p in range(0, BLOCK, 8):
        x = points[t, 0, p : p + 8] - cx
        y = points[t, 1, p : p + 8] - cy
        z = points[t, 2, p : p + 8] - cz
        mass = points[t, 3, p : p + 8]
        scaled = jnp.sqrt(x * x + y * y + z * z) * scale
        half = mass * 0.5
        reach = half - mass * scaled
        for k in range(SHELLS + 1):
            add(ramps, k, jnp.maximum(reach, 0.0))
            if k == SHELLS // 2 - 1:
                weight = jnp.maximum(jnp.minimum(reach + half, mass), 0.0)
            reach = reach + mass
        add(inner, 0, weight)
        add(inner, 1, weight * x)
        add(inner, 2, weight * y)
        add(inner, 3, weight * z)
    for k in range(SHELLS):
        cumulative = ramps[k + 1] - ramps[k] - ramps[0]
        out[o, k : k + 1] = jnp.sum(cumulative, axis=0, keepdims=True)
    for k in range(4):
        out[o, SHELLS + k : SHELLS + k + 1] = jnp.sum(inner[k], axis=0, keepdims=True)


def halo_sums(terms, halo_hot):
    high, low = [part.astype(jnp.float32) for part in split(terms, 2)]
    both = jnp.concatenate([high, low], axis=0).astype(jnp.bfloat16)
    sums = jnp.dot(both, halo_hot, preferred_element_type=jnp.float32)
    return sums[:ROWS] + sums[ROWS:]


def first_pass(slots, blocks, place, state, *refs):
    whole, (one_hot, halo_hot, points, sums, slot_state, partial) = refs[:-6], refs[-6:]
    halos = state.shape[1]
    domain = 4 * blocks
    rows = 8 * domain + 16
    chunks = [ref.at[pl.ds(at, rows)] for ref in whole for at in range(0, ref.shape[0], rows)]
    tiles = len(chunks)
    count = 8 * blocks
    lane_group = lax.broadcasted_iota(jnp.int32, (8, LANES), 1) // slots
    own = lane_group == lax.broadcasted_iota(jnp.int32, (8, LANES), 0)
    keep = lane_group == place[0] * 2 + place[1]
    halo_index = lax.broadcasted_iota(jnp.int32, (halos, LANES), 0).astype(jnp.float32)
    across = lax.broadcasted_iota(jnp.int32, (LANES, halos), 1).astype(jnp.float32)
    block_index = lax.broadcasted_iota(jnp.int32, (count, LANES), 0).astype(jnp.float32)
    first = (lax.broadcasted_iota(jnp.int32, (1, LANES), 1) // slots * blocks).astype(jnp.float32)
    for t in range(tiles):
        at = 8 * domain
        halo_row = spread(chunks[t][at : at + 8], keep, own, slots)
        hit = halo_index == halo_row
        one_hot[:, t * LANES : (t + 1) * LANES] = jnp.where(hit, 1.0, 0.0).astype(jnp.bfloat16)
        column = jnp.broadcast_to(halo_row, (LANES, LANES)).T
        for h in range(0, halos, LANES):
            hit = across[:, h : h + LANES] == column
            halo_hot[t * LANES : (t + 1) * LANES, h : h + LANES] = jnp.where(hit, 1.0, 0.0).astype(jnp.bfloat16)
        hit = block_index == spread(chunks[t][at + 8 : at + 16], keep, own, slots) + first
        pick = jnp.where(hit, 1.0, 0.0).astype(jnp.bfloat16)
        for c in range(4):
            parts = [chunks[t][a + c * blocks : a + (c + 1) * blocks] for a in range(0, 8 * domain, domain)]
            chosen = jnp.concatenate(parts, axis=0).T
            high, low = split(chosen, 2)
            points[t, c] = jnp.dot(high, pick, preferred_element_type=jnp.float32) + jnp.dot(
                low, pick, preferred_element_type=jnp.float32
            )
    slab_sums(state[...], one_hot, halo_hot, points, sums, slot_state, partial)


def slab_sums(state, one_hot, halo_hot, points, sums, slot_state, partial):
    tiles = points.shape[0]
    got = gather_state(state, one_hot[...])
    for t in range(tiles):
        slot_state[t, 0:4] = got[:, t * LANES : (t + 1) * LANES]
    partial[...] = jnp.zeros_like(partial)

    def one_tile(t, carry):
        tile_sums(slot_state[t], points, t, partial, t)
        return carry

    lax.fori_loop(0, tiles, one_tile, 0)
    sums[...] = halo_sums(jnp.concatenate([partial[t] for t in range(tiles)], axis=1), halo_hot[...])


def finish(slabs, state, *refs):
    inputs, (centers_out, radii_out, profile_out, held, slot_state, partial) = refs[: 4 * slabs], refs[4 * slabs :]
    parts = [inputs[4 * i : 4 * i + 4] for i in range(slabs)]

    def advance(center, radius, sums):
        profile = sums[:SHELLS]
        enclosed = profile[SHELLS // 2 - 1 : SHELLS // 2]
        ratio = (1.0 + enclosed) / (1.0 + radius * radius * radius)
        radius = radius * jnp.exp(jnp.log(ratio) * (1.0 / 3.0))
        center = center + sums[SHELLS + 1 : SHELLS + 4] / jnp.maximum(sums[SHELLS : SHELLS + 1], 1.0)
        return center, radius, profile

    sums = sum(part[3][...] for part in parts)
    center, radius, _ = advance(state[0:3], state[3:4], sums)
    both = jnp.concatenate([center, radius], axis=0)
    for i, (one_hot, halo_hot, points, _) in enumerate(parts):
        slab_sums(both, one_hot, halo_hot, points, held.at[i], slot_state, partial)
    center, radius, profile = advance(center, radius, sum(held[i] for i in range(slabs)))
    centers_out[...] = center
    radii_out[...] = radius
    profile_out[...] = profile


def step(value, axis, by):
    size = lax.axis_size(axis)
    return lax.ppermute(value, axis, [(i, (i + by) % size) for i in range(size)])


def call(fn, outs, *args, scratch=(), near=True):
    place = VMEM if near else pl.BlockSpec(memory_space=pltpu.HBM)
    specs = [pl.BlockSpec(memory_space=pltpu.SMEM) if a.ndim == 1 else place for a in args]
    out_specs = [VMEM] * len(outs)
    return pl.pallas_call(
        fn, in_specs=specs, out_specs=out_specs, out_shape=outs, scratch_shapes=scratch, compiler_params=PARAMS
    )(*args)


def body(positions, masses, centers, radii, pair_block, pair_halo):
    devices = lax.axis_size(AXES)
    halos = radii.shape[0]
    blocks = masses.shape[0] // BLOCK
    slots = pair_halo.shape[0] // devices
    domain = 4 * blocks
    half = 8 * domain + 16
    place = jnp.stack([lax.axis_index(axis) for axis in AXES]).astype(jnp.int32)
    row = lambda a: a.reshape(-1, LANES)
    inputs = (positions, row(masses), row(pair_halo), row(pair_block), centers, radii[None])
    payload, state = call(
        pack,
        [f32(domain + 2 * row(pair_halo).shape[0], LANES), f32(4, halos)],
        *inputs,
        scratch=[pltpu.VMEM(a.shape, a.dtype) for a in inputs] + [pltpu.SemaphoreType.DMA((len(inputs),))],
        near=False,
    )
    along_z = [payload] + [step(payload, "z", k) for k in range(1, 4)]
    to_y = call(functools.partial(merge_z, slots, domain), [f32(4 * domain + 8, LANES)] * 4, place, *along_z)
    along_y = [step(to_y[k], "y", k) if k else to_y[k] for k in range(4)]
    low, high, both = call(merge_y, [f32(rows, LANES) for rows in (half, half, 2 * half)], *along_y)
    below_low, above_high = step(low, "x", 1), step(high, "x", -1)
    below_high, above_low = step(high, "x", 1), step(low, "x", -1)
    far_low, far_high = step(below_low, "x", 1), step(above_high, "x", -1)
    slabs = [(both,), (below_low, below_high), (far_low, far_high), (above_low, above_high)]
    each = devices * slots // LANES // len(slabs)
    held = [pltpu.VMEM((each, 8, LANES), jnp.float32), pltpu.VMEM((each, ROWS, LANES), jnp.float32)]
    outs = [
        jax.ShapeDtypeStruct((halos, each * LANES), jnp.bfloat16),
        jax.ShapeDtypeStruct((each * LANES, halos), jnp.bfloat16),
        f32(each, 4, BLOCK, LANES),
        f32(ROWS, halos),
    ]
    got = {}
    for i in (0, 1, 3, 2):
        slab = slabs[i]
        if i == 2:
            slab = lax.optimization_barrier((*slab, *[got[k][3] for k in got]))[: len(slab)]
        others = [step(part, "core", 1) for part in slab]
        got[i] = call(functools.partial(first_pass, slots, blocks), outs, place, state, *slab, *others, scratch=held)
    centers, radii, profile = call(
        functools.partial(finish, len(slabs)),
        [f32(3, halos), f32(1, halos), f32(SHELLS, halos)],
        state,
        *[array for i in got for array in got[i]],
        scratch=[pltpu.VMEM((len(slabs), ROWS, halos), jnp.float32), *held],
    )
    return (centers, radii[0], profile)


def solution(mesh):
    chips = Mesh(mesh.devices.reshape(4, 2, 4, 4), AXES)
    in_specs = (
        P(None, AXES),
        P(AXES),
        P(None, AXES),
        P(AXES),
        P(AXES),
        P(AXES),
    )
    out_specs = (P(None, AXES), P(AXES), P(None, AXES))
    return jax.shard_map(body, mesh=chips, in_specs=in_specs, out_specs=out_specs, check_vma=False)
```

```python
import functools

import jax
import jax.numpy as jnp
from jax import lax
from jax.experimental import pallas as pl
from jax.experimental.pallas import tpu as pltpu
from jax.sharding import Mesh, PartitionSpec as P

SHELLS = 16
BLOCK = 128
LANES = 128
ROWS = 24
AXES = ("x", "core", "y", "z")
VMEM = pl.BlockSpec(memory_space=pltpu.VMEM)
PARAMS = pltpu.CompilerParams(vmem_limit_bytes=16 * 2**20)


def f32(*shape):
    return jax.ShapeDtypeStruct(shape, jnp.float32)


def split(value, terms):
    parts = []
    for _ in range(terms):
        part = value.astype(jnp.bfloat16)
        parts.append(part)
        value = value - part.astype(jnp.float32)
    return parts


def gather_state(state, one_hot):
    stacked = jnp.concatenate([s.astype(jnp.float32) for s in split(state, 3)] + [jnp.zeros_like(state)], axis=0)
    got = jnp.dot(stacked.astype(jnp.bfloat16), one_hot, preferred_element_type=jnp.float32)
    return got[0:4] + got[4:8] + got[8:12]


def spread(rows, keep, own, slots):
    rows = jnp.where(keep, rows, 0.0)
    shift = slots
    while shift < LANES:
        rows = rows + pltpu.roll(rows, shift, 1)
        shift *= 2
    return jnp.sum(jnp.where(own, rows, 0.0), axis=0, keepdims=True)


def pack(positions, masses, halo, block, centers, radii, out, state, *scratch):
    arrays = (positions, masses, halo, block, centers, radii)
    held, sems = scratch[:-1], scratch[-1]
    copies = [pltpu.make_async_copy(a, v, sems.at[n]) for n, (a, v) in enumerate(zip(arrays, held))]
    for copy in copies:
        copy.start()
    for copy in copies:
        copy.wait()
    blocks = masses.shape[0]
    for c in range(3):
        for b in range(blocks):
            out[c * blocks + b : c * blocks + b + 1] = held[0][c : c + 1, b * BLOCK : (b + 1) * BLOCK]
    at = 3 * blocks
    for part in held[1:4]:
        out[at : at + part.shape[0]] = part[...].astype(jnp.float32)
        at += part.shape[0]
    state[0:3] = held[4][...]
    state[3:4] = held[5][...]


def merge_z(slots, width, place, *refs):
    size = len(refs) // 2
    parts, outs = refs[:size], refs[size:]
    index_rows = (parts[0].shape[0] - width) // 2
    row = lax.broadcasted_iota(jnp.int32, (index_rows, LANES), 0)
    group = lax.broadcasted_iota(jnp.int32, (index_rows, LANES), 1) // slots
    for k in range(size):
        for i in range(size):
            outs[k][i * width : (i + 1) * width] = parts[i][:width]
        y = (place[2] + k) % size
        keep = (group == y % 2 * size + place[3]) & (row % 2 == y // 2)
        for which in range(2):
            for i in range(size):
                at = width + which * index_rows
                to = size * width + which * size + i
                outs[k][to : to + 1] = spread(parts[i][at : at + index_rows], keep, group == row // 2, slots)


def merge_y(*refs):
    size = len(refs) - 2
    parts, halves = refs[:size], refs[size:]
    rows = parts[0].shape[0] - 2 * size
    for i in range(size):
        half, at = halves[i // 2], i % 2
        half[at * rows : (at + 1) * rows] = parts[i][:rows]
        for which in range(2):
            to = 2 * rows + which * 2 * size + at * size
            half[to : to + size] = parts[i][rows + which * size : rows + (which + 1) * size]


def tile_sums(mine, points, t, out, o):
    cx, cy, cz, rad = mine[0:1], mine[1:2], mine[2:3], mine[3:4]
    scale = (SHELLS / 2.0) / jnp.where(rad > 0.0, rad, 1.0)
    ramps = [None] * (SHELLS + 1)
    inner = [None] * 4

    def add(sums, k, value):
        sums[k] = value if sums[k] is None else sums[k] + value

    for p in range(0, BLOCK, 8):
        x = points[t, 0, p : p + 8] - cx
        y = points[t, 1, p : p + 8] - cy
        z = points[t, 2, p : p + 8] - cz
        mass = points[t, 3, p : p + 8]
        scaled = jnp.sqrt(x * x + y * y + z * z) * scale
        half = mass * 0.5
        reach = half - mass * scaled
        for k in range(SHELLS + 1):
            add(ramps, k, jnp.maximum(reach, 0.0))
            if k == SHELLS // 2 - 1:
                weight = jnp.maximum(jnp.minimum(reach + half, mass), 0.0)
            reach = reach + mass
        add(inner, 0, weight)
        add(inner, 1, weight * x)
        add(inner, 2, weight * y)
        add(inner, 3, weight * z)
    for k in range(SHELLS):
        cumulative = ramps[k + 1] - ramps[k] - ramps[0]
        out[o, k : k + 1] = jnp.sum(cumulative, axis=0, keepdims=True)
    for k in range(4):
        out[o, SHELLS + k : SHELLS + k + 1] = jnp.sum(inner[k], axis=0, keepdims=True)


def halo_sums(terms, halo_hot):
    high, low = [part.astype(jnp.float32) for part in split(terms, 2)]
    both = jnp.concatenate([high, low], axis=0).astype(jnp.bfloat16)
    sums = jnp.dot(both, halo_hot, preferred_element_type=jnp.float32)
    return sums[:ROWS] + sums[ROWS:]


def first_pass(slots, blocks, place, *refs):
    inputs, (one_hot, halo_hot, points, sums, slot_state, partial) = refs[:-6], refs[-6:]
    states, before, halves = inputs[:2], inputs[2:-2], inputs[-2:]
    halos = states[0].shape[1]
    domain = 4 * blocks
    count = 8 * blocks
    lane_group = lax.broadcasted_iota(jnp.int32, (8, LANES), 1) // slots
    own = lane_group == lax.broadcasted_iota(jnp.int32, (8, LANES), 0)
    halo_index = lax.broadcasted_iota(jnp.int32, (halos, LANES), 0).astype(jnp.float32)
    across = lax.broadcasted_iota(jnp.int32, (LANES, halos), 1).astype(jnp.float32)
    block_index = lax.broadcasted_iota(jnp.int32, (count, LANES), 0).astype(jnp.float32)
    first = (lax.broadcasted_iota(jnp.int32, (1, LANES), 1) // slots * blocks).astype(jnp.float32)
    for h, half in enumerate(halves):
        picks = []
        for o in range(2):
            t = o * 2 + h
            at = 8 * domain
            keep = lane_group == place[0] * 2 + (place[1] if o == 0 else 1 - place[1])
            halo_row = spread(half[at : at + 8], keep, own, slots)
            hit = halo_index == halo_row
            one_hot[:, t * LANES : (t + 1) * LANES] = jnp.where(hit, 1.0, 0.0).astype(jnp.bfloat16)
            column = jnp.broadcast_to(halo_row, (LANES, LANES)).T
            for a in range(0, halos, LANES):
                hit = across[:, a : a + LANES] == column
                halo_hot[t * LANES : (t + 1) * LANES, a : a + LANES] = jnp.where(hit, 1.0, 0.0).astype(jnp.bfloat16)
            hit = block_index == spread(half[at + 8 : at + 16], keep, own, slots) + first
            picks.append(jnp.where(hit, 1.0, 0.0).astype(jnp.bfloat16))
        pick = jnp.concatenate(picks, axis=1)
        for c in range(4):
            parts = [half[a + c * blocks : a + (c + 1) * blocks] for a in range(0, 8 * domain, domain)]
            high, low = split(jnp.concatenate(parts, axis=0).T, 2)
            chosen = jnp.dot(high, pick, preferred_element_type=jnp.float32) + jnp.dot(
                low, pick, preferred_element_type=jnp.float32
            )
            for o in range(2):
                points[o * 2 + h, c] = chosen[:, o * LANES : (o + 1) * LANES]
    value = slab_sums([state[...] for state in states], one_hot, halo_hot, points, slot_state, partial)
    for ref in before:
        value = value + ref[...]
    sums[...] = value


def slab_sums(states, one_hot, halo_hot, points, slot_state, partial):
    tiles = points.shape[0]
    each = tiles // 2
    width = each * LANES
    for o in range(2):
        got = gather_state(states[o], one_hot[:, o * width : (o + 1) * width])
        for t in range(each):
            slot_state[o * each + t, 0:4] = got[:, t * LANES : (t + 1) * LANES]
    partial[...] = jnp.zeros_like(partial)

    def one_tile(t, carry):
        tile_sums(slot_state[t], points, t, partial, t)
        return carry

    lax.fori_loop(0, tiles, one_tile, 0)
    sums = []
    for o in range(2):
        terms = jnp.concatenate([partial[o * each + t] for t in range(each)], axis=1)
        sums.append(halo_sums(terms, halo_hot[o * width : (o + 1) * width]))
    return jnp.concatenate(sums, axis=0)


def advance(state, sums):
    center, radius = state[0:3], state[3:4]
    profile = sums[:SHELLS]
    enclosed = profile[SHELLS // 2 - 1 : SHELLS // 2]
    ratio = (1.0 + enclosed) / (1.0 + radius * radius * radius)
    radius = radius * jnp.exp(jnp.log(ratio) * (1.0 / 3.0))
    center = center + sums[SHELLS + 1 : SHELLS + 4] / jnp.maximum(sums[SHELLS : SHELLS + 1], 1.0)
    return center, radius, profile


def second_pass(mine, other, sums, received, *refs):
    inputs, (state, own, partner, slot_state, partial) = refs[:-5], refs[-5:]
    totals = (sums[:ROWS] + received[ROWS:], sums[ROWS:] + received[:ROWS])
    states = [jnp.concatenate(advance(s[...], t)[:2], axis=0) for s, t in zip((mine, other), totals)]
    state[...] = states[0]
    value = None
    for i in range(0, len(inputs), 3):
        part = slab_sums(states, *inputs[i : i + 3], slot_state, partial)
        value = part if value is None else value + part
    own[...] = value[:ROWS]
    partner[...] = value[ROWS:]


def finish(state, own, received, centers_out, radii_out, profile_out):
    centers_out[...], radii_out[...], profile_out[...] = advance(state[...], own[...] + received[...])


def step(value, axis, by):
    size = lax.axis_size(axis)
    return lax.ppermute(value, axis, [(i, (i + by) % size) for i in range(size)])


def call(fn, outs, *args, scratch=(), near=True):
    place = VMEM if near else pl.BlockSpec(memory_space=pltpu.HBM)
    specs = [pl.BlockSpec(memory_space=pltpu.SMEM) if a.ndim == 1 else place for a in args]
    out_specs = [VMEM] * len(outs)
    return pl.pallas_call(
        fn, in_specs=specs, out_specs=out_specs, out_shape=outs, scratch_shapes=scratch, compiler_params=PARAMS
    )(*args)


def body(positions, masses, centers, radii, pair_block, pair_halo):
    devices = lax.axis_size(AXES)
    halos = radii.shape[0]
    blocks = masses.shape[0] // BLOCK
    slots = pair_halo.shape[0] // devices
    domain = 4 * blocks
    place = jnp.stack([lax.axis_index(axis) for axis in AXES]).astype(jnp.int32)
    row = lambda a: a.reshape(-1, LANES)
    inputs = (positions, row(masses), row(pair_halo), row(pair_block), centers, radii[None])
    inputs = [pltpu.with_memory_space_constraint(a, pltpu.HBM) for a in inputs]
    payload, state = call(
        pack,
        [f32(domain + 2 * row(pair_halo).shape[0], LANES), f32(4, halos)],
        *inputs,
        scratch=[pltpu.VMEM(a.shape, a.dtype) for a in inputs] + [pltpu.SemaphoreType.DMA((len(inputs),))],
        near=False,
    )
    other = step(state, "core", 1)
    along_z = [payload] + [step(payload, "z", k) for k in range(1, 4)]
    to_y = call(functools.partial(merge_z, slots, domain), [f32(4 * domain + 8, LANES)] * 4, place, *along_z)
    along_y = [step(to_y[k], "y", k) if k else to_y[k] for k in range(4)]
    low, high = call(merge_y, [f32(8 * domain + 16, LANES)] * 2, *along_y)
    below_low, above_high = step(low, "x", 1), step(high, "x", -1)
    below_high, above_low = step(high, "x", 1), step(low, "x", -1)
    far_low, far_high = step(below_low, "x", 1), step(above_high, "x", -1)
    slabs = [(low, high), (below_low, below_high), (above_low, above_high), (far_low, far_high)]
    each = devices * slots // LANES // len(slabs)
    held = [pltpu.VMEM((each, 8, LANES), jnp.float32), pltpu.VMEM((each, ROWS, LANES), jnp.float32)]
    outs = [
        jax.ShapeDtypeStruct((halos, each * LANES), jnp.bfloat16),
        jax.ShapeDtypeStruct((each * LANES, halos), jnp.bfloat16),
        f32(each, 4, BLOCK, LANES),
        f32(2 * ROWS, halos),
    ]
    kept, sums = [], []
    for slab in slabs:
        *arrays, total = call(functools.partial(first_pass, slots, blocks), outs, place, state, other, *sums, *slab, scratch=held)
        kept.extend(arrays)
        sums = [total]
    state, own, partner = call(
        second_pass,
        [f32(4, halos), f32(ROWS, halos), f32(ROWS, halos)],
        state,
        other,
        sums[0],
        step(sums[0], "core", 1),
        *kept,
        scratch=held,
    )
    outs = [f32(3, halos), f32(1, halos), f32(SHELLS, halos)]
    centers, radii, profile = call(finish, outs, state, own, step(partner, "core", 1))
    return (centers, radii[0], profile)


def solution(mesh):
    chips = Mesh(mesh.devices.reshape(4, 2, 4, 4), AXES)
    in_specs = (
        P(None, AXES),
        P(AXES),
        P(None, AXES),
        P(AXES),
        P(AXES),
        P(AXES),
    )
    out_specs = (P(None, AXES), P(AXES), P(None, AXES))
    return jax.shard_map(body, mesh=chips, in_specs=in_specs, out_specs=out_specs, check_vma=False)
```

```python
import functools

import jax
import jax.numpy as jnp
from jax import lax
from jax.experimental import pallas as pl
from jax.experimental.pallas import tpu as pltpu
from jax.sharding import Mesh, PartitionSpec as P

SHELLS = 16
BLOCK = 128
LANES = 128
ROWS = 24
AXES = ("x", "core", "y", "z")
VMEM = pl.BlockSpec(memory_space=pltpu.VMEM)
PARAMS = pltpu.CompilerParams(vmem_limit_bytes=16 * 2**20)


def f32(*shape):
    return jax.ShapeDtypeStruct(shape, jnp.float32)


def split(value, terms):
    parts = []
    for _ in range(terms):
        part = value.astype(jnp.bfloat16)
        parts.append(part)
        value = value - part.astype(jnp.float32)
    return parts


def gather_state(state, one_hot):
    stacked = jnp.concatenate([s.astype(jnp.float32) for s in split(state, 3)] + [jnp.zeros_like(state)], axis=0)
    got = jnp.dot(stacked.astype(jnp.bfloat16), one_hot, preferred_element_type=jnp.float32)
    return got[0:4] + got[4:8] + got[8:12]


def spread(rows, keep, own, slots):
    rows = jnp.where(keep, rows, 0.0)
    shift = slots
    while shift < LANES:
        rows = rows + pltpu.roll(rows, shift, 1)
        shift *= 2
    return jnp.sum(jnp.where(own, rows, 0.0), axis=0, keepdims=True)


def pack(positions, masses, halo, block, centers, radii, out, state, *scratch):
    arrays = (positions, masses, halo, block, centers, radii)
    held, sems = scratch[:-1], scratch[-1]
    copies = [pltpu.make_async_copy(a, v, sems.at[n]) for n, (a, v) in enumerate(zip(arrays, held))]
    for copy in copies:
        copy.start()
    for copy in copies:
        copy.wait()
    blocks = masses.shape[0]
    for c in range(3):
        for b in range(blocks):
            out[c * blocks + b : c * blocks + b + 1] = held[0][c : c + 1, b * BLOCK : (b + 1) * BLOCK]
    at = 3 * blocks
    for part in held[1:4]:
        out[at : at + part.shape[0]] = part[...].astype(jnp.float32)
        at += part.shape[0]
    state[0:3] = held[4][...]
    state[3:4] = held[5][...]


def merge_z(slots, width, place, *refs):
    size = len(refs) // 2
    parts, outs = refs[:size], refs[size:]
    index_rows = (parts[0].shape[0] - width) // 2
    row = lax.broadcasted_iota(jnp.int32, (index_rows, LANES), 0)
    group = lax.broadcasted_iota(jnp.int32, (index_rows, LANES), 1) // slots
    for k in range(size):
        for i in range(size):
            outs[k][i * width : (i + 1) * width] = parts[i][:width]
        y = (place[2] + k) % size
        keep = (group == y % 2 * size + place[3]) & (row % 2 == y // 2)
        for which in range(2):
            for i in range(size):
                at = width + which * index_rows
                to = size * width + which * size + i
                outs[k][to : to + 1] = spread(parts[i][at : at + index_rows], keep, group == row // 2, slots)


def merge_y(*refs):
    size = len(refs) - 2
    parts, halves = refs[:size], refs[size:]
    rows = parts[0].shape[0] - 2 * size
    for i in range(size):
        half, at = halves[i // 2], i % 2
        half[at * rows : (at + 1) * rows] = parts[i][:rows]
        for which in range(2):
            to = 2 * rows + which * 2 * size + at * size
            half[to : to + size] = parts[i][rows + which * size : rows + (which + 1) * size]


def tile_sums(mine, points, t, out, o):
    cx, cy, cz, rad = mine[0:1], mine[1:2], mine[2:3], mine[3:4]
    scale = (SHELLS / 2.0) / jnp.where(rad > 0.0, rad, 1.0)
    ramps = [None] * (SHELLS + 1)
    inner = [None] * 4

    def add(sums, k, value):
        sums[k] = value if sums[k] is None else sums[k] + value

    for p in range(0, BLOCK, 8):
        x = points[t, 0, p : p + 8] - cx
        y = points[t, 1, p : p + 8] - cy
        z = points[t, 2, p : p + 8] - cz
        mass = points[t, 3, p : p + 8]
        scaled = jnp.sqrt(x * x + y * y + z * z) * scale
        half = mass * 0.5
        reach = half - mass * scaled
        for k in range(SHELLS + 1):
            add(ramps, k, jnp.maximum(reach, 0.0))
            if k == SHELLS // 2 - 1:
                weight = jnp.maximum(jnp.minimum(reach + half, mass), 0.0)
            reach = reach + mass
        add(inner, 0, weight)
        add(inner, 1, weight * x)
        add(inner, 2, weight * y)
        add(inner, 3, weight * z)
    for k in range(SHELLS):
        cumulative = ramps[k + 1] - ramps[k] - ramps[0]
        out[o, k : k + 1] = jnp.sum(cumulative, axis=0, keepdims=True)
    for k in range(4):
        out[o, SHELLS + k : SHELLS + k + 1] = jnp.sum(inner[k], axis=0, keepdims=True)


def halo_sums(terms, halo_hot):
    high, low = [part.astype(jnp.float32) for part in split(terms, 2)]
    both = jnp.concatenate([high, low], axis=0).astype(jnp.bfloat16)
    sums = jnp.dot(both, halo_hot, preferred_element_type=jnp.float32)
    return sums[:ROWS] + sums[ROWS:]


def first_pass(slots, blocks, place, *refs):
    inputs, (one_hot, halo_hot, points, sums, slot_state, partial) = refs[:-6], refs[-6:]
    states, before, halves = inputs[:2], inputs[2:-2], inputs[-2:]
    halos = states[0].shape[1]
    domain = 4 * blocks
    count = 8 * blocks
    lane_group = lax.broadcasted_iota(jnp.int32, (8, LANES), 1) // slots
    own = lane_group == lax.broadcasted_iota(jnp.int32, (8, LANES), 0)
    halo_index = lax.broadcasted_iota(jnp.int32, (halos, LANES), 0).astype(jnp.float32)
    across = lax.broadcasted_iota(jnp.int32, (LANES, halos), 1).astype(jnp.float32)
    block_index = lax.broadcasted_iota(jnp.int32, (count, LANES), 0).astype(jnp.float32)
    first = (lax.broadcasted_iota(jnp.int32, (1, LANES), 1) // slots * blocks).astype(jnp.float32)
    for h, half in enumerate(halves):
        picks = []
        for o in range(2):
            t = o * 2 + h
            at = 8 * domain
            keep = lane_group == place[0] * 2 + (place[1] if o == 0 else 1 - place[1])
            halo_row = spread(half[at : at + 8], keep, own, slots)
            hit = halo_index == halo_row
            one_hot[:, t * LANES : (t + 1) * LANES] = jnp.where(hit, 1.0, 0.0).astype(jnp.bfloat16)
            column = jnp.broadcast_to(halo_row, (LANES, LANES)).T
            for a in range(0, halos, LANES):
                hit = across[:, a : a + LANES] == column
                halo_hot[t * LANES : (t + 1) * LANES, a : a + LANES] = jnp.where(hit, 1.0, 0.0).astype(jnp.bfloat16)
            hit = block_index == spread(half[at + 8 : at + 16], keep, own, slots) + first
            picks.append(jnp.where(hit, 1.0, 0.0).astype(jnp.bfloat16))
        pick = jnp.concatenate(picks, axis=1)
        for c in range(4):
            parts = [half[a + c * blocks : a + (c + 1) * blocks] for a in range(0, 8 * domain, domain)]
            high, low = split(jnp.concatenate(parts, axis=0).T, 2)
            chosen = jnp.dot(high, pick, preferred_element_type=jnp.float32) + jnp.dot(
                low, pick, preferred_element_type=jnp.float32
            )
            for o in range(2):
                points[o * 2 + h, c] = chosen[:, o * LANES : (o + 1) * LANES]
    value = slab_sums([state[...] for state in states], one_hot, halo_hot, points, slot_state, partial)
    for ref in before:
        value = value + ref[...]
    sums[...] = value


def slab_sums(states, one_hot, halo_hot, points, slot_state, partial):
    tiles = points.shape[0]
    each = tiles // 2
    width = each * LANES
    for o in range(2):
        got = gather_state(states[o], one_hot[:, o * width : (o + 1) * width])
        for t in range(each):
            slot_state[o * each + t, 0:4] = got[:, t * LANES : (t + 1) * LANES]
    partial[...] = jnp.zeros_like(partial)

    def one_tile(t, carry):
        tile_sums(slot_state[t], points, t, partial, t)
        return carry

    lax.fori_loop(0, tiles, one_tile, 0)
    sums = []
    for o in range(2):
        terms = jnp.concatenate([partial[o * each + t] for t in range(each)], axis=1)
        sums.append(halo_sums(terms, halo_hot[o * width : (o + 1) * width]))
    return jnp.concatenate(sums, axis=0)


def advance(state, sums):
    center, radius = state[0:3], state[3:4]
    profile = sums[:SHELLS]
    enclosed = profile[SHELLS // 2 - 1 : SHELLS // 2]
    ratio = (1.0 + enclosed) / (1.0 + radius * radius * radius)
    radius = radius * jnp.exp(jnp.log(ratio) * (1.0 / 3.0))
    center = center + sums[SHELLS + 1 : SHELLS + 4] / jnp.maximum(sums[SHELLS : SHELLS + 1], 1.0)
    return center, radius, profile


def second_pass(mine, other, sums, received, *refs):
    inputs, (state, own, partner, slot_state, partial) = refs[:-5], refs[-5:]
    totals = (sums[:ROWS] + received[ROWS:], sums[ROWS:] + received[:ROWS])
    states = [jnp.concatenate(advance(s[...], t)[:2], axis=0) for s, t in zip((mine, other), totals)]
    state[...] = states[0]
    value = None
    for i in range(0, len(inputs), 3):
        part = slab_sums(states, *inputs[i : i + 3], slot_state, partial)
        value = part if value is None else value + part
    own[...] = value[:ROWS]
    partner[...] = value[ROWS:]


def finish(state, own, received, centers_out, radii_out, profile_out):
    centers_out[...], radii_out[...], profile_out[...] = advance(state[...], own[...] + received[...])


def step(value, axis, by):
    size = lax.axis_size(axis)
    return lax.ppermute(value, axis, [(i, (i + by) % size) for i in range(size)])


def call(fn, outs, *args, scratch=(), near=True):
    place = VMEM if near else pl.BlockSpec(memory_space=pltpu.HBM)
    specs = [pl.BlockSpec(memory_space=pltpu.SMEM) if a.ndim == 1 else place for a in args]
    out_specs = [VMEM] * len(outs)
    return pl.pallas_call(
        fn, in_specs=specs, out_specs=out_specs, out_shape=outs, scratch_shapes=scratch, compiler_params=PARAMS
    )(*args)


def body(positions, masses, centers, radii, pair_block, pair_halo):
    devices = lax.axis_size(AXES)
    halos = radii.shape[0]
    blocks = masses.shape[0] // BLOCK
    slots = pair_halo.shape[0] // devices
    domain = 4 * blocks
    place = jnp.stack([lax.axis_index(axis) for axis in AXES]).astype(jnp.int32)
    row = lambda a: a.reshape(-1, LANES)
    inputs = (positions, row(masses), row(pair_halo), row(pair_block), centers, radii[None])
    inputs = [pltpu.with_memory_space_constraint(a, pltpu.HBM) for a in inputs]
    payload, state = call(
        pack,
        [f32(domain + 2 * row(pair_halo).shape[0], LANES), f32(4, halos)],
        *inputs,
        scratch=[pltpu.VMEM(a.shape, a.dtype) for a in inputs] + [pltpu.SemaphoreType.DMA((len(inputs),))],
        near=False,
    )
    other = step(state, "core", 1)
    along_z = [payload] + [step(payload, "z", k) for k in range(1, 4)]
    *along_z, other = lax.optimization_barrier((*along_z, other))
    to_y = call(functools.partial(merge_z, slots, domain), [f32(4 * domain + 8, LANES)] * 4, place, *along_z)
    along_y = [step(to_y[k], "y", k) if k else to_y[k] for k in range(4)]
    low, high = call(merge_y, [f32(8 * domain + 16, LANES)] * 2, *along_y)
    below_low, above_high = step(low, "x", 1), step(high, "x", -1)
    below_high, above_low = step(high, "x", 1), step(low, "x", -1)
    far_low, far_high = step(below_low, "x", 1), step(above_high, "x", -1)
    slabs = [(low, high), (below_low, below_high), (above_low, above_high), (far_low, far_high)]
    each = devices * slots // LANES // len(slabs)
    held = [pltpu.VMEM((each, 8, LANES), jnp.float32), pltpu.VMEM((each, ROWS, LANES), jnp.float32)]
    outs = [
        jax.ShapeDtypeStruct((halos, each * LANES), jnp.bfloat16),
        jax.ShapeDtypeStruct((each * LANES, halos), jnp.bfloat16),
        f32(each, 4, BLOCK, LANES),
        f32(2 * ROWS, halos),
    ]
    kept, sums = [], []
    for slab in slabs:
        *arrays, total = call(functools.partial(first_pass, slots, blocks), outs, place, state, other, *sums, *slab, scratch=held)
        kept.extend(arrays)
        sums = [total]
    state, own, partner = call(
        second_pass,
        [f32(4, halos), f32(ROWS, halos), f32(ROWS, halos)],
        state,
        other,
        sums[0],
        step(sums[0], "core", 1),
        *kept,
        scratch=held,
    )
    outs = [f32(3, halos), f32(1, halos), f32(SHELLS, halos)]
    centers, radii, profile = call(finish, outs, state, own, step(partner, "core", 1))
    return (centers, radii[0], profile)


def solution(mesh):
    chips = Mesh(mesh.devices.reshape(4, 2, 4, 4), AXES)
    in_specs = (
        P(None, AXES),
        P(AXES),
        P(None, AXES),
        P(AXES),
        P(AXES),
        P(AXES),
    )
    out_specs = (P(None, AXES), P(AXES), P(None, AXES))
    return jax.shard_map(body, mesh=chips, in_specs=in_specs, out_specs=out_specs, check_vma=False)
```

```python
import functools

import jax
import jax.numpy as jnp
from jax import lax
from jax.experimental import pallas as pl
from jax.experimental.pallas import tpu as pltpu
from jax.sharding import Mesh, PartitionSpec as P

SHELLS = 16
BLOCK = 128
LANES = 128
ROWS = 24
AXES = ("x", "core", "y", "z")
VMEM = pl.BlockSpec(memory_space=pltpu.VMEM)
PARAMS = pltpu.CompilerParams(vmem_limit_bytes=16 * 2**20)


def f32(*shape):
    return jax.ShapeDtypeStruct(shape, jnp.float32)


def split(value, terms):
    parts = []
    for _ in range(terms):
        part = value.astype(jnp.bfloat16)
        parts.append(part)
        value = value - part.astype(jnp.float32)
    return parts


def gather_state(state, one_hot):
    stacked = jnp.concatenate([s.astype(jnp.float32) for s in split(state, 3)] + [jnp.zeros_like(state)], axis=0)
    got = jnp.dot(stacked.astype(jnp.bfloat16), one_hot, preferred_element_type=jnp.float32)
    return got[0:4] + got[4:8] + got[8:12]


def spread(rows, keep, own, slots):
    rows = jnp.where(keep, rows, 0.0)
    shift = slots
    while shift < LANES:
        rows = rows + pltpu.roll(rows, shift, 1)
        shift *= 2
    return jnp.sum(jnp.where(own, rows, 0.0), axis=0, keepdims=True)


def pack(positions, masses, halo, block, centers, radii, out, state, *scratch):
    arrays = (positions, masses, halo, block, centers, radii)
    held, sems = scratch[:-1], scratch[-1]
    copies = [pltpu.make_async_copy(a, v, sems.at[n]) for n, (a, v) in enumerate(zip(arrays, held))]
    for copy in copies:
        copy.start()
    for copy in copies:
        copy.wait()
    blocks = masses.shape[0]
    for c in range(3):
        for b in range(blocks):
            out[c * blocks + b : c * blocks + b + 1] = held[0][c : c + 1, b * BLOCK : (b + 1) * BLOCK]
    at = 3 * blocks
    for part in held[1:4]:
        out[at : at + part.shape[0]] = part[...].astype(jnp.float32)
        at += part.shape[0]
    state[0:3] = held[4][...]
    state[3:4] = held[5][...]


def merge_z(slots, width, place, *refs):
    parts, outs = refs[:-3], refs[-3:]
    size = len(parts)
    index_rows = (parts[0].shape[0] - width) // 2
    row = lax.broadcasted_iota(jnp.int32, (index_rows, LANES), 0)
    group = lax.broadcasted_iota(jnp.int32, (index_rows, LANES), 1) // slots
    for out, steps in zip(outs, ((0,), (1, 2), (size - 1,))):
        for i in range(size):
            out[i * width : (i + 1) * width] = parts[i][:width]
        for n, k in enumerate(steps):
            y = (place[2] + k) % size
            keep = (group == y % 2 * size + place[3]) & (row % 2 == y // 2)
            for which in range(2):
                for i in range(size):
                    at = width + which * index_rows
                    to = size * width + (2 * n + which) * size + i
                    out[to : to + 1] = spread(parts[i][at : at + index_rows], keep, group == row // 2, slots)


def merge_y(*refs):
    size = len(refs) - 2
    parts, halves = refs[:size], refs[size:]
    rows = parts[0].shape[0] - 2 * size
    for i in range(size):
        half, at = halves[i // 2], i % 2
        start = rows + (2 * size if i == 2 else 0)
        half[at * rows : (at + 1) * rows] = parts[i][:rows]
        for which in range(2):
            to = 2 * rows + which * 2 * size + at * size
            half[to : to + size] = parts[i][start + which * size : start + (which + 1) * size]


def tile_sums(mine, points, t, out, o):
    cx, cy, cz, rad = mine[0:1], mine[1:2], mine[2:3], mine[3:4]
    scale = (SHELLS / 2.0) / jnp.where(rad > 0.0, rad, 1.0)
    ramps = [None] * (SHELLS + 1)
    inner = [None] * 4

    def add(sums, k, value):
        sums[k] = value if sums[k] is None else sums[k] + value

    for p in range(0, BLOCK, 8):
        x = points[t, 0, p : p + 8] - cx
        y = points[t, 1, p : p + 8] - cy
        z = points[t, 2, p : p + 8] - cz
        mass = points[t, 3, p : p + 8]
        scaled = jnp.sqrt(x * x + y * y + z * z) * scale
        half = mass * 0.5
        reach = half - mass * scaled
        for k in range(SHELLS + 1):
            add(ramps, k, jnp.maximum(reach, 0.0))
            if k == SHELLS // 2 - 1:
                weight = jnp.maximum(jnp.minimum(reach + half, mass), 0.0)
            reach = reach + mass
        add(inner, 0, weight)
        add(inner, 1, weight * x)
        add(inner, 2, weight * y)
        add(inner, 3, weight * z)
    for k in range(SHELLS):
        cumulative = ramps[k + 1] - ramps[k] - ramps[0]
        out[o, k : k + 1] = jnp.sum(cumulative, axis=0, keepdims=True)
    for k in range(4):
        out[o, SHELLS + k : SHELLS + k + 1] = jnp.sum(inner[k], axis=0, keepdims=True)


def halo_sums(terms, halo_hot):
    high, low = [part.astype(jnp.float32) for part in split(terms, 2)]
    both = jnp.concatenate([high, low], axis=0).astype(jnp.bfloat16)
    sums = jnp.dot(both, halo_hot, preferred_element_type=jnp.float32)
    return sums[:ROWS] + sums[ROWS:]


def first_pass(slots, blocks, place, *refs):
    inputs, (one_hot, halo_hot, points, sums, slot_state, partial) = refs[:-6], refs[-6:]
    states, before, halves = inputs[:2], inputs[2:-2], inputs[-2:]
    halos = states[0].shape[1]
    domain = 4 * blocks
    count = 8 * blocks
    lane_group = lax.broadcasted_iota(jnp.int32, (8, LANES), 1) // slots
    own = lane_group == lax.broadcasted_iota(jnp.int32, (8, LANES), 0)
    halo_index = lax.broadcasted_iota(jnp.int32, (halos, LANES), 0).astype(jnp.float32)
    across = lax.broadcasted_iota(jnp.int32, (LANES, halos), 1).astype(jnp.float32)
    block_index = lax.broadcasted_iota(jnp.int32, (count, LANES), 0).astype(jnp.float32)
    first = (lax.broadcasted_iota(jnp.int32, (1, LANES), 1) // slots * blocks).astype(jnp.float32)
    for h, half in enumerate(halves):
        picks = []
        for o in range(2):
            t = o * 2 + h
            at = 8 * domain
            keep = lane_group == place[0] * 2 + (place[1] if o == 0 else 1 - place[1])
            halo_row = spread(half[at : at + 8], keep, own, slots)
            hit = halo_index == halo_row
            one_hot[:, t * LANES : (t + 1) * LANES] = jnp.where(hit, 1.0, 0.0).astype(jnp.bfloat16)
            column = jnp.broadcast_to(halo_row, (LANES, LANES)).T
            for a in range(0, halos, LANES):
                hit = across[:, a : a + LANES] == column
                halo_hot[t * LANES : (t + 1) * LANES, a : a + LANES] = jnp.where(hit, 1.0, 0.0).astype(jnp.bfloat16)
            hit = block_index == spread(half[at + 8 : at + 16], keep, own, slots) + first
            picks.append(jnp.where(hit, 1.0, 0.0).astype(jnp.bfloat16))
        pick = jnp.concatenate(picks, axis=1)
        for c in range(4):
            parts = [half[a + c * blocks : a + (c + 1) * blocks] for a in range(0, 8 * domain, domain)]
            high, low = split(jnp.concatenate(parts, axis=0).T, 2)
            chosen = jnp.dot(high, pick, preferred_element_type=jnp.float32) + jnp.dot(
                low, pick, preferred_element_type=jnp.float32
            )
            for o in range(2):
                points[o * 2 + h, c] = chosen[:, o * LANES : (o + 1) * LANES]
    value = slab_sums([state[...] for state in states], one_hot, halo_hot, points, slot_state, partial)
    for ref in before:
        value = value + ref[...]
    sums[...] = value


def slab_sums(states, one_hot, halo_hot, points, slot_state, partial):
    tiles = points.shape[0]
    each = tiles // 2
    width = each * LANES
    for o in range(2):
        got = gather_state(states[o], one_hot[:, o * width : (o + 1) * width])
        for t in range(each):
            slot_state[o * each + t, 0:4] = got[:, t * LANES : (t + 1) * LANES]
    partial[...] = jnp.zeros_like(partial)

    def one_tile(t, carry):
        tile_sums(slot_state[t], points, t, partial, t)
        return carry

    lax.fori_loop(0, tiles, one_tile, 0)
    sums = []
    for o in range(2):
        terms = jnp.concatenate([partial[o * each + t] for t in range(each)], axis=1)
        sums.append(halo_sums(terms, halo_hot[o * width : (o + 1) * width]))
    return jnp.concatenate(sums, axis=0)


def advance(state, sums):
    center, radius = state[0:3], state[3:4]
    profile = sums[:SHELLS]
    enclosed = profile[SHELLS // 2 - 1 : SHELLS // 2]
    ratio = (1.0 + enclosed) / (1.0 + radius * radius * radius)
    radius = radius * jnp.exp(jnp.log(ratio) * (1.0 / 3.0))
    center = center + sums[SHELLS + 1 : SHELLS + 4] / jnp.maximum(sums[SHELLS : SHELLS + 1], 1.0)
    return center, radius, profile


def second_pass(mine, other, sums, received, *refs):
    inputs, (state, own, partner, slot_state, partial) = refs[:-5], refs[-5:]
    totals = (sums[:ROWS] + received[ROWS:], sums[ROWS:] + received[:ROWS])
    states = [jnp.concatenate(advance(s[...], t)[:2], axis=0) for s, t in zip((mine, other), totals)]
    state[...] = states[0]
    value = None
    for i in range(0, len(inputs), 3):
        part = slab_sums(states, *inputs[i : i + 3], slot_state, partial)
        value = part if value is None else value + part
    own[...] = value[:ROWS]
    partner[...] = value[ROWS:]


def finish(state, own, received, centers_out, radii_out, profile_out):
    centers_out[...], radii_out[...], profile_out[...] = advance(state[...], own[...] + received[...])


def step(value, axis, by):
    size = lax.axis_size(axis)
    return lax.ppermute(value, axis, [(i, (i + by) % size) for i in range(size)])


def call(fn, outs, *args, scratch=(), near=True):
    place = VMEM if near else pl.BlockSpec(memory_space=pltpu.HBM)
    specs = [pl.BlockSpec(memory_space=pltpu.SMEM) if a.ndim == 1 else place for a in args]
    out_specs = [VMEM] * len(outs)
    return pl.pallas_call(
        fn, in_specs=specs, out_specs=out_specs, out_shape=outs, scratch_shapes=scratch, compiler_params=PARAMS
    )(*args)


def body(positions, masses, centers, radii, pair_block, pair_halo):
    devices = lax.axis_size(AXES)
    halos = radii.shape[0]
    blocks = masses.shape[0] // BLOCK
    slots = pair_halo.shape[0] // devices
    domain = 4 * blocks
    place = jnp.stack([lax.axis_index(axis) for axis in AXES]).astype(jnp.int32)
    row = lambda a: a.reshape(-1, LANES)
    inputs = (positions, row(masses), row(pair_halo), row(pair_block), centers, radii[None])
    inputs = [pltpu.with_memory_space_constraint(a, pltpu.HBM) for a in inputs]
    payload, state = call(
        pack,
        [f32(domain + 2 * row(pair_halo).shape[0], LANES), f32(4, halos)],
        *inputs,
        scratch=[pltpu.VMEM(a.shape, a.dtype) for a in inputs] + [pltpu.SemaphoreType.DMA((len(inputs),))],
        near=False,
    )
    other = step(state, "core", 1)
    up, down = step(payload, "z", 1), step(payload, "z", -1)
    along_z = lax.optimization_barrier((payload, up, step(up, "z", 1), down, other))
    *along_z, other = along_z
    here, above, below = call(
        functools.partial(merge_z, slots, domain), [f32(4 * domain + rows, LANES) for rows in (8, 16, 8)], place, *along_z
    )
    up, down = step(above, "y", 1), step(below, "y", -1)
    up, down = lax.optimization_barrier((up, down))
    low, high = call(merge_y, [f32(8 * domain + 16, LANES)] * 2, here, up, step(up, "y", 1), down)
    below_low, above_high = step(low, "x", 1), step(high, "x", -1)
    below_high, above_low = step(high, "x", 1), step(low, "x", -1)
    slabs = [(low, high), (below_low, below_high), (above_low, above_high)]
    each = devices * slots // LANES // 4
    held = [pltpu.VMEM((each, 8, LANES), jnp.float32), pltpu.VMEM((each, ROWS, LANES), jnp.float32)]
    outs = [
        jax.ShapeDtypeStruct((halos, each * LANES), jnp.bfloat16),
        jax.ShapeDtypeStruct((each * LANES, halos), jnp.bfloat16),
        f32(each, 4, BLOCK, LANES),
        f32(2 * ROWS, halos),
    ]
    kept, sums = [], []
    for slab in slabs:
        *arrays, total = call(functools.partial(first_pass, slots, blocks), outs, place, state, other, *sums, *slab, scratch=held)
        kept.extend(arrays)
        if not sums:
            first, second, _ = lax.optimization_barrier((below_low, above_high, total))
            slabs.append((step(first, "x", 1), step(second, "x", -1)))
        sums = [total]
    state, own, partner = call(
        second_pass,
        [f32(4, halos), f32(ROWS, halos), f32(ROWS, halos)],
        state,
        other,
        sums[0],
        step(sums[0], "core", 1),
        *kept,
        scratch=held,
    )
    outs = [f32(3, halos), f32(1, halos), f32(SHELLS, halos)]
    centers, radii, profile = call(finish, outs, state, own, step(partner, "core", 1))
    return (centers, radii[0], profile)


def solution(mesh):
    chips = Mesh(mesh.devices.reshape(4, 2, 4, 4), AXES)
    in_specs = (
        P(None, AXES),
        P(AXES),
        P(None, AXES),
        P(AXES),
        P(AXES),
        P(AXES),
    )
    out_specs = (P(None, AXES), P(AXES), P(None, AXES))
    return jax.shard_map(body, mesh=chips, in_specs=in_specs, out_specs=out_specs, check_vma=False)
```

```python
import functools

import jax
import jax.numpy as jnp
from jax import lax
from jax.experimental import pallas as pl
from jax.experimental.pallas import tpu as pltpu
from jax.sharding import Mesh, PartitionSpec as P

SHELLS = 16
BLOCK = 128
LANES = 128
ROWS = 24
AXES = ("x", "core", "y", "z")
VMEM = pl.BlockSpec(memory_space=pltpu.VMEM)
PARAMS = pltpu.CompilerParams(vmem_limit_bytes=16 * 2**20)


def f32(*shape):
    return jax.ShapeDtypeStruct(shape, jnp.float32)


def split(value, terms):
    parts = []
    for _ in range(terms):
        part = value.astype(jnp.bfloat16)
        parts.append(part)
        value = value - part.astype(jnp.float32)
    return parts


def gather_state(state, one_hot):
    stacked = jnp.concatenate([s.astype(jnp.float32) for s in split(state, 3)] + [jnp.zeros_like(state)], axis=0)
    got = jnp.dot(stacked.astype(jnp.bfloat16), one_hot, preferred_element_type=jnp.float32)
    return got[0:4] + got[4:8] + got[8:12]


def spread(rows, keep, own, slots):
    rows = jnp.where(keep, rows, 0.0)
    shift = slots
    while shift < LANES:
        rows = rows + pltpu.roll(rows, shift, 1)
        shift *= 2
    return jnp.sum(jnp.where(own, rows, 0.0), axis=0, keepdims=True)


def pack(positions, masses, halo, block, centers, radii, out, state, *scratch):
    arrays = (positions, masses, halo, block, centers, radii)
    held, sems = scratch[:-1], scratch[-1]
    copies = [pltpu.make_async_copy(a, v, sems.at[n]) for n, (a, v) in enumerate(zip(arrays, held))]
    for copy in copies:
        copy.start()
    for copy in copies:
        copy.wait()
    blocks = masses.shape[0]
    for c in range(3):
        for b in range(blocks):
            out[c * blocks + b : c * blocks + b + 1] = held[0][c : c + 1, b * BLOCK : (b + 1) * BLOCK]
    at = 3 * blocks
    for part in held[1:4]:
        out[at : at + part.shape[0]] = part[...].astype(jnp.float32)
        at += part.shape[0]
    state[0:3] = held[4][...]
    state[3:4] = held[5][...]


def merge_z(slots, width, place, *refs):
    size = len(refs) // 2
    parts, outs = refs[:size], refs[size:]
    index_rows = (parts[0].shape[0] - width) // 2
    row = lax.broadcasted_iota(jnp.int32, (index_rows, LANES), 0)
    group = lax.broadcasted_iota(jnp.int32, (index_rows, LANES), 1) // slots
    for k in range(size):
        for i in range(size):
            outs[k][i * width : (i + 1) * width] = parts[i][:width]
        y = (place[2] + k) % size
        keep = (group == y % 2 * size + place[3]) & (row % 2 == y // 2)
        for which in range(2):
            for i in range(size):
                at = width + which * index_rows
                to = size * width + which * size + i
                outs[k][to : to + 1] = spread(parts[i][at : at + index_rows], keep, group == row // 2, slots)


def merge_y(*refs):
    size = len(refs) - 2
    parts, halves = refs[:size], refs[size:]
    rows = parts[0].shape[0] - 2 * size
    for i in range(size):
        half, at = halves[i // 2], i % 2
        half[at * rows : (at + 1) * rows] = parts[i][:rows]
        for which in range(2):
            to = 2 * rows + which * 2 * size + at * size
            half[to : to + size] = parts[i][rows + which * size : rows + (which + 1) * size]


def tile_sums(mine, points, t, out, o):
    cx, cy, cz, rad = mine[0:1], mine[1:2], mine[2:3], mine[3:4]
    scale = (SHELLS / 2.0) / jnp.where(rad > 0.0, rad, 1.0)
    ramps = [None] * (SHELLS + 1)
    inner = [None] * 4

    def add(sums, k, value):
        sums[k] = value if sums[k] is None else sums[k] + value

    for p in range(0, BLOCK, 8):
        x = points[t, 0, p : p + 8] - cx
        y = points[t, 1, p : p + 8] - cy
        z = points[t, 2, p : p + 8] - cz
        mass = points[t, 3, p : p + 8]
        scaled = jnp.sqrt(x * x + y * y + z * z) * scale
        half = mass * 0.5
        reach = half - mass * scaled
        for k in range(SHELLS + 1):
            add(ramps, k, jnp.maximum(reach, 0.0))
            if k == SHELLS // 2 - 1:
                weight = jnp.maximum(jnp.minimum(reach + half, mass), 0.0)
            reach = reach + mass
        add(inner, 0, weight)
        add(inner, 1, weight * x)
        add(inner, 2, weight * y)
        add(inner, 3, weight * z)
    for k in range(SHELLS):
        cumulative = ramps[k + 1] - ramps[k] - ramps[0]
        out[o, k : k + 1] = jnp.sum(cumulative, axis=0, keepdims=True)
    for k in range(4):
        out[o, SHELLS + k : SHELLS + k + 1] = jnp.sum(inner[k], axis=0, keepdims=True)


def halo_sums(terms, halo_hot):
    high, low = [part.astype(jnp.float32) for part in split(terms, 2)]
    both = jnp.concatenate([high, low], axis=0).astype(jnp.bfloat16)
    sums = jnp.dot(both, halo_hot, preferred_element_type=jnp.float32)
    return sums[:ROWS] + sums[ROWS:]


def first_pass(slots, blocks, place, *refs):
    inputs, (one_hot, halo_hot, points, sums, slot_state, partial) = refs[:-6], refs[-6:]
    states, before, halves = inputs[:2], inputs[2:-2], inputs[-2:]
    halos = states[0].shape[1]
    domain = 4 * blocks
    count = 8 * blocks
    lane_group = lax.broadcasted_iota(jnp.int32, (8, LANES), 1) // slots
    own = lane_group == lax.broadcasted_iota(jnp.int32, (8, LANES), 0)
    halo_index = lax.broadcasted_iota(jnp.int32, (halos, LANES), 0).astype(jnp.float32)
    across = lax.broadcasted_iota(jnp.int32, (LANES, halos), 1).astype(jnp.float32)
    block_index = lax.broadcasted_iota(jnp.int32, (count, LANES), 0).astype(jnp.float32)
    first = (lax.broadcasted_iota(jnp.int32, (1, LANES), 1) // slots * blocks).astype(jnp.float32)
    for h, half in enumerate(halves):
        picks = []
        for o in range(2):
            t = o * 2 + h
            at = 8 * domain
            keep = lane_group == place[0] * 2 + (place[1] if o == 0 else 1 - place[1])
            halo_row = spread(half[at : at + 8], keep, own, slots)
            hit = halo_index == halo_row
            one_hot[:, t * LANES : (t + 1) * LANES] = jnp.where(hit, 1.0, 0.0).astype(jnp.bfloat16)
            column = jnp.broadcast_to(halo_row, (LANES, LANES)).T
            for a in range(0, halos, LANES):
                hit = across[:, a : a + LANES] == column
                halo_hot[t * LANES : (t + 1) * LANES, a : a + LANES] = jnp.where(hit, 1.0, 0.0).astype(jnp.bfloat16)
            hit = block_index == spread(half[at + 8 : at + 16], keep, own, slots) + first
            picks.append(jnp.where(hit, 1.0, 0.0).astype(jnp.bfloat16))
        pick = jnp.concatenate(picks, axis=1)
        for c in range(4):
            parts = [half[a + c * blocks : a + (c + 1) * blocks] for a in range(0, 8 * domain, domain)]
            high, low = split(jnp.concatenate(parts, axis=0).T, 2)
            chosen = jnp.dot(high, pick, preferred_element_type=jnp.float32) + jnp.dot(
                low, pick, preferred_element_type=jnp.float32
            )
            for o in range(2):
                points[o * 2 + h, c] = chosen[:, o * LANES : (o + 1) * LANES]
    value = slab_sums([state[...] for state in states], one_hot, halo_hot, points, slot_state, partial)
    for ref in before:
        value = value + ref[...]
    sums[...] = value


def slab_sums(states, one_hot, halo_hot, points, slot_state, partial):
    tiles = points.shape[0]
    each = tiles // 2
    width = each * LANES
    for o in range(2):
        got = gather_state(states[o], one_hot[:, o * width : (o + 1) * width])
        for t in range(each):
            slot_state[o * each + t, 0:4] = got[:, t * LANES : (t + 1) * LANES]
    partial[...] = jnp.zeros_like(partial)

    def one_tile(t, carry):
        tile_sums(slot_state[t], points, t, partial, t)
        return carry

    lax.fori_loop(0, tiles, one_tile, 0)
    sums = []
    for o in range(2):
        terms = jnp.concatenate([partial[o * each + t] for t in range(each)], axis=1)
        sums.append(halo_sums(terms, halo_hot[o * width : (o + 1) * width]))
    return jnp.concatenate(sums, axis=0)


def advance(state, sums):
    center, radius = state[0:3], state[3:4]
    profile = sums[:SHELLS]
    enclosed = profile[SHELLS // 2 - 1 : SHELLS // 2]
    ratio = (1.0 + enclosed) / (1.0 + radius * radius * radius)
    radius = radius * jnp.exp(jnp.log(ratio) * (1.0 / 3.0))
    center = center + sums[SHELLS + 1 : SHELLS + 4] / jnp.maximum(sums[SHELLS : SHELLS + 1], 1.0)
    return center, radius, profile


def second_pass(mine, other, sums, received, *refs):
    inputs, (state, own, partner, slot_state, partial) = refs[:-5], refs[-5:]
    totals = (sums[:ROWS] + received[ROWS:], sums[ROWS:] + received[:ROWS])
    states = [jnp.concatenate(advance(s[...], t)[:2], axis=0) for s, t in zip((mine, other), totals)]
    state[...] = states[0]
    value = None
    for i in range(0, len(inputs), 3):
        part = slab_sums(states, *inputs[i : i + 3], slot_state, partial)
        value = part if value is None else value + part
    own[...] = value[:ROWS]
    partner[...] = value[ROWS:]


def finish(state, own, received, centers_out, radii_out, profile_out):
    centers_out[...], radii_out[...], profile_out[...] = advance(state[...], own[...] + received[...])


def step(value, axis, by):
    size = lax.axis_size(axis)
    return lax.ppermute(value, axis, [(i, (i + by) % size) for i in range(size)])


def call(fn, outs, *args, scratch=(), near=True):
    place = VMEM if near else pl.BlockSpec(memory_space=pltpu.HBM)
    specs = [pl.BlockSpec(memory_space=pltpu.SMEM) if a.ndim == 1 else place for a in args]
    out_specs = [VMEM] * len(outs)
    return pl.pallas_call(
        fn, in_specs=specs, out_specs=out_specs, out_shape=outs, scratch_shapes=scratch, compiler_params=PARAMS
    )(*args)


def body(positions, masses, centers, radii, pair_block, pair_halo):
    devices = lax.axis_size(AXES)
    halos = radii.shape[0]
    blocks = masses.shape[0] // BLOCK
    slots = pair_halo.shape[0] // devices
    domain = 4 * blocks
    place = jnp.stack([lax.axis_index(axis) for axis in AXES]).astype(jnp.int32)
    row = lambda a: a.reshape(-1, LANES)
    inputs = (positions, row(masses), row(pair_halo), row(pair_block), centers, radii[None])
    inputs = [pltpu.with_memory_space_constraint(a, pltpu.HBM) for a in inputs]
    payload, state = call(
        pack,
        [f32(domain + 2 * row(pair_halo).shape[0], LANES), f32(4, halos)],
        *inputs,
        scratch=[pltpu.VMEM(a.shape, a.dtype) for a in inputs] + [pltpu.SemaphoreType.DMA((len(inputs),))],
        near=False,
    )
    other = step(state, "core", 1)
    along_z = [payload] + [step(payload, "z", k) for k in range(1, 4)]
    *along_z, other = lax.optimization_barrier((*along_z, other))
    to_y = call(functools.partial(merge_z, slots, domain), [f32(4 * domain + 8, LANES)] * 4, place, *along_z)
    along_y = [step(to_y[k], "y", k) if k else to_y[k] for k in range(4)]
    low, high = call(merge_y, [f32(8 * domain + 16, LANES)] * 2, *along_y)
    below_low, above_high = step(low, "x", 1), step(high, "x", -1)
    below_high, above_low = step(high, "x", 1), step(low, "x", -1)
    slabs = [(low, high), (below_low, below_high), (above_low, above_high)]
    each = devices * slots // LANES // 4
    held = [pltpu.VMEM((each, 8, LANES), jnp.float32), pltpu.VMEM((each, ROWS, LANES), jnp.float32)]
    outs = [
        jax.ShapeDtypeStruct((halos, each * LANES), jnp.bfloat16),
        jax.ShapeDtypeStruct((each * LANES, halos), jnp.bfloat16),
        f32(each, 4, BLOCK, LANES),
        f32(2 * ROWS, halos),
    ]
    kept, sums = [], []
    for slab in slabs:
        *arrays, total = call(functools.partial(first_pass, slots, blocks), outs, place, state, other, *sums, *slab, scratch=held)
        kept.extend(arrays)
        if not sums:
            first, second, _ = lax.optimization_barrier((below_low, above_high, total))
            slabs.append((step(first, "x", 1), step(second, "x", -1)))
        sums = [total]
    state, own, partner = call(
        second_pass,
        [f32(4, halos), f32(ROWS, halos), f32(ROWS, halos)],
        state,
        other,
        sums[0],
        step(sums[0], "core", 1),
        *kept,
        scratch=held,
    )
    outs = [f32(3, halos), f32(1, halos), f32(SHELLS, halos)]
    centers, radii, profile = call(finish, outs, state, own, step(partner, "core", 1))
    return (centers, radii[0], profile)


def solution(mesh):
    chips = Mesh(mesh.devices.reshape(4, 2, 4, 4), AXES)
    in_specs = (
        P(None, AXES),
        P(AXES),
        P(None, AXES),
        P(AXES),
        P(AXES),
        P(AXES),
    )
    out_specs = (P(None, AXES), P(AXES), P(None, AXES))
    return jax.shard_map(body, mesh=chips, in_specs=in_specs, out_specs=out_specs, check_vma=False)
```

```python
import functools

import jax
import jax.numpy as jnp
from jax import lax
from jax.experimental import pallas as pl
from jax.experimental.pallas import tpu as pltpu
from jax.sharding import Mesh, PartitionSpec as P

SHELLS = 16
BLOCK = 128
LANES = 128
ROWS = 24
AXES = ("x", "core", "y", "z")
VMEM = pl.BlockSpec(memory_space=pltpu.VMEM)
PARAMS = pltpu.CompilerParams(vmem_limit_bytes=16 * 2**20)


def f32(*shape):
    return jax.ShapeDtypeStruct(shape, jnp.float32)


def split(value, terms):
    parts = []
    for _ in range(terms):
        part = value.astype(jnp.bfloat16)
        parts.append(part)
        value = value - part.astype(jnp.float32)
    return parts


def gather_state(state, one_hot):
    stacked = jnp.concatenate([s.astype(jnp.float32) for s in split(state, 3)] + [jnp.zeros_like(state)], axis=0)
    got = jnp.dot(stacked.astype(jnp.bfloat16), one_hot, preferred_element_type=jnp.float32)
    return got[0:4] + got[4:8] + got[8:12]


def spread(rows, keep, own, slots):
    rows = jnp.where(keep, rows, 0.0)
    shift = slots
    while shift < LANES:
        rows = rows + pltpu.roll(rows, shift, 1)
        shift *= 2
    return jnp.sum(jnp.where(own, rows, 0.0), axis=0, keepdims=True)


def pack(positions, masses, halo, block, centers, radii, out, state, *scratch):
    arrays = (positions, masses, halo, block, centers, radii)
    held, sems = scratch[:-1], scratch[-1]
    copies = [pltpu.make_async_copy(a, v, sems.at[n]) for n, (a, v) in enumerate(zip(arrays, held))]
    for copy in copies:
        copy.start()
    for copy in copies:
        copy.wait()
    blocks = masses.shape[0]
    for c in range(3):
        for b in range(blocks):
            out[c * blocks + b : c * blocks + b + 1] = held[0][c : c + 1, b * BLOCK : (b + 1) * BLOCK]
    at = 3 * blocks
    for part in held[1:4]:
        out[at : at + part.shape[0]] = part[...].astype(jnp.float32)
        at += part.shape[0]
    state[0:3] = held[4][...]
    state[3:4] = held[5][...]


def merge_z(slots, width, place, *refs):
    size = len(refs) // 2
    parts, outs = refs[:size], refs[size:]
    index_rows = (parts[0].shape[0] - width) // 2
    row = lax.broadcasted_iota(jnp.int32, (index_rows, LANES), 0)
    group = lax.broadcasted_iota(jnp.int32, (index_rows, LANES), 1) // slots
    for k in range(size):
        for i in range(size):
            outs[k][i * width : (i + 1) * width] = parts[i][:width]
        y = (place[2] + k) % size
        keep = (group == y % 2 * size + place[3]) & (row % 2 == y // 2)
        for which in range(2):
            for i in range(size):
                at = width + which * index_rows
                to = size * width + which * size + i
                outs[k][to : to + 1] = spread(parts[i][at : at + index_rows], keep, group == row // 2, slots)


def merge_y(*refs):
    size = len(refs) - 2
    parts, halves = refs[:size], refs[size:]
    rows = parts[0].shape[0] - 2 * size
    for i in range(size):
        half, at = halves[i // 2], i % 2
        half[at * rows : (at + 1) * rows] = parts[i][:rows]
        for which in range(2):
            to = 2 * rows + which * 2 * size + at * size
            half[to : to + size] = parts[i][rows + which * size : rows + (which + 1) * size]


def tile_sums(mine, points, t, out, o):
    cx, cy, cz, rad = mine[0:1], mine[1:2], mine[2:3], mine[3:4]
    scale = (SHELLS / 2.0) / jnp.where(rad > 0.0, rad, 1.0)
    ramps = [None] * (SHELLS + 1)
    inner = [None] * 4

    def add(sums, k, value):
        sums[k] = value if sums[k] is None else sums[k] + value

    for p in range(0, BLOCK, 8):
        x = points[t, 0, p : p + 8] - cx
        y = points[t, 1, p : p + 8] - cy
        z = points[t, 2, p : p + 8] - cz
        mass = points[t, 3, p : p + 8]
        scaled = jnp.sqrt(x * x + y * y + z * z) * scale
        half = mass * 0.5
        reach = half - mass * scaled
        for k in range(SHELLS + 1):
            add(ramps, k, jnp.maximum(reach, 0.0))
            if k == SHELLS // 2 - 1:
                weight = jnp.maximum(jnp.minimum(reach + half, mass), 0.0)
            reach = reach + mass
        add(inner, 0, weight)
        add(inner, 1, weight * x)
        add(inner, 2, weight * y)
        add(inner, 3, weight * z)
    rows = [jnp.sum(ramps[k + 1] - ramps[k] - ramps[0], axis=0, keepdims=True) for k in range(SHELLS)]
    rows += [jnp.sum(value, axis=0, keepdims=True) for value in inner]
    rows += [jnp.zeros_like(rows[0])] * (ROWS - len(rows))
    out[o] = jnp.concatenate(rows, axis=0)


def halo_sums(terms, halo_hot):
    high, low = [part.astype(jnp.float32) for part in split(terms, 2)]
    both = jnp.concatenate([high, low], axis=0).astype(jnp.bfloat16)
    sums = jnp.dot(both, halo_hot, preferred_element_type=jnp.float32)
    return sums[:ROWS] + sums[ROWS:]


def first_pass(slots, blocks, place, *refs):
    inputs, (one_hot, halo_hot, points, sums, slot_state, partial) = refs[:-6], refs[-6:]
    states, before, halves = inputs[:2], inputs[2:-2], inputs[-2:]
    halos = states[0].shape[1]
    domain = 4 * blocks
    count = 8 * blocks
    lane_group = lax.broadcasted_iota(jnp.int32, (8, LANES), 1) // slots
    own = lane_group == lax.broadcasted_iota(jnp.int32, (8, LANES), 0)
    halo_index = lax.broadcasted_iota(jnp.int32, (halos, LANES), 0).astype(jnp.float32)
    across = lax.broadcasted_iota(jnp.int32, (LANES, halos), 1).astype(jnp.float32)
    block_index = lax.broadcasted_iota(jnp.int32, (count, LANES), 0).astype(jnp.float32)
    first = (lax.broadcasted_iota(jnp.int32, (1, LANES), 1) // slots * blocks).astype(jnp.float32)
    for h, half in enumerate(halves):
        picks = []
        for o in range(2):
            t = o * 2 + h
            at = 8 * domain
            keep = lane_group == place[0] * 2 + (place[1] if o == 0 else 1 - place[1])
            halo_row = spread(half[at : at + 8], keep, own, slots)
            hit = halo_index == halo_row
            one_hot[:, t * LANES : (t + 1) * LANES] = jnp.where(hit, 1.0, 0.0).astype(jnp.bfloat16)
            column = jnp.broadcast_to(halo_row, (LANES, LANES)).T
            for a in range(0, halos, LANES):
                hit = across[:, a : a + LANES] == column
                halo_hot[t * LANES : (t + 1) * LANES, a : a + LANES] = jnp.where(hit, 1.0, 0.0).astype(jnp.bfloat16)
            hit = block_index == spread(half[at + 8 : at + 16], keep, own, slots) + first
            picks.append(jnp.where(hit, 1.0, 0.0).astype(jnp.bfloat16))
        pick = jnp.concatenate(picks, axis=1)
        pick = jnp.concatenate([pick, pick], axis=0)
        stacked = []
        for c in range(4):
            parts = [half[a + c * blocks : a + (c + 1) * blocks] for a in range(0, 8 * domain, domain)]
            stacked.append(jnp.concatenate(split(jnp.concatenate(parts, axis=0), 2), axis=0))
        chosen = lax.dot_general(
            jnp.concatenate(stacked, axis=1), pick, (((0,), (0,)), ((), ())), preferred_element_type=jnp.float32
        )
        for c in range(4):
            for o in range(2):
                points[o * 2 + h, c] = chosen[c * BLOCK : (c + 1) * BLOCK, o * LANES : (o + 1) * LANES]
    slot_states([state[...] for state in states], one_hot, slot_state)
    slab_terms(points, slot_state, partial)
    value = slab_sums(halo_hot, partial)
    for ref in before:
        value = value + ref[...]
    sums[...] = value


def slot_states(states, one_hot, slot_state):
    tiles = slot_state.shape[0]
    each = tiles // 2
    width = each * LANES
    for o in range(2):
        got = gather_state(states[o], one_hot[:, o * width : (o + 1) * width])
        for t in range(each):
            slot_state[o * each + t, 0:4] = got[:, t * LANES : (t + 1) * LANES]


def slab_terms(points, slot_state, partial):
    for t in range(points.shape[0]):
        tile_sums(slot_state[t], points, t, partial, t)


def slab_sums(halo_hot, partial):
    each = partial.shape[0] // 2
    width = each * LANES
    sums = []
    for o in range(2):
        terms = jnp.concatenate([partial[o * each + t] for t in range(each)], axis=1)
        sums.append(halo_sums(terms, halo_hot[o * width : (o + 1) * width]))
    return jnp.concatenate(sums, axis=0)


def advance(state, sums):
    center, radius = state[0:3], state[3:4]
    profile = sums[:SHELLS]
    enclosed = profile[SHELLS // 2 - 1 : SHELLS // 2]
    ratio = (1.0 + enclosed) / (1.0 + radius * radius * radius)
    radius = radius * jnp.exp(jnp.log(ratio) * (1.0 / 3.0))
    center = center + sums[SHELLS + 1 : SHELLS + 4] / jnp.maximum(sums[SHELLS : SHELLS + 1], 1.0)
    return center, radius, profile


def second_pass(mine, other, sums, received, *refs):
    inputs, (state, own, partner, slot_state, partial) = refs[:-5], refs[-5:]
    totals = (sums[:ROWS] + received[ROWS:], sums[ROWS:] + received[:ROWS])
    states = [jnp.concatenate(advance(s[...], t)[:2], axis=0) for s, t in zip((mine, other), totals)]
    state[...] = states[0]
    one_hots, halo_hots, points = inputs[0::3], inputs[1::3], inputs[2::3]
    slabs = len(points)
    each = points[0].shape[0]
    at = [pl.ds(i * each, each) for i in range(slabs)]
    value = None
    slot_states(states, one_hots[0], slot_state.at[at[0]])
    for i in range(slabs):
        if i + 1 < slabs:
            slot_states(states, one_hots[i + 1], slot_state.at[at[i + 1]])
        if i:
            part = slab_sums(halo_hots[i - 1], partial.at[at[i - 1]])
            value = part if value is None else value + part
        slab_terms(points[i], slot_state.at[at[i]], partial.at[at[i]])
    value = value + slab_sums(halo_hots[-1], partial.at[at[-1]])
    own[...] = value[:ROWS]
    partner[...] = value[ROWS:]


def finish(state, own, received, centers_out, radii_out, profile_out):
    centers_out[...], radii_out[...], profile_out[...] = advance(state[...], own[...] + received[...])


def step(value, axis, by):
    size = lax.axis_size(axis)
    return lax.ppermute(value, axis, [(i, (i + by) % size) for i in range(size)])


def call(fn, outs, *args, scratch=(), near=True):
    place = VMEM if near else pl.BlockSpec(memory_space=pltpu.HBM)
    specs = [pl.BlockSpec(memory_space=pltpu.SMEM) if a.ndim == 1 else place for a in args]
    out_specs = [VMEM] * len(outs)
    return pl.pallas_call(
        fn, in_specs=specs, out_specs=out_specs, out_shape=outs, scratch_shapes=scratch, compiler_params=PARAMS
    )(*args)


def body(positions, masses, centers, radii, pair_block, pair_halo):
    devices = lax.axis_size(AXES)
    halos = radii.shape[0]
    blocks = masses.shape[0] // BLOCK
    slots = pair_halo.shape[0] // devices
    domain = 4 * blocks
    place = jnp.stack([lax.axis_index(axis) for axis in AXES]).astype(jnp.int32)
    row = lambda a: a.reshape(-1, LANES)
    inputs = (positions, row(masses), row(pair_halo), row(pair_block), centers, radii[None])
    inputs = [pltpu.with_memory_space_constraint(a, pltpu.HBM) for a in inputs]
    payload, state = call(
        pack,
        [f32(domain + 2 * row(pair_halo).shape[0], LANES), f32(4, halos)],
        *inputs,
        scratch=[pltpu.VMEM(a.shape, a.dtype) for a in inputs] + [pltpu.SemaphoreType.DMA((len(inputs),))],
        near=False,
    )
    other = step(state, "core", 1)
    along_z = [payload] + [step(payload, "z", k) for k in range(1, 4)]
    *along_z, other = lax.optimization_barrier((*along_z, other))
    to_y = call(functools.partial(merge_z, slots, domain), [f32(4 * domain + 8, LANES)] * 4, place, *along_z)
    along_y = [step(to_y[k], "y", k) if k else to_y[k] for k in range(4)]
    low, high = call(merge_y, [f32(8 * domain + 16, LANES)] * 2, *along_y)
    below_low, above_high = step(low, "x", 1), step(high, "x", -1)
    below_high, above_low = step(high, "x", 1), step(low, "x", -1)
    slabs = [(low, high), (below_low, below_high), (above_low, above_high)]
    each = devices * slots // LANES // 4
    held, all_held = (
        [pltpu.VMEM((n, 8, LANES), jnp.float32), pltpu.VMEM((n, ROWS, LANES), jnp.float32)] for n in (each, 4 * each)
    )
    outs = [
        jax.ShapeDtypeStruct((halos, each * LANES), jnp.bfloat16),
        jax.ShapeDtypeStruct((each * LANES, halos), jnp.bfloat16),
        f32(each, 4, BLOCK, LANES),
        f32(2 * ROWS, halos),
    ]
    kept, sums = [], []
    for slab in slabs:
        *arrays, total = call(functools.partial(first_pass, slots, blocks), outs, place, state, other, *sums, *slab, scratch=held)
        kept.extend(arrays)
        if not sums:
            first, second, _ = lax.optimization_barrier((below_low, above_high, total))
            slabs.append((step(first, "x", 1), step(second, "x", -1)))
        sums = [total]
    state, own, partner = call(
        second_pass,
        [f32(4, halos), f32(ROWS, halos), f32(ROWS, halos)],
        state,
        other,
        sums[0],
        step(sums[0], "core", 1),
        *kept,
        scratch=all_held,
    )
    outs = [f32(3, halos), f32(1, halos), f32(SHELLS, halos)]
    centers, radii, profile = call(finish, outs, state, own, step(partner, "core", 1))
    return (centers, radii[0], profile)


def solution(mesh):
    chips = Mesh(mesh.devices.reshape(4, 2, 4, 4), AXES)
    in_specs = (
        P(None, AXES),
        P(AXES),
        P(None, AXES),
        P(AXES),
        P(AXES),
        P(AXES),
    )
    out_specs = (P(None, AXES), P(AXES), P(None, AXES))
    return jax.shard_map(body, mesh=chips, in_specs=in_specs, out_specs=out_specs, check_vma=False)
```

```python
import functools

import jax
import jax.numpy as jnp
from jax import lax
from jax.experimental import pallas as pl
from jax.experimental.pallas import tpu as pltpu
from jax.sharding import Mesh, PartitionSpec as P

SHELLS = 16
BLOCK = 128
LANES = 128
ROWS = 24
AXES = ("x", "core", "y", "z")
VMEM = pl.BlockSpec(memory_space=pltpu.VMEM)
PARAMS = pltpu.CompilerParams(vmem_limit_bytes=16 * 2**20)


def f32(*shape):
    return jax.ShapeDtypeStruct(shape, jnp.float32)


def split(value, terms):
    parts = []
    for _ in range(terms):
        part = value.astype(jnp.bfloat16)
        parts.append(part)
        value = value - part.astype(jnp.float32)
    return parts


def state_rows(states):
    rows = []
    for state in states:
        rows += [part.astype(jnp.float32) for part in split(state, 3)] + [jnp.zeros_like(state)]
    return jnp.concatenate(rows, axis=0).astype(jnp.bfloat16)


def spread(rows, keep, own, slots):
    rows = jnp.where(keep, rows, 0.0)
    shift = slots
    while shift < LANES:
        rows = rows + pltpu.roll(rows, shift, 1)
        shift *= 2
    return jnp.sum(jnp.where(own, rows, 0.0), axis=0, keepdims=True)


def pack(positions, masses, halo, block, centers, radii, out, state, *scratch):
    arrays = (positions, masses, halo, block, centers, radii)
    held, sems = scratch[:-1], scratch[-1]
    copies = [pltpu.make_async_copy(a, v, sems.at[n]) for n, (a, v) in enumerate(zip(arrays, held))]
    for copy in copies:
        copy.start()
    for copy in copies:
        copy.wait()
    blocks = masses.shape[0]
    for c in range(3):
        for b in range(blocks):
            out[c * blocks + b : c * blocks + b + 1] = held[0][c : c + 1, b * BLOCK : (b + 1) * BLOCK]
    at = 3 * blocks
    for part in held[1:4]:
        out[at : at + part.shape[0]] = part[...].astype(jnp.float32)
        at += part.shape[0]
    state[0:3] = held[4][...]
    state[3:4] = held[5][...]


def merge_z(slots, width, place, *refs):
    size = len(refs) // 2
    parts, outs = refs[:size], refs[size:]
    index_rows = (parts[0].shape[0] - width) // 2
    row = lax.broadcasted_iota(jnp.int32, (index_rows, LANES), 0)
    group = lax.broadcasted_iota(jnp.int32, (index_rows, LANES), 1) // slots
    for k in range(size):
        for i in range(size):
            outs[k][i * width : (i + 1) * width] = parts[i][:width]
        y = (place[2] + k) % size
        keep = (group == y % 2 * size + place[3]) & (row % 2 == y // 2)
        for which in range(2):
            for i in range(size):
                at = width + which * index_rows
                to = size * width + which * size + i
                outs[k][to : to + 1] = spread(parts[i][at : at + index_rows], keep, group == row // 2, slots)


def merge_y(*refs):
    size = len(refs) - 2
    parts, halves = refs[:size], refs[size:]
    rows = parts[0].shape[0] - 2 * size
    for i in range(size):
        half, at = halves[i // 2], i % 2
        half[at * rows : (at + 1) * rows] = parts[i][:rows]
        for which in range(2):
            to = 2 * rows + which * 2 * size + at * size
            half[to : to + size] = parts[i][rows + which * size : rows + (which + 1) * size]


def tile_sums(mine, points, t, out, o):
    cx, cy, cz, rad = mine[0:1], mine[1:2], mine[2:3], mine[3:4]
    scale = (SHELLS / 2.0) / jnp.where(rad > 0.0, rad, 1.0)
    ramps = [None] * (SHELLS + 1)
    inner = [None] * 4

    def add(sums, k, value):
        sums[k] = value if sums[k] is None else sums[k] + value

    for p in range(0, BLOCK, 8):
        x = points[t, 0, p : p + 8] - cx
        y = points[t, 1, p : p + 8] - cy
        z = points[t, 2, p : p + 8] - cz
        mass = points[t, 3, p : p + 8]
        scaled = jnp.sqrt(x * x + y * y + z * z) * scale
        half = mass * 0.5
        reach = half - mass * scaled
        for k in range(SHELLS + 1):
            add(ramps, k, jnp.maximum(reach, 0.0))
            if k == SHELLS // 2 - 1:
                weight = jnp.maximum(jnp.minimum(reach + half, mass), 0.0)
            reach = reach + mass
        add(inner, 0, weight)
        add(inner, 1, weight * x)
        add(inner, 2, weight * y)
        add(inner, 3, weight * z)
    rows = [jnp.sum(ramps[k + 1] - ramps[k] - ramps[0], axis=0, keepdims=True) for k in range(SHELLS)]
    rows += [jnp.sum(value, axis=0, keepdims=True) for value in inner]
    rows += [jnp.zeros_like(rows[0])] * (ROWS - len(rows))
    out[o] = jnp.concatenate(rows, axis=0)


def first_pass(slots, blocks, place, *refs):
    inputs, (one_hot, halo_hot, points, sums, slot_state, partial) = refs[:-6], refs[-6:]
    states, before, half = inputs[:2], inputs[2:-1], inputs[-1]
    halos = states[0].shape[1]
    domain = 4 * blocks
    count = 8 * blocks
    lane_group = lax.broadcasted_iota(jnp.int32, (8, LANES), 1) // slots
    own = lane_group == lax.broadcasted_iota(jnp.int32, (8, LANES), 0)
    halo_index = lax.broadcasted_iota(jnp.int32, (halos, LANES), 0).astype(jnp.float32)
    across = lax.broadcasted_iota(jnp.int32, (LANES, halos), 1).astype(jnp.float32)
    block_index = lax.broadcasted_iota(jnp.int32, (count, LANES), 0).astype(jnp.float32)
    first = (lax.broadcasted_iota(jnp.int32, (1, LANES), 1) // slots * blocks).astype(jnp.float32)
    picks = []
    for o in range(2):
        t = o
        at = 8 * domain
        keep = lane_group == place[0] * 2 + (place[1] if o == 0 else 1 - place[1])
        halo_row = spread(half[at : at + 8], keep, own, slots)
        hit = halo_index == halo_row
        one_hot[:, t * LANES : (t + 1) * LANES] = jnp.where(hit, 1.0, 0.0).astype(jnp.bfloat16)
        column = jnp.broadcast_to(halo_row, (LANES, LANES)).T
        for a in range(0, halos, LANES):
            hit = across[:, a : a + LANES] == column
            halo_hot[t * LANES : (t + 1) * LANES, a : a + LANES] = jnp.where(hit, 1.0, 0.0).astype(jnp.bfloat16)
        hit = block_index == spread(half[at + 8 : at + 16], keep, own, slots) + first
        picks.append(jnp.where(hit, 1.0, 0.0).astype(jnp.bfloat16))
    pick = jnp.concatenate(picks, axis=1)
    pick = jnp.concatenate([pick, pick], axis=0)
    stacked = []
    for c in range(4):
        parts = [half[a + c * blocks : a + (c + 1) * blocks] for a in range(0, 8 * domain, domain)]
        stacked.append(jnp.concatenate(split(jnp.concatenate(parts, axis=0), 2), axis=0))
    chosen = lax.dot_general(
        jnp.concatenate(stacked, axis=1), pick, (((0,), (0,)), ((), ())), preferred_element_type=jnp.float32
    )
    for c in range(4):
        for o in range(2):
            points[o, c] = chosen[c * BLOCK : (c + 1) * BLOCK, o * LANES : (o + 1) * LANES]
    slot_states(state_rows([state[...] for state in states]), one_hot, slot_state)
    slab_terms(points, slot_state, partial)
    value = slab_sums(halo_hot, partial)
    for ref in before:
        value = value + ref[...]
    sums[...] = value


def slot_states(rows, one_hot, slot_state):
    got = jnp.dot(rows, one_hot[...], preferred_element_type=jnp.float32)
    for o in range(2):
        part = got[o * 16 : (o + 1) * 16, o * LANES : (o + 1) * LANES]
        slot_state[o, 0:4] = part[0:4] + part[4:8] + part[8:12]


def slab_terms(points, slot_state, partial):
    for t in range(points.shape[0]):
        tile_sums(slot_state[t], points, t, partial, t)


def slab_sums(halo_hot, partial):
    rows = []
    for o in range(2):
        for part in split(partial[o], 2):
            value = part.astype(jnp.float32)
            zero = jnp.zeros_like(value)
            rows.append(jnp.concatenate([value, zero] if o == 0 else [zero, value], axis=1))
    sums = jnp.dot(jnp.concatenate(rows, axis=0).astype(jnp.bfloat16), halo_hot[...], preferred_element_type=jnp.float32)
    return jnp.concatenate([sums[:ROWS] + sums[ROWS : 2 * ROWS], sums[2 * ROWS : 3 * ROWS] + sums[3 * ROWS :]], axis=0)


def advance(state, sums):
    center, radius = state[0:3], state[3:4]
    profile = sums[:SHELLS]
    enclosed = profile[SHELLS // 2 - 1 : SHELLS // 2]
    ratio = (1.0 + enclosed) / (1.0 + radius * radius * radius)
    radius = radius * jnp.exp(jnp.log(ratio) * (1.0 / 3.0))
    center = center + sums[SHELLS + 1 : SHELLS + 4] / jnp.maximum(sums[SHELLS : SHELLS + 1], 1.0)
    return center, radius, profile


def second_pass(mine, other, sums, received, *refs):
    inputs, (state, own, partner, slot_state, partial) = refs[:-5], refs[-5:]
    totals = (sums[:ROWS] + received[ROWS:], sums[ROWS:] + received[:ROWS])
    states = [jnp.concatenate(advance(s[...], t)[:2], axis=0) for s, t in zip((mine, other), totals)]
    state[...] = states[0]
    one_hots, halo_hots, points = inputs[0::3], inputs[1::3], inputs[2::3]
    slabs = len(points)
    each = points[0].shape[0]
    at = [pl.ds(i * each, each) for i in range(slabs)]
    value = None
    rows = state_rows(states)
    slot_states(rows, one_hots[0], slot_state.at[at[0]])
    for i in range(slabs):
        if i + 1 < slabs:
            slot_states(rows, one_hots[i + 1], slot_state.at[at[i + 1]])
        if i:
            part = slab_sums(halo_hots[i - 1], partial.at[at[i - 1]])
            value = part if value is None else value + part
        slab_terms(points[i], slot_state.at[at[i]], partial.at[at[i]])
    value = value + slab_sums(halo_hots[-1], partial.at[at[-1]])
    own[...] = value[:ROWS]
    partner[...] = value[ROWS:]


def finish(state, own, received, centers_out, radii_out, profile_out):
    centers_out[...], radii_out[...], profile_out[...] = advance(state[...], own[...] + received[...])


def step(value, axis, by):
    size = lax.axis_size(axis)
    return lax.ppermute(value, axis, [(i, (i + by) % size) for i in range(size)])


def call(fn, outs, *args, scratch=(), near=True):
    place = VMEM if near else pl.BlockSpec(memory_space=pltpu.HBM)
    specs = [pl.BlockSpec(memory_space=pltpu.SMEM) if a.ndim == 1 else place for a in args]
    out_specs = [VMEM] * len(outs)
    return pl.pallas_call(
        fn, in_specs=specs, out_specs=out_specs, out_shape=outs, scratch_shapes=scratch, compiler_params=PARAMS
    )(*args)


def body(positions, masses, centers, radii, pair_block, pair_halo):
    devices = lax.axis_size(AXES)
    halos = radii.shape[0]
    blocks = masses.shape[0] // BLOCK
    slots = pair_halo.shape[0] // devices
    domain = 4 * blocks
    place = jnp.stack([lax.axis_index(axis) for axis in AXES]).astype(jnp.int32)
    row = lambda a: a.reshape(-1, LANES)
    inputs = (positions, row(masses), row(pair_halo), row(pair_block), centers, radii[None])
    inputs = [pltpu.with_memory_space_constraint(a, pltpu.HBM) for a in inputs]
    payload, state = call(
        pack,
        [f32(domain + 2 * row(pair_halo).shape[0], LANES), f32(4, halos)],
        *inputs,
        scratch=[pltpu.VMEM(a.shape, a.dtype) for a in inputs] + [pltpu.SemaphoreType.DMA((len(inputs),))],
        near=False,
    )
    other = step(state, "core", 1)
    along_z = [payload] + [step(payload, "z", k) for k in range(1, 4)]
    *along_z, other = lax.optimization_barrier((*along_z, other))
    to_y = call(functools.partial(merge_z, slots, domain), [f32(4 * domain + 8, LANES)] * 4, place, *along_z)
    along_y = [step(to_y[k], "y", k) if k else to_y[k] for k in range(4)]
    low, high = call(merge_y, [f32(8 * domain + 16, LANES)] * 2, *along_y)
    below_low, above_high = step(low, "x", 1), step(high, "x", -1)
    below_high, above_low = step(high, "x", 1), step(low, "x", -1)
    halves = [low, high, below_low, above_high, below_high, above_low]
    each = 2
    units = devices * slots // LANES // each
    held, all_held = (
        [pltpu.VMEM((n, 8, LANES), jnp.float32), pltpu.VMEM((n, ROWS, LANES), jnp.float32)] for n in (each, units * each)
    )
    outs = [
        jax.ShapeDtypeStruct((halos, each * LANES), jnp.bfloat16),
        jax.ShapeDtypeStruct((each * LANES, halos), jnp.bfloat16),
        f32(each, 4, BLOCK, LANES),
        f32(2 * ROWS, halos),
    ]
    kept, sums = [], []
    for n in range(units):
        *arrays, total = call(functools.partial(first_pass, slots, blocks), outs, place, state, other, *sums, halves[n], scratch=held)
        kept.extend(arrays)
        if n == 1:
            first, second, _ = lax.optimization_barrier((below_low, above_high, total))
            halves += [step(first, "x", 1), step(second, "x", -1)]
        sums = [total]
    state, own, partner = call(
        second_pass,
        [f32(4, halos), f32(ROWS, halos), f32(ROWS, halos)],
        state,
        other,
        sums[0],
        step(sums[0], "core", 1),
        *kept,
        scratch=all_held,
    )
    outs = [f32(3, halos), f32(1, halos), f32(SHELLS, halos)]
    centers, radii, profile = call(finish, outs, state, own, step(partner, "core", 1))
    return (centers, radii[0], profile)


def solution(mesh):
    chips = Mesh(mesh.devices.reshape(4, 2, 4, 4), AXES)
    in_specs = (
        P(None, AXES),
        P(AXES),
        P(None, AXES),
        P(AXES),
        P(AXES),
        P(AXES),
    )
    out_specs = (P(None, AXES), P(AXES), P(None, AXES))
    return jax.shard_map(body, mesh=chips, in_specs=in_specs, out_specs=out_specs, check_vma=False)
```

```python
import functools

import jax
import jax.numpy as jnp
from jax import lax
from jax.experimental import pallas as pl
from jax.experimental.pallas import tpu as pltpu
from jax.sharding import Mesh, PartitionSpec as P

SHELLS = 16
BLOCK = 128
LANES = 128
ROWS = 24
AXES = ("x", "core", "y", "z")
VMEM = pl.BlockSpec(memory_space=pltpu.VMEM)
PARAMS = pltpu.CompilerParams(vmem_limit_bytes=16 * 2**20)


def f32(*shape):
    return jax.ShapeDtypeStruct(shape, jnp.float32)


def split(value, terms):
    parts = []
    for _ in range(terms):
        part = value.astype(jnp.bfloat16)
        parts.append(part)
        value = value - part.astype(jnp.float32)
    return parts


def gather_state(state, one_hot):
    stacked = jnp.concatenate([s.astype(jnp.float32) for s in split(state, 3)] + [jnp.zeros_like(state)], axis=0)
    got = jnp.dot(stacked.astype(jnp.bfloat16), one_hot, preferred_element_type=jnp.float32)
    return got[0:4] + got[4:8] + got[8:12]


def spread(rows, keep, own, slots):
    rows = jnp.where(keep, rows, 0.0)
    shift = slots
    while shift < LANES:
        rows = rows + pltpu.roll(rows, shift, 1)
        shift *= 2
    return jnp.sum(jnp.where(own, rows, 0.0), axis=0, keepdims=True)


def pack(positions, masses, halo, block, centers, radii, out, state, *scratch):
    arrays = (positions, masses, halo, block, centers, radii)
    held, sems = scratch[:-1], scratch[-1]
    copies = [pltpu.make_async_copy(a, v, sems.at[n]) for n, (a, v) in enumerate(zip(arrays, held))]
    for copy in copies:
        copy.start()
    for copy in copies:
        copy.wait()
    blocks = masses.shape[0]
    for c in range(3):
        for b in range(blocks):
            out[c * blocks + b : c * blocks + b + 1] = held[0][c : c + 1, b * BLOCK : (b + 1) * BLOCK]
    at = 3 * blocks
    for part in held[1:4]:
        out[at : at + part.shape[0]] = part[...].astype(jnp.float32)
        at += part.shape[0]
    state[0:3] = held[4][...]
    state[3:4] = held[5][...]


def merge_z(slots, width, place, *refs):
    size = len(refs) // 2
    parts, outs = refs[:size], refs[size:]
    index_rows = (parts[0].shape[0] - width) // 2
    row = lax.broadcasted_iota(jnp.int32, (index_rows, LANES), 0)
    group = lax.broadcasted_iota(jnp.int32, (index_rows, LANES), 1) // slots
    for k in range(size):
        for i in range(size):
            outs[k][i * width : (i + 1) * width] = parts[i][:width]
        y = (place[2] + k) % size
        keep = (group == y % 2 * size + place[3]) & (row % 2 == y // 2)
        for which in range(2):
            for i in range(size):
                at = width + which * index_rows
                to = size * width + which * size + i
                outs[k][to : to + 1] = spread(parts[i][at : at + index_rows], keep, group == row // 2, slots)


def merge_y(*refs):
    size = len(refs) - 2
    parts, halves = refs[:size], refs[size:]
    rows = parts[0].shape[0] - 2 * size
    for i in range(size):
        half, at = halves[i // 2], i % 2
        half[at * rows : (at + 1) * rows] = parts[i][:rows]
        for which in range(2):
            to = 2 * rows + which * 2 * size + at * size
            half[to : to + size] = parts[i][rows + which * size : rows + (which + 1) * size]


def tile_sums(mine, points, t, out, o):
    cx, cy, cz, rad = mine[0:1], mine[1:2], mine[2:3], mine[3:4]
    scale = (SHELLS / 2.0) / jnp.where(rad > 0.0, rad, 1.0)
    ramps = [None] * (SHELLS + 1)
    inner = [None] * 4

    def add(sums, k, value):
        sums[k] = value if sums[k] is None else sums[k] + value

    for p in range(0, BLOCK, 8):
        x = points[t, 0, p : p + 8] - cx
        y = points[t, 1, p : p + 8] - cy
        z = points[t, 2, p : p + 8] - cz
        mass = points[t, 3, p : p + 8]
        scaled = jnp.sqrt(x * x + y * y + z * z) * scale
        half = mass * 0.5
        reach = half - mass * scaled
        for k in range(SHELLS + 1):
            add(ramps, k, jnp.maximum(reach, 0.0))
            if k == SHELLS // 2 - 1:
                weight = jnp.maximum(jnp.minimum(reach + half, mass), 0.0)
            reach = reach + mass
        add(inner, 0, weight)
        add(inner, 1, weight * x)
        add(inner, 2, weight * y)
        add(inner, 3, weight * z)
    rows = [jnp.sum(ramps[k + 1] - ramps[k] - ramps[0], axis=0, keepdims=True) for k in range(SHELLS)]
    rows += [jnp.sum(value, axis=0, keepdims=True) for value in inner]
    rows += [jnp.zeros_like(rows[0])] * (ROWS - len(rows))
    out[o] = jnp.concatenate(rows, axis=0)


def halo_sums(terms, halo_hot):
    high, low = [part.astype(jnp.float32) for part in split(terms, 2)]
    both = jnp.concatenate([high, low], axis=0).astype(jnp.bfloat16)
    sums = jnp.dot(both, halo_hot, preferred_element_type=jnp.float32)
    return sums[:ROWS] + sums[ROWS:]


def first_pass(slots, blocks, place, *refs):
    inputs, (one_hot, halo_hot, points, sums, slot_state, partial) = refs[:-6], refs[-6:]
    states, before, halves = inputs[:2], inputs[2:-2], inputs[-2:]
    halos = states[0].shape[1]
    domain = 4 * blocks
    count = 8 * blocks
    lane_group = lax.broadcasted_iota(jnp.int32, (8, LANES), 1) // slots
    own = lane_group == lax.broadcasted_iota(jnp.int32, (8, LANES), 0)
    halo_index = lax.broadcasted_iota(jnp.int32, (halos, LANES), 0).astype(jnp.float32)
    across = lax.broadcasted_iota(jnp.int32, (LANES, halos), 1).astype(jnp.float32)
    block_index = lax.broadcasted_iota(jnp.int32, (count, LANES), 0).astype(jnp.float32)
    first = (lax.broadcasted_iota(jnp.int32, (1, LANES), 1) // slots * blocks).astype(jnp.float32)
    for h, half in enumerate(halves):
        picks = []
        for o in range(2):
            t = o * 2 + h
            at = 8 * domain
            keep = lane_group == place[0] * 2 + (place[1] if o == 0 else 1 - place[1])
            halo_row = spread(half[at : at + 8], keep, own, slots)
            hit = halo_index == halo_row
            one_hot[:, t * LANES : (t + 1) * LANES] = jnp.where(hit, 1.0, 0.0).astype(jnp.bfloat16)
            column = jnp.broadcast_to(halo_row, (LANES, LANES)).T
            for a in range(0, halos, LANES):
                hit = across[:, a : a + LANES] == column
                halo_hot[t * LANES : (t + 1) * LANES, a : a + LANES] = jnp.where(hit, 1.0, 0.0).astype(jnp.bfloat16)
            hit = block_index == spread(half[at + 8 : at + 16], keep, own, slots) + first
            picks.append(jnp.where(hit, 1.0, 0.0).astype(jnp.bfloat16))
        pick = jnp.concatenate(picks, axis=1)
        pick = jnp.concatenate([pick, pick], axis=0)
        stacked = []
        for c in range(4):
            parts = [half[a + c * blocks : a + (c + 1) * blocks] for a in range(0, 8 * domain, domain)]
            stacked.append(jnp.concatenate(split(jnp.concatenate(parts, axis=0), 2), axis=0))
        chosen = lax.dot_general(
            jnp.concatenate(stacked, axis=1), pick, (((0,), (0,)), ((), ())), preferred_element_type=jnp.float32
        )
        for c in range(4):
            for o in range(2):
                points[o * 2 + h, c] = chosen[c * BLOCK : (c + 1) * BLOCK, o * LANES : (o + 1) * LANES]
    slot_states([state[...] for state in states], one_hot, slot_state)
    slab_terms(points, slot_state, partial)
    value = slab_sums(halo_hot, partial)
    for ref in before:
        value = value + ref[...]
    sums[...] = value


def slot_states(states, one_hot, slot_state):
    tiles = slot_state.shape[0]
    each = tiles // 2
    width = each * LANES
    for o in range(2):
        got = gather_state(states[o], one_hot[:, o * width : (o + 1) * width])
        for t in range(each):
            slot_state[o * each + t, 0:4] = got[:, t * LANES : (t + 1) * LANES]


def slab_terms(points, slot_state, partial):
    for t in range(points.shape[0]):
        tile_sums(slot_state[t], points, t, partial, t)


def slab_sums(halo_hot, partial):
    each = partial.shape[0] // 2
    width = each * LANES
    sums = []
    for o in range(2):
        terms = jnp.concatenate([partial[o * each + t] for t in range(each)], axis=1)
        sums.append(halo_sums(terms, halo_hot[o * width : (o + 1) * width]))
    return jnp.concatenate(sums, axis=0)


def advance(state, sums):
    center, radius = state[0:3], state[3:4]
    profile = sums[:SHELLS]
    enclosed = profile[SHELLS // 2 - 1 : SHELLS // 2]
    ratio = (1.0 + enclosed) / (1.0 + radius * radius * radius)
    radius = radius * jnp.exp(jnp.log(ratio) * (1.0 / 3.0))
    center = center + sums[SHELLS + 1 : SHELLS + 4] / jnp.maximum(sums[SHELLS : SHELLS + 1], 1.0)
    return center, radius, profile


def second_pass(mine, other, sums, received, *refs):
    inputs, (state, own, partner, slot_state, partial) = refs[:-5], refs[-5:]
    totals = (sums[:ROWS] + received[ROWS:], sums[ROWS:] + received[:ROWS])
    states = [jnp.concatenate(advance(s[...], t)[:2], axis=0) for s, t in zip((mine, other), totals)]
    state[...] = states[0]
    one_hots, halo_hots, points = inputs[0::3], inputs[1::3], inputs[2::3]
    slabs = len(points)
    each = points[0].shape[0]
    at = [pl.ds(i * each, each) for i in range(slabs)]
    value = None
    slot_states(states, one_hots[0], slot_state.at[at[0]])
    for i in range(slabs):
        if i + 1 < slabs:
            slot_states(states, one_hots[i + 1], slot_state.at[at[i + 1]])
        if i:
            part = slab_sums(halo_hots[i - 1], partial.at[at[i - 1]])
            value = part if value is None else value + part
        slab_terms(points[i], slot_state.at[at[i]], partial.at[at[i]])
    value = value + slab_sums(halo_hots[-1], partial.at[at[-1]])
    own[...] = value[:ROWS]
    partner[...] = value[ROWS:]


def finish(state, own, received, centers_out, radii_out, profile_out):
    centers_out[...], radii_out[...], profile_out[...] = advance(state[...], own[...] + received[...])


def step(value, axis, by):
    size = lax.axis_size(axis)
    return lax.ppermute(value, axis, [(i, (i + by) % size) for i in range(size)])


def call(fn, outs, *args, scratch=(), near=True):
    place = VMEM if near else pl.BlockSpec(memory_space=pltpu.HBM)
    specs = [pl.BlockSpec(memory_space=pltpu.SMEM) if a.ndim == 1 else place for a in args]
    out_specs = [VMEM] * len(outs)
    return pl.pallas_call(
        fn, in_specs=specs, out_specs=out_specs, out_shape=outs, scratch_shapes=scratch, compiler_params=PARAMS
    )(*args)


def body(positions, masses, centers, radii, pair_block, pair_halo):
    devices = lax.axis_size(AXES)
    halos = radii.shape[0]
    blocks = masses.shape[0] // BLOCK
    slots = pair_halo.shape[0] // devices
    domain = 4 * blocks
    place = jnp.stack([lax.axis_index(axis) for axis in AXES]).astype(jnp.int32)
    row = lambda a: a.reshape(-1, LANES)
    inputs = (positions, row(masses), row(pair_halo), row(pair_block), centers, radii[None])
    inputs = [pltpu.with_memory_space_constraint(a, pltpu.HBM) for a in inputs]
    payload, state = call(
        pack,
        [f32(domain + 2 * row(pair_halo).shape[0], LANES), f32(4, halos)],
        *inputs,
        scratch=[pltpu.VMEM(a.shape, a.dtype) for a in inputs] + [pltpu.SemaphoreType.DMA((len(inputs),))],
        near=False,
    )
    other = step(state, "core", 1)
    along_z = [payload] + [step(payload, "z", k) for k in range(1, 4)]
    *along_z, other = lax.optimization_barrier((*along_z, other))
    to_y = call(functools.partial(merge_z, slots, domain), [f32(4 * domain + 8, LANES)] * 4, place, *along_z)
    along_y = [step(to_y[k], "y", k) if k else to_y[k] for k in range(4)]
    low, high = call(merge_y, [f32(8 * domain + 16, LANES)] * 2, *along_y)
    below_low, above_high = step(low, "x", 1), step(high, "x", -1)
    below_high, above_low = step(high, "x", 1), step(low, "x", -1)
    slabs = [(low, high), (below_low, above_high), (below_high, above_low)]
    each = devices * slots // LANES // 4
    held, all_held = (
        [pltpu.VMEM((n, 8, LANES), jnp.float32), pltpu.VMEM((n, ROWS, LANES), jnp.float32)] for n in (each, 4 * each)
    )
    outs = [
        jax.ShapeDtypeStruct((halos, each * LANES), jnp.bfloat16),
        jax.ShapeDtypeStruct((each * LANES, halos), jnp.bfloat16),
        f32(each, 4, BLOCK, LANES),
        f32(2 * ROWS, halos),
    ]
    kept, sums = [], []
    for slab in slabs:
        *arrays, total = call(functools.partial(first_pass, slots, blocks), outs, place, state, other, *sums, *slab, scratch=held)
        kept.extend(arrays)
        if not sums:
            first, second, _ = lax.optimization_barrier((below_low, above_high, total))
            slabs.append((step(first, "x", 1), step(second, "x", -1)))
        sums = [total]
    state, own, partner = call(
        second_pass,
        [f32(4, halos), f32(ROWS, halos), f32(ROWS, halos)],
        state,
        other,
        sums[0],
        step(sums[0], "core", 1),
        *kept,
        scratch=all_held,
    )
    outs = [f32(3, halos), f32(1, halos), f32(SHELLS, halos)]
    centers, radii, profile = call(finish, outs, state, own, step(partner, "core", 1))
    return (centers, radii[0], profile)


def solution(mesh):
    chips = Mesh(mesh.devices.reshape(4, 2, 4, 4), AXES)
    in_specs = (
        P(None, AXES),
        P(AXES),
        P(None, AXES),
        P(AXES),
        P(AXES),
        P(AXES),
    )
    out_specs = (P(None, AXES), P(AXES), P(None, AXES))
    return jax.shard_map(body, mesh=chips, in_specs=in_specs, out_specs=out_specs, check_vma=False)
```

```python
import functools

import jax
import jax.numpy as jnp
from jax import lax
from jax.experimental import pallas as pl
from jax.experimental.pallas import tpu as pltpu
from jax.sharding import Mesh, PartitionSpec as P

SHELLS = 16
BLOCK = 128
LANES = 128
ROWS = 24
AXES = ("x", "core", "y", "z")
VMEM = pl.BlockSpec(memory_space=pltpu.VMEM)
PARAMS = pltpu.CompilerParams(vmem_limit_bytes=16 * 2**20)


def f32(*shape):
    return jax.ShapeDtypeStruct(shape, jnp.float32)


def split(value, terms):
    parts = []
    for _ in range(terms):
        part = value.astype(jnp.bfloat16)
        parts.append(part)
        value = value - part.astype(jnp.float32)
    return parts


def gather_state(state, one_hot):
    stacked = jnp.concatenate([s.astype(jnp.float32) for s in split(state, 3)] + [jnp.zeros_like(state)], axis=0)
    got = jnp.dot(stacked.astype(jnp.bfloat16), one_hot, preferred_element_type=jnp.float32)
    return got[0:4] + got[4:8] + got[8:12]


def spread(rows, keep, own, slots):
    rows = jnp.where(keep, rows, 0.0)
    shift = slots
    while shift < LANES:
        rows = rows + pltpu.roll(rows, shift, 1)
        shift *= 2
    return jnp.sum(jnp.where(own, rows, 0.0), axis=0, keepdims=True)


def pack(positions, masses, halo, block, centers, radii, out, state, *scratch):
    arrays = (positions, masses, halo, block, centers, radii)
    held, sems = scratch[:-1], scratch[-1]
    copies = [pltpu.make_async_copy(a, v, sems.at[n]) for n, (a, v) in enumerate(zip(arrays, held))]
    for copy in copies:
        copy.start()
    for copy in copies:
        copy.wait()
    blocks = masses.shape[0]
    for c in range(3):
        for b in range(blocks):
            out[c * blocks + b : c * blocks + b + 1] = held[0][c : c + 1, b * BLOCK : (b + 1) * BLOCK]
    at = 3 * blocks
    for part in held[1:4]:
        out[at : at + part.shape[0]] = part[...].astype(jnp.float32)
        at += part.shape[0]
    state[0:3] = held[4][...]
    state[3:4] = held[5][...]


def merge_z(slots, width, place, *refs):
    size = len(refs) // 2
    parts, outs = refs[:size], refs[size:]
    index_rows = (parts[0].shape[0] - width) // 2
    row = lax.broadcasted_iota(jnp.int32, (index_rows, LANES), 0)
    group = lax.broadcasted_iota(jnp.int32, (index_rows, LANES), 1) // slots
    for k in range(size):
        for i in range(size):
            outs[k][i * width : (i + 1) * width] = parts[i][:width]
        y = (place[2] + k) % size
        keep = (group == y % 2 * size + place[3]) & (row % 2 == y // 2)
        for which in range(2):
            for i in range(size):
                at = width + which * index_rows
                to = size * width + which * size + i
                outs[k][to : to + 1] = spread(parts[i][at : at + index_rows], keep, group == row // 2, slots)


def merge_y(*refs):
    size = len(refs) - 2
    parts, halves = refs[:size], refs[size:]
    rows = parts[0].shape[0] - 2 * size
    for i in range(size):
        half, at = halves[i // 2], i % 2
        half[at * rows : (at + 1) * rows] = parts[i][:rows]
        for which in range(2):
            to = 2 * rows + which * 2 * size + at * size
            half[to : to + size] = parts[i][rows + which * size : rows + (which + 1) * size]


def tile_sums(mine, points, t, out, o):
    cx, cy, cz, rad = mine[0:1], mine[1:2], mine[2:3], mine[3:4]
    scale = (SHELLS / 2.0) / jnp.where(rad > 0.0, rad, 1.0)
    ramps = [None] * (SHELLS + 1)
    inner = [None] * 4

    def add(sums, k, value):
        sums[k] = value if sums[k] is None else sums[k] + value

    for p in range(0, BLOCK, 8):
        x = points[t, 0, p : p + 8] - cx
        y = points[t, 1, p : p + 8] - cy
        z = points[t, 2, p : p + 8] - cz
        mass = points[t, 3, p : p + 8]
        scaled = jnp.sqrt(x * x + y * y + z * z) * scale
        half = mass * 0.5
        reach = half - mass * scaled
        for k in range(SHELLS + 1):
            add(ramps, k, jnp.maximum(reach, 0.0))
            if k == SHELLS // 2 - 1:
                weight = jnp.maximum(jnp.minimum(reach + half, mass), 0.0)
            reach = reach + mass
        add(inner, 0, weight)
        add(inner, 1, weight * x)
        add(inner, 2, weight * y)
        add(inner, 3, weight * z)
    rows = [jnp.sum(ramps[k + 1] - ramps[k] - ramps[0], axis=0, keepdims=True) for k in range(SHELLS)]
    rows += [jnp.sum(value, axis=0, keepdims=True) for value in inner]
    rows += [jnp.zeros_like(rows[0])] * (ROWS - len(rows))
    out[o] = jnp.concatenate(rows, axis=0)


def halo_sums(terms, halo_hot):
    high, low = [part.astype(jnp.float32) for part in split(terms, 2)]
    both = jnp.concatenate([high, low], axis=0).astype(jnp.bfloat16)
    sums = jnp.dot(both, halo_hot, preferred_element_type=jnp.float32)
    return sums[:ROWS] + sums[ROWS:]


def first_pass(slots, blocks, place, *refs):
    inputs, (one_hot, halo_hot, points, sums, slot_state, partial) = refs[:-6], refs[-6:]
    states, before, halves = inputs[:2], inputs[2:-2], inputs[-2:]
    halos = states[0].shape[1]
    domain = 4 * blocks
    count = 8 * blocks
    lane_group = lax.broadcasted_iota(jnp.int32, (8, LANES), 1) // slots
    own = lane_group == lax.broadcasted_iota(jnp.int32, (8, LANES), 0)
    halo_index = lax.broadcasted_iota(jnp.int32, (halos, LANES), 0).astype(jnp.float32)
    across = lax.broadcasted_iota(jnp.int32, (LANES, halos), 1).astype(jnp.float32)
    block_index = lax.broadcasted_iota(jnp.int32, (count, LANES), 0).astype(jnp.float32)
    first = (lax.broadcasted_iota(jnp.int32, (1, LANES), 1) // slots * blocks).astype(jnp.float32)
    for h, half in enumerate(halves):
        picks = []
        for o in range(2):
            t = o * 2 + h
            at = 8 * domain
            keep = lane_group == place[0] * 2 + (place[1] if o == 0 else 1 - place[1])
            halo_row = spread(half[at : at + 8], keep, own, slots)
            hit = halo_index == halo_row
            one_hot[:, t * LANES : (t + 1) * LANES] = jnp.where(hit, 1.0, 0.0).astype(jnp.bfloat16)
            column = jnp.broadcast_to(halo_row, (LANES, LANES)).T
            for a in range(0, halos, LANES):
                hit = across[:, a : a + LANES] == column
                halo_hot[t * LANES : (t + 1) * LANES, a : a + LANES] = jnp.where(hit, 1.0, 0.0).astype(jnp.bfloat16)
            hit = block_index == spread(half[at + 8 : at + 16], keep, own, slots) + first
            picks.append(jnp.where(hit, 1.0, 0.0).astype(jnp.bfloat16))
        pick = jnp.concatenate(picks, axis=1)
        pick = jnp.concatenate([pick, pick], axis=0)
        stacked = []
        for c in range(4):
            parts = [half[a + c * blocks : a + (c + 1) * blocks] for a in range(0, 8 * domain, domain)]
            stacked.append(jnp.concatenate(split(jnp.concatenate(parts, axis=0), 2), axis=0))
        chosen = lax.dot_general(
            jnp.concatenate(stacked, axis=1), pick, (((0,), (0,)), ((), ())), preferred_element_type=jnp.float32
        )
        for c in range(4):
            for o in range(2):
                points[o * 2 + h, c] = chosen[c * BLOCK : (c + 1) * BLOCK, o * LANES : (o + 1) * LANES]
    slot_states([state[...] for state in states], one_hot, slot_state)
    slab_terms(points, slot_state, partial)
    value = slab_sums(halo_hot, partial)
    for ref in before:
        value = value + ref[...]
    sums[...] = value


def slot_states(states, one_hot, slot_state):
    tiles = slot_state.shape[0]
    each = tiles // 2
    width = each * LANES
    for o in range(2):
        got = gather_state(states[o], one_hot[:, o * width : (o + 1) * width])
        for t in range(each):
            slot_state[o * each + t, 0:4] = got[:, t * LANES : (t + 1) * LANES]


def slab_terms(points, slot_state, partial):
    for t in range(points.shape[0]):
        tile_sums(slot_state[t], points, t, partial, t)


def slab_sums(halo_hot, partial):
    each = partial.shape[0] // 2
    width = each * LANES
    sums = []
    for o in range(2):
        terms = jnp.concatenate([partial[o * each + t] for t in range(each)], axis=1)
        sums.append(halo_sums(terms, halo_hot[o * width : (o + 1) * width]))
    return jnp.concatenate(sums, axis=0)


def advance(state, sums):
    center, radius = state[0:3], state[3:4]
    profile = sums[:SHELLS]
    enclosed = profile[SHELLS // 2 - 1 : SHELLS // 2]
    ratio = (1.0 + enclosed) / (1.0 + radius * radius * radius)
    radius = radius * jnp.exp(jnp.log(ratio) * (1.0 / 3.0))
    center = center + sums[SHELLS + 1 : SHELLS + 4] / jnp.maximum(sums[SHELLS : SHELLS + 1], 1.0)
    return center, radius, profile


def second_pass(mine, other, sums, received, *refs):
    inputs, (state, own, partner, slot_state, partial) = refs[:-5], refs[-5:]
    totals = (sums[:ROWS] + received[ROWS:], sums[ROWS:] + received[:ROWS])
    states = [jnp.concatenate(advance(s[...], t)[:2], axis=0) for s, t in zip((mine, other), totals)]
    state[...] = states[0]
    one_hots, halo_hots, points = inputs[0::3], inputs[1::3], inputs[2::3]
    slabs = len(points)
    each = points[0].shape[0]
    at = [pl.ds(i * each, each) for i in range(slabs)]
    value = None
    slot_states(states, one_hots[0], slot_state.at[at[0]])
    for i in range(slabs):
        if i + 1 < slabs:
            slot_states(states, one_hots[i + 1], slot_state.at[at[i + 1]])
        if i:
            part = slab_sums(halo_hots[i - 1], partial.at[at[i - 1]])
            value = part if value is None else value + part
        slab_terms(points[i], slot_state.at[at[i]], partial.at[at[i]])
    value = value + slab_sums(halo_hots[-1], partial.at[at[-1]])
    own[...] = value[:ROWS]
    partner[...] = value[ROWS:]


def finish(state, own, received, centers_out, radii_out, profile_out):
    centers_out[...], radii_out[...], profile_out[...] = advance(state[...], own[...] + received[...])


def step(value, axis, by):
    size = lax.axis_size(axis)
    return lax.ppermute(value, axis, [(i, (i + by) % size) for i in range(size)])


def call(fn, outs, *args, scratch=(), near=True):
    place = VMEM if near else pl.BlockSpec(memory_space=pltpu.HBM)
    specs = [pl.BlockSpec(memory_space=pltpu.SMEM) if a.ndim == 1 else place for a in args]
    out_specs = [VMEM] * len(outs)
    return pl.pallas_call(
        fn, in_specs=specs, out_specs=out_specs, out_shape=outs, scratch_shapes=scratch, compiler_params=PARAMS
    )(*args)


def body(positions, masses, centers, radii, pair_block, pair_halo):
    devices = lax.axis_size(AXES)
    halos = radii.shape[0]
    blocks = masses.shape[0] // BLOCK
    slots = pair_halo.shape[0] // devices
    domain = 4 * blocks
    place = jnp.stack([lax.axis_index(axis) for axis in AXES]).astype(jnp.int32)
    row = lambda a: a.reshape(-1, LANES)
    inputs = (positions, row(masses), row(pair_halo), row(pair_block), centers, radii[None])
    inputs = [pltpu.with_memory_space_constraint(a, pltpu.HBM) for a in inputs]
    payload, state = call(
        pack,
        [f32(domain + 2 * row(pair_halo).shape[0], LANES), f32(4, halos)],
        *inputs,
        scratch=[pltpu.VMEM(a.shape, a.dtype) for a in inputs] + [pltpu.SemaphoreType.DMA((len(inputs),))],
        near=False,
    )
    other = step(state, "core", 1)
    along_z = [payload] + [step(payload, "z", k) for k in range(1, 4)]
    *along_z, other = lax.optimization_barrier((*along_z, other))
    to_y = call(functools.partial(merge_z, slots, domain), [f32(4 * domain + 8, LANES)] * 4, place, *along_z)
    along_y = [step(to_y[k], "y", k) if k else to_y[k] for k in range(4)]
    low, high = call(merge_y, [f32(8 * domain + 16, LANES)] * 2, *along_y)
    below_low, above_high = step(low, "x", 1), step(high, "x", -1)
    slabs = [[low, high], [below_low, above_high]]
    each = devices * slots // LANES // 4
    held, all_held = (
        [pltpu.VMEM((n, 8, LANES), jnp.float32), pltpu.VMEM((n, ROWS, LANES), jnp.float32)] for n in (each, 4 * each)
    )
    outs = [
        jax.ShapeDtypeStruct((halos, each * LANES), jnp.bfloat16),
        jax.ShapeDtypeStruct((each * LANES, halos), jnp.bfloat16),
        f32(each, 4, BLOCK, LANES),
        f32(2 * ROWS, halos),
    ]
    kept, sums = [], []
    for n in range(4):
        *arrays, total = call(functools.partial(first_pass, slots, blocks), outs, place, state, other, *sums, *slabs[n], scratch=held)
        kept.extend(arrays)
        if not sums:
            *slabs[1], low, high, _ = lax.optimization_barrier((*slabs[1], low, high, total))
            far = (step(slabs[1][0], "x", 1), step(slabs[1][1], "x", -1))
            slabs += [(step(high, "x", 1), step(low, "x", -1)), far]
        sums = [total]
    state, own, partner = call(
        second_pass,
        [f32(4, halos), f32(ROWS, halos), f32(ROWS, halos)],
        state,
        other,
        sums[0],
        step(sums[0], "core", 1),
        *kept,
        scratch=all_held,
    )
    outs = [f32(3, halos), f32(1, halos), f32(SHELLS, halos)]
    centers, radii, profile = call(finish, outs, state, own, step(partner, "core", 1))
    return (centers, radii[0], profile)


def solution(mesh):
    chips = Mesh(mesh.devices.reshape(4, 2, 4, 4), AXES)
    in_specs = (
        P(None, AXES),
        P(AXES),
        P(None, AXES),
        P(AXES),
        P(AXES),
        P(AXES),
    )
    out_specs = (P(None, AXES), P(AXES), P(None, AXES))
    return jax.shard_map(body, mesh=chips, in_specs=in_specs, out_specs=out_specs, check_vma=False)
```

```python
import functools

import jax
import jax.numpy as jnp
from jax import lax
from jax.experimental import pallas as pl
from jax.experimental.pallas import tpu as pltpu
from jax.sharding import Mesh, PartitionSpec as P

SHELLS = 16
BLOCK = 128
LANES = 128
ROWS = 24
AXES = ("x", "core", "y", "z")
VMEM = pl.BlockSpec(memory_space=pltpu.VMEM)
PARAMS = pltpu.CompilerParams(vmem_limit_bytes=16 * 2**20)


def f32(*shape):
    return jax.ShapeDtypeStruct(shape, jnp.float32)


def split(value, terms):
    parts = []
    for _ in range(terms):
        part = value.astype(jnp.bfloat16)
        parts.append(part)
        value = value - part.astype(jnp.float32)
    return parts


def gather_state(state, one_hot):
    stacked = jnp.concatenate([s.astype(jnp.float32) for s in split(state, 3)] + [jnp.zeros_like(state)], axis=0)
    got = jnp.dot(stacked.astype(jnp.bfloat16), one_hot, preferred_element_type=jnp.float32)
    return got[0:4] + got[4:8] + got[8:12]


def spread(rows, keep, own, slots):
    rows = jnp.where(keep, rows, 0.0)
    shift = slots
    while shift < LANES:
        rows = rows + pltpu.roll(rows, shift, 1)
        shift *= 2
    return jnp.sum(jnp.where(own, rows, 0.0), axis=0, keepdims=True)


def pack(positions, masses, halo, block, centers, radii, out, state, *scratch):
    arrays = (positions, masses, halo, block, centers, radii)
    held, sems = scratch[:-1], scratch[-1]
    copies = [pltpu.make_async_copy(a, v, sems.at[n]) for n, (a, v) in enumerate(zip(arrays, held))]
    for copy in copies:
        copy.start()
    for copy in copies:
        copy.wait()
    blocks = masses.shape[0]
    for c in range(3):
        for b in range(blocks):
            out[c * blocks + b : c * blocks + b + 1] = held[0][c : c + 1, b * BLOCK : (b + 1) * BLOCK]
    at = 3 * blocks
    for part in held[1:4]:
        out[at : at + part.shape[0]] = part[...].astype(jnp.float32)
        at += part.shape[0]
    state[0:3] = held[4][...]
    state[3:4] = held[5][...]


def merge_z(slots, width, place, *refs):
    size = len(refs) // 2
    parts, outs = refs[:size], refs[size:]
    index_rows = (parts[0].shape[0] - width) // 2
    row = lax.broadcasted_iota(jnp.int32, (index_rows, LANES), 0)
    group = lax.broadcasted_iota(jnp.int32, (index_rows, LANES), 1) // slots
    for k in range(size):
        for i in range(size):
            outs[k][i * width : (i + 1) * width] = parts[i][:width]
        y = (place[2] + k) % size
        keep = (group == y % 2 * size + place[3]) & (row % 2 == y // 2)
        for which in range(2):
            for i in range(size):
                at = width + which * index_rows
                to = size * width + which * size + i
                outs[k][to : to + 1] = spread(parts[i][at : at + index_rows], keep, group == row // 2, slots)


def merge_y(*refs):
    size = len(refs) - 2
    parts, halves = refs[:size], refs[size:]
    rows = parts[0].shape[0] - 2 * size
    for i in range(size):
        half, at = halves[i // 2], i % 2
        half[at * rows : (at + 1) * rows] = parts[i][:rows]
        for which in range(2):
            to = 2 * rows + which * 2 * size + at * size
            half[to : to + size] = parts[i][rows + which * size : rows + (which + 1) * size]


def tile_sums(mine, points, t, out, o):
    cx, cy, cz, rad = mine[0:1], mine[1:2], mine[2:3], mine[3:4]
    scale = (SHELLS / 2.0) / jnp.where(rad > 0.0, rad, 1.0)
    ramps = [None] * (SHELLS + 1)
    inner = [None] * 4

    def add(sums, k, value):
        sums[k] = value if sums[k] is None else sums[k] + value

    for p in range(0, BLOCK, 8):
        x = points[t, 0, p : p + 8] - cx
        y = points[t, 1, p : p + 8] - cy
        z = points[t, 2, p : p + 8] - cz
        mass = points[t, 3, p : p + 8]
        scaled = jnp.sqrt(x * x + y * y + z * z) * scale
        half = mass * 0.5
        reach = half - mass * scaled
        for k in range(SHELLS + 1):
            add(ramps, k, jnp.maximum(reach, 0.0))
            if k == SHELLS // 2 - 1:
                weight = jnp.maximum(jnp.minimum(reach + half, mass), 0.0)
            reach = reach + mass
        add(inner, 0, weight)
        add(inner, 1, weight * x)
        add(inner, 2, weight * y)
        add(inner, 3, weight * z)
    rows = [jnp.sum(ramps[k + 1] - ramps[k] - ramps[0], axis=0, keepdims=True) for k in range(SHELLS)]
    rows += [jnp.sum(value, axis=0, keepdims=True) for value in inner]
    rows += [jnp.zeros_like(rows[0])] * (ROWS - len(rows))
    out[o] = jnp.concatenate(rows, axis=0)


def halo_sums(terms, halo_hot):
    high, low = [part.astype(jnp.float32) for part in split(terms, 2)]
    both = jnp.concatenate([high, low], axis=0).astype(jnp.bfloat16)
    sums = jnp.dot(both, halo_hot, preferred_element_type=jnp.float32)
    return sums[:ROWS] + sums[ROWS:]


def first_pass(slots, blocks, place, *refs):
    inputs, (one_hot, halo_hot, points, sums, slot_state, partial) = refs[:-6], refs[-6:]
    states, before, halves = inputs[:2], inputs[2:-2], inputs[-2:]
    halos = states[0].shape[1]
    domain = 4 * blocks
    count = 8 * blocks
    lane_group = lax.broadcasted_iota(jnp.int32, (8, LANES), 1) // slots
    own = lane_group == lax.broadcasted_iota(jnp.int32, (8, LANES), 0)
    halo_index = lax.broadcasted_iota(jnp.int32, (halos, LANES), 0).astype(jnp.float32)
    across = lax.broadcasted_iota(jnp.int32, (LANES, halos), 1).astype(jnp.float32)
    block_index = lax.broadcasted_iota(jnp.int32, (count, LANES), 0).astype(jnp.float32)
    first = (lax.broadcasted_iota(jnp.int32, (1, LANES), 1) // slots * blocks).astype(jnp.float32)
    for h, half in enumerate(halves):
        picks = []
        for o in range(2):
            t = o * 2 + h
            at = 8 * domain
            keep = lane_group == place[0] * 2 + (place[1] if o == 0 else 1 - place[1])
            halo_row = spread(half[at : at + 8], keep, own, slots)
            hit = halo_index == halo_row
            one_hot[:, t * LANES : (t + 1) * LANES] = jnp.where(hit, 1.0, 0.0).astype(jnp.bfloat16)
            column = jnp.broadcast_to(halo_row, (LANES, LANES)).T
            for a in range(0, halos, LANES):
                hit = across[:, a : a + LANES] == column
                halo_hot[t * LANES : (t + 1) * LANES, a : a + LANES] = jnp.where(hit, 1.0, 0.0).astype(jnp.bfloat16)
            hit = block_index == spread(half[at + 8 : at + 16], keep, own, slots) + first
            picks.append(jnp.where(hit, 1.0, 0.0).astype(jnp.bfloat16))
        pick = jnp.concatenate(picks, axis=1)
        pick = jnp.concatenate([pick, pick], axis=0)
        stacked = []
        for c in range(4):
            parts = [half[a + c * blocks : a + (c + 1) * blocks] for a in range(0, 8 * domain, domain)]
            stacked.append(jnp.concatenate(split(jnp.concatenate(parts, axis=0), 2), axis=0))
        chosen = lax.dot_general(
            jnp.concatenate(stacked, axis=1), pick, (((0,), (0,)), ((), ())), preferred_element_type=jnp.float32
        )
        for c in range(4):
            for o in range(2):
                points[o * 2 + h, c] = chosen[c * BLOCK : (c + 1) * BLOCK, o * LANES : (o + 1) * LANES]
    slot_states([state[...] for state in states], one_hot, slot_state)
    slab_terms(points, slot_state, partial)
    value = slab_sums(halo_hot, partial)
    for ref in before:
        value = value + ref[...]
    sums[...] = value


def slot_states(states, one_hot, slot_state):
    tiles = slot_state.shape[0]
    each = tiles // 2
    width = each * LANES
    for o in range(2):
        got = gather_state(states[o], one_hot[:, o * width : (o + 1) * width])
        for t in range(each):
            slot_state[o * each + t, 0:4] = got[:, t * LANES : (t + 1) * LANES]


def slab_terms(points, slot_state, partial):
    for t in range(points.shape[0]):
        tile_sums(slot_state[t], points, t, partial, t)


def slab_sums(halo_hot, partial):
    each = partial.shape[0] // 2
    width = each * LANES
    sums = []
    for o in range(2):
        terms = jnp.concatenate([partial[o * each + t] for t in range(each)], axis=1)
        sums.append(halo_sums(terms, halo_hot[o * width : (o + 1) * width]))
    return jnp.concatenate(sums, axis=0)


def advance(state, sums):
    center, radius = state[0:3], state[3:4]
    profile = sums[:SHELLS]
    enclosed = profile[SHELLS // 2 - 1 : SHELLS // 2]
    ratio = (1.0 + enclosed) / (1.0 + radius * radius * radius)
    radius = radius * jnp.exp(jnp.log(ratio) * (1.0 / 3.0))
    center = center + sums[SHELLS + 1 : SHELLS + 4] / jnp.maximum(sums[SHELLS : SHELLS + 1], 1.0)
    return center, radius, profile


def second_pass(mine, other, sums, received, *refs):
    inputs, (state, own, partner, slot_state, partial) = refs[:-5], refs[-5:]
    totals = (sums[:ROWS] + received[ROWS:], sums[ROWS:] + received[:ROWS])
    states = [jnp.concatenate(advance(s[...], t)[:2], axis=0) for s, t in zip((mine, other), totals)]
    state[...] = states[0]
    one_hots, halo_hots, points = inputs[0::3], inputs[1::3], inputs[2::3]
    slabs = len(points)
    each = points[0].shape[0]
    at = [pl.ds(i * each, each) for i in range(slabs)]
    value = None
    slot_states(states, one_hots[0], slot_state.at[at[0]])
    for i in range(slabs):
        if i + 1 < slabs:
            slot_states(states, one_hots[i + 1], slot_state.at[at[i + 1]])
        if i:
            part = slab_sums(halo_hots[i - 1], partial.at[at[i - 1]])
            value = part if value is None else value + part
        slab_terms(points[i], slot_state.at[at[i]], partial.at[at[i]])
    value = value + slab_sums(halo_hots[-1], partial.at[at[-1]])
    own[...] = value[:ROWS]
    partner[...] = value[ROWS:]


def finish(state, own, received, centers_out, radii_out, profile_out):
    centers_out[...], radii_out[...], profile_out[...] = advance(state[...], own[...] + received[...])


def step(value, axis, by):
    size = lax.axis_size(axis)
    return lax.ppermute(value, axis, [(i, (i + by) % size) for i in range(size)])


def call(fn, outs, *args, scratch=(), near=True):
    place = VMEM if near else pl.BlockSpec(memory_space=pltpu.HBM)
    specs = [pl.BlockSpec(memory_space=pltpu.SMEM) if a.ndim == 1 else place for a in args]
    out_specs = [VMEM] * len(outs)
    return pl.pallas_call(
        fn, in_specs=specs, out_specs=out_specs, out_shape=outs, scratch_shapes=scratch, compiler_params=PARAMS
    )(*args)


def body(positions, masses, centers, radii, pair_block, pair_halo):
    devices = lax.axis_size(AXES)
    halos = radii.shape[0]
    blocks = masses.shape[0] // BLOCK
    slots = pair_halo.shape[0] // devices
    domain = 4 * blocks
    place = jnp.stack([lax.axis_index(axis) for axis in AXES]).astype(jnp.int32)
    row = lambda a: a.reshape(-1, LANES)
    inputs = (positions, row(masses), row(pair_halo), row(pair_block), centers, radii[None])
    inputs = [pltpu.with_memory_space_constraint(a, pltpu.HBM) for a in inputs]
    payload, state = call(
        pack,
        [f32(domain + 2 * row(pair_halo).shape[0], LANES), f32(4, halos)],
        *inputs,
        scratch=[pltpu.VMEM(a.shape, a.dtype) for a in inputs] + [pltpu.SemaphoreType.DMA((len(inputs),))],
        near=False,
    )
    other = step(state, "core", 1)
    along_z = [payload] + [step(payload, "z", k) for k in range(1, 4)]
    to_y = call(functools.partial(merge_z, slots, domain), [f32(4 * domain + 8, LANES)] * 4, place, *along_z)
    along_y = [step(to_y[k], "y", k) if k else to_y[k] for k in range(4)]
    *along_y, other = lax.optimization_barrier((*along_y, other))
    low, high = call(merge_y, [f32(8 * domain + 16, LANES)] * 2, *along_y)
    below_low, above_high = step(low, "x", 1), step(high, "x", -1)
    below_high, above_low = step(high, "x", 1), step(low, "x", -1)
    slabs = [(low, high), (below_low, above_high), (below_high, above_low)]
    each = devices * slots // LANES // 4
    held, all_held = (
        [pltpu.VMEM((n, 8, LANES), jnp.float32), pltpu.VMEM((n, ROWS, LANES), jnp.float32)] for n in (each, 4 * each)
    )
    outs = [
        jax.ShapeDtypeStruct((halos, each * LANES), jnp.bfloat16),
        jax.ShapeDtypeStruct((each * LANES, halos), jnp.bfloat16),
        f32(each, 4, BLOCK, LANES),
        f32(2 * ROWS, halos),
    ]
    kept, sums = [], []
    for slab in slabs:
        *arrays, total = call(functools.partial(first_pass, slots, blocks), outs, place, state, other, *sums, *slab, scratch=held)
        kept.extend(arrays)
        if not sums:
            first, second, _ = lax.optimization_barrier((below_low, above_high, total))
            slabs.append((step(first, "x", 1), step(second, "x", -1)))
        sums = [total]
    state, own, partner = call(
        second_pass,
        [f32(4, halos), f32(ROWS, halos), f32(ROWS, halos)],
        state,
        other,
        sums[0],
        step(sums[0], "core", 1),
        *kept,
        scratch=all_held,
    )
    outs = [f32(3, halos), f32(1, halos), f32(SHELLS, halos)]
    centers, radii, profile = call(finish, outs, state, own, step(partner, "core", 1))
    return (centers, radii[0], profile)


def solution(mesh):
    chips = Mesh(mesh.devices.reshape(4, 2, 4, 4), AXES)
    in_specs = (
        P(None, AXES),
        P(AXES),
        P(None, AXES),
        P(AXES),
        P(AXES),
        P(AXES),
    )
    out_specs = (P(None, AXES), P(AXES), P(None, AXES))
    return jax.shard_map(body, mesh=chips, in_specs=in_specs, out_specs=out_specs, check_vma=False)
```
